32 devices in a mesh: dp: 16 (over z, y, x), head: 2 (over core).
Axes of the slice: x: 2, y: 2, z: 4, core: 2. Of those that a mesh axis runs over, the one named last changes fastest.
Arguments:
- inputs: bfloat16 [16, 2, 512, 768], P('dp'), may hold values from -6 to 6
- cotangent: bfloat16 [16, 2, 512, 768], P('dp'), may hold values from -6 to 6
- seg_counts: int32 [16], P('dp'), may hold values from 1 to 2
- qkv_weight: float32 [3, 768, 768], P(None, 'dp', 'head'), may hold values from -0.3125 to 0.3125
- out_weight: float32 [768, 768], P('head', 'dp'), may hold values from -0.875 to 0.875
- up_weight: float32 [768, 3072], P('dp', 'head'), may hold values from -0.21875 to 0.21875
- down_weight: float32 [3072, 768], P('head', 'dp'), may hold values from -0.109375 to 0.109375
- head_bias: float32 [2, 2304], P('head'), may hold values from -3 to 3
- shared_params: float32 [16, 768], replicated, may hold values from -5 to 5
- qkv_first: float32 [3, 768, 768], P(None, 'dp', 'head'), may hold values from -0.00024414062 to 0.00024414062
- out_first: float32 [768, 768], P('head', 'dp'), may hold values from -0.00024414062 to 0.00024414062
- up_first: float32 [768, 3072], P('dp', 'head'), may hold values from -0.00024414062 to 0.00024414062
- down_first: float32 [3072, 768], P('head', 'dp'), may hold values from -0.00024414062 to 0.00024414062
- bias_first: float32 [2, 2304], P('head'), may hold values from -0.00024414062 to 0.00024414062
- shared_first: float32 [16, 768], replicated, may hold values from -0.00024414062 to 0.00024414062
- qkv_second: float32 [3, 768, 768], P(None, 'dp', 'head'), may hold values from 1.4094861e-10 to 5.6379446e-10
- out_second: float32 [768, 768], P('head', 'dp'), may hold values from 1.4094861e-10 to 5.6379446e-10
- up_second: float32 [768, 3072], P('dp', 'head'), may hold values from 1.4094861e-10 to 5.6379446e-10
- down_second: float32 [3072, 768], P('head', 'dp'), may hold values from 1.4094861e-10 to 5.6379446e-10
- bias_second: float32 [2, 2304], P('head'), may hold values from 1.4094861e-10 to 5.6379446e-10
- shared_second: float32 [16, 768], replicated, may hold values from 1.4094861e-10 to 5.6379446e-10
Outputs:
- outputs: bfloat16 [16, 2, 512, 768], P('dp')
- input_grad: bfloat16 [16, 2, 512, 768], P('dp')
- grad_norm: float32 [], replicated
- qkv_update: float32 [3, 768, 768], P(None, 'dp', 'head')
- out_update: float32 [768, 768], P('head', 'dp')
- up_update: float32 [768, 3072], P('dp', 'head')
- down_update: float32 [3072, 768], P('head', 'dp')
- bias_update: float32 [2, 2304], P('head')
- shared_update: float32 [16, 768], replicated
- qkv_moment: float32 [3, 768, 768], P(None, 'dp', 'head')
- out_moment: float32 [768, 768], P('head', 'dp')
- up_moment: float32 [768, 3072], P('dp', 'head')
- down_moment: float32 [3072, 768], P('head', 'dp')
- bias_moment: float32 [2, 2304], P('head')
- shared_moment: float32 [16, 768], replicated
- qkv_square: float32 [3, 768, 768], P(None, 'dp', 'head')
- out_square: float32 [768, 768], P('head', 'dp')
- up_square: float32 [768, 3072], P('dp', 'head')
- down_square: float32 [3072, 768], P('head', 'dp')
- bias_square: float32 [2, 2304], P('head')
- shared_square: float32 [16, 768], replicated
The draws below stay inside these ranges and needn't reach their ends.
Inputs may be any that keep to these rules, and one draw needn't show every extreme that they name: `seg_counts`: a chain's slots 0 to its count minus 1 are live.
All inputs are finite; a program needn't handle non-finite values.
Results may differ from the reference program's by a relative error of at most 0.02.
The reference program's roundings to bfloat16 on the way count: a program that leaves them out, or rounds other values in their place, can miss the bound.
Values may be sent and summed in bfloat16 or wider, within the bound.
No kernel may reach another device: no remote copies, remote signals or barrier semaphores. Data moves between devices by JAX's collectives and lax.ppermute only.
A program may use at most 192 MiB of HBM per device.

```python
import math
import jax
import jax.numpy as jnp
from jax import lax

D = 768
HEADS = 12
HD = 64
FF = 3072
MEM = 10
SEG = 512
MAX_SEG = 2
STEP = 10
CHAINS = 16
SEGROWS = 532
BIAS_ROW = 2304
NPARAMS = 7094784
N_HEAD = 2


def draw_shared_params(key, part):
    base_values = jnp.clip(jax.random.normal(key, (MEM + 6, D), jnp.float32), -5.0, 5.0)
    row_number = jnp.arange(MEM + 6)[:, None]
    scaling = jnp.where(row_number < MEM, 1.0, 0.3)
    gain_rows = (row_number == MEM + 2) | (row_number == MEM + 4)
    return jnp.where(gain_rows, 1.0 + 0.1 * base_values, scaling * base_values)


def set_ends(values, rng, least, high):
    dims = values.shape
    index_at = [jax.random.randint(jax.random.fold_in(rng, axis), (), 0, dims[axis]) for axis in range(len(dims))]
    values = values.at[tuple(index_at)].set(least)
    longest = dims.index(max(dims))
    index_at[longest] = (index_at[longest] + 1) % dims[longest]
    return values.at[tuple(index_at)].set(high)


def shard_levels(own_key, dims, cuts, least, largest):
    factor_of, own = 1.0, jax.random.fold_in(own_key, 6)
    for dim, blocks in cuts:
        heights = jnp.exp(jax.random.uniform(jax.random.fold_in(own, dim), (blocks,), jnp.float32, least / len(cuts), largest / len(cuts)))
        factor_of = factor_of * jnp.repeat(heights, dims[dim] // blocks).reshape([-1 if axis == dim else 1 for axis in range(len(dims))])
    return factor_of


def bell_draw(stream_key, dims, deviation, reach, shards=(), held_as=jnp.bfloat16):
    array = jax.random.normal(stream_key, dims, jnp.float32) * deviation
    if len(shards) > 0:
        array = shard_levels(stream_key, dims, shards, -0.22, 0.18) * array
    return jnp.clip(array, min=-reach, max=reach).astype(held_as)


def setup_inputs(seed: int = 0) -> dict:
    splits = jax.random.split(jax.random.key(seed), 22)
    inputs = bell_draw(splits[0], (CHAINS, MAX_SEG, SEG, D), 1.0, 6.0, ((0, 16),))
    cotangent = bell_draw(splits[1], (CHAINS, MAX_SEG, SEG, D), 1.0, 6.0, ((0, 16),))
    seg_counts = set_ends(jax.random.randint(splits[2], (CHAINS,), 1, MAX_SEG + 1), jax.random.fold_in(splits[2], 1), 1, MAX_SEG).astype(jnp.int32)
    qkv_weight = bell_draw(splits[3], (3, D, D), (D // 2) ** -0.5, 0.3125, ((1, 16), (2, 2)), jnp.float32)
    out_weight = bell_draw(splits[4], (D, D), (D // 16) ** -0.5, 0.875, ((0, 2), (1, 16)), jnp.float32)
    up_weight = bell_draw(splits[5], (D, FF), D ** -0.5, 0.21875, ((0, 16), (1, 2)), jnp.float32)
    down_weight = bell_draw(splits[6], (FF, D), FF ** -0.5, 0.109375, ((0, 2), (1, 16)), jnp.float32)
    head_bias = bell_draw(splits[7], (N_HEAD, BIAS_ROW), 0.5, 3.0, ((0, 2),), jnp.float32)
    shared_params = draw_shared_params(jax.random.fold_in(splits[21], 71), 0)
    qkv_first = bell_draw(splits[9], (3, D, D), (NPARAMS ** -0.5 * 0.11), 0.00024414062, ((1, 16), (2, 2)), jnp.float32)
    out_first = bell_draw(splits[10], (D, D), (NPARAMS ** -0.5 * 0.11), 0.00024414062, ((0, 2), (1, 16)), jnp.float32)
    up_first = bell_draw(splits[11], (D, FF), (NPARAMS ** -0.5 * 0.11), 0.00024414062, ((0, 16), (1, 2)), jnp.float32)
    down_first = bell_draw(splits[12], (FF, D), (NPARAMS ** -0.5 * 0.11), 0.00024414062, ((0, 2), (1, 16)), jnp.float32)
    bias_first = bell_draw(splits[13], (N_HEAD, BIAS_ROW), (NPARAMS ** -0.5 * 0.11), 0.00024414062, ((0, 2),), jnp.float32)
    shared_first = bell_draw(splits[14], (MEM + 6, D), (NPARAMS ** -0.5 * 0.11), 0.00024414062, (), jnp.float32)
    qkv_second = jnp.clip(jnp.exp(math.log(5.637944555658692e-10) - 1.3862944 * jax.random.uniform(splits[15], (3, D, D), jnp.float32) ** shard_levels(splits[15], (3, D, D), ((1, 16), (2, 2)), -0.2, 0.2)), 1.409486138914673e-10, 5.637944555658692e-10)
    out_second = jnp.clip(jnp.exp(math.log(5.637944555658692e-10) - 1.3862944 * jax.random.uniform(splits[16], (D, D), jnp.float32) ** shard_levels(splits[16], (D, D), ((0, 2), (1, 16)), -0.2, 0.2)), 1.409486138914673e-10, 5.637944555658692e-10)
    up_second = jnp.clip(jnp.exp(math.log(5.637944555658692e-10) - 1.3862944 * jax.random.uniform(splits[17], (D, FF), jnp.float32) ** shard_levels(splits[17], (D, FF), ((0, 16), (1, 2)), -0.2, 0.2)), 1.409486138914673e-10, 5.637944555658692e-10)
    down_second = jnp.clip(jnp.exp(math.log(5.637944555658692e-10) - 1.3862944 * jax.random.uniform(splits[18], (FF, D), jnp.float32) ** shard_levels(splits[18], (FF, D), ((0, 2), (1, 16)), -0.2, 0.2)), 1.409486138914673e-10, 5.637944555658692e-10)
    bias_second = jnp.clip(jnp.exp(math.log(5.637944555658692e-10) - 1.3862944 * jax.random.uniform(splits[19], (N_HEAD, BIAS_ROW), jnp.float32) ** shard_levels(splits[19], (N_HEAD, BIAS_ROW), ((0, 2),), -0.2, 0.2)), 1.409486138914673e-10, 5.637944555658692e-10)
    shared_second = jnp.clip(jnp.exp(jax.random.uniform(splits[20], (MEM + 6, D), jnp.float32, math.log(1.409486138914673e-10), math.log(5.637944555658692e-10))), 1.409486138914673e-10, 5.637944555658692e-10)
    return {"inputs": inputs, "cotangent": cotangent, "seg_counts": seg_counts, "qkv_weight": qkv_weight, "out_weight": out_weight, "up_weight": up_weight, "down_weight": down_weight, "head_bias": head_bias, "shared_params": shared_params, "qkv_first": qkv_first, "out_first": out_first, "up_first": up_first, "down_first": down_first, "bias_first": bias_first, "shared_first": shared_first, "qkv_second": qkv_second, "out_second": out_second, "up_second": up_second, "down_second": down_second, "bias_second": bias_second, "shared_second": shared_second}


PRECISE = lax.Precision.HIGHEST
EPSILON = 1e-06
BETA_ONE = 0.9
BETA_TWO = 0.999
LEARN_RATE = 0.1
VECTOR_RATE = 0.6
DECAY_RATE = 0.01
ADAM_EPSILON = 1e-08
CLIP_NORM = 1.0

@jax.custom_vjp
def low(v):
    return lax.optimization_barrier(v.astype(jnp.bfloat16)).astype(jnp.float32)

@jax.custom_vjp
def low_back(v):
    return v

def low_keep(v):
    return (low(v), None)

def low_pass(kept, grad):
    return (grad,)

def back_keep(v):
    return (v, None)

def back_low(kept, grad):
    return (low(grad),)
low.defvjp(low_keep, low_pass)
low_back.defvjp(back_keep, back_low)

def norm_rows(values, gain, shift):
    average = lax.optimization_barrier(jnp.mean(values, axis=-1, keepdims=True))
    centered = values - average
    variance = lax.optimization_barrier(jnp.mean(centered * centered, axis=-1, keepdims=True))
    return centered * lax.rsqrt(variance + EPSILON) * gain + shift

def adam_update(weight, first_old, second_old, gradient, factor, decay_rate, step_rate):
    clipped = gradient * factor
    first_new = BETA_ONE * first_old + (1.0 - BETA_ONE) * clipped
    second_new = BETA_TWO * second_old + (1.0 - BETA_TWO) * clipped * clipped
    first_hat = first_new / (1.0 - BETA_ONE ** STEP)
    second_hat = second_new / (1.0 - BETA_TWO ** STEP)
    weight_new = weight - step_rate * (first_hat / (jnp.sqrt(second_hat) + ADAM_EPSILON) + decay_rate * weight)
    return (weight_new, first_new, second_new)

def segment_layer(memory, seg_piece, layer_params):
    qkv_low, out_low, up_low, down_low, q_bias, v_bias, up_bias, out_bias, down_bias, gain_one, shift_one, gain_two, shift_two = layer_params
    layer_in = jnp.concatenate([memory, seg_piece, memory], axis=0)
    layer_low = low(layer_in)
    projected = jnp.einsum('ld,tde->tle', layer_low, qkv_low, precision=PRECISE)
    query_low = low(low_back(projected[0]) + q_bias).reshape(SEGROWS, HEADS, HD)
    key_low = low(low_back(projected[1])).reshape(SEGROWS, HEADS, HD)
    value_low = low(low_back(projected[2]) + v_bias).reshape(SEGROWS, HEADS, HD)
    scores = low_back(jnp.einsum('qhe,khe->hqk', query_low, key_low, precision=PRECISE) * HD ** (-0.5))
    chances = jax.nn.softmax(scores, axis=-1)
    context = jnp.einsum('hqk,khe->qhe', low(chances), value_low, precision=PRECISE).reshape(SEGROWS, D)
    context_low = low(low_back(context))
    attn_out = low_back(jnp.dot(context_low, out_low, precision=PRECISE)) + out_bias
    hidden = norm_rows(layer_in + attn_out, gain_one, shift_one)
    upper_in = low_back(jnp.dot(low(hidden), up_low, precision=PRECISE)) + up_bias
    active_low = low(jax.nn.gelu(upper_in, approximate=False))
    ffn_out = low_back(jnp.dot(active_low, down_low, precision=PRECISE)) + down_bias
    return norm_rows(hidden + ffn_out, gain_two, shift_two)

def reference(inputs, cotangent, seg_counts, qkv_weight, out_weight, up_weight, down_weight, head_bias, shared_params, qkv_first, out_first, up_first, down_first, bias_first, shared_first, qkv_second, out_second, up_second, down_second, bias_second, shared_second):
    params = (qkv_weight, out_weight, up_weight, down_weight, head_bias, shared_params)
    firsts = (qkv_first, out_first, up_first, down_first, bias_first, shared_first)
    seconds = (qkv_second, out_second, up_second, down_second, bias_second, shared_second)

    def forward(source, weights):
        qkv_w, out_w, up_w, down_w, bias_rows, shared = weights
        part_width = D // N_HEAD
        layer_params = (low(qkv_w), low(out_w), low(up_w), low(down_w), bias_rows[:, :part_width].reshape(D), bias_rows[:, part_width:2 * part_width].reshape(D), bias_rows[:, 2 * part_width:].reshape(FF), shared[MEM], shared[MEM + 1], shared[MEM + 2], shared[MEM + 3], shared[MEM + 4], shared[MEM + 5])
        memory_start = shared[:MEM]

        def one_chain(packed):
            pieces, seg_total = packed

            def advance(memory, packed_step):
                seg_piece, position = packed_step
                result = segment_layer(memory, seg_piece, layer_params)
                alive_now = position < seg_total
                tokens_out = jnp.where(alive_now, result[MEM:MEM + SEG], jnp.zeros_like(seg_piece))
                memory_next = jnp.where(alive_now, result[MEM + SEG:], memory)
                return (memory_next, tokens_out)
            unused, tokens_all = lax.scan(advance, memory_start, (pieces, jnp.arange(MAX_SEG, dtype=jnp.int32)))
            return tokens_all
        return lax.map(jax.checkpoint(one_chain), (source, seg_counts))
    source = inputs.astype(jnp.float32)
    outputs, backward = jax.vjp(forward, source, params)
    source_grad, grads = backward(cotangent.astype(jnp.float32))
    grad_norm = jnp.sqrt(sum((jnp.sum(gradient * gradient) for gradient in grads)))
    factor = CLIP_NORM / jnp.maximum(grad_norm, CLIP_NORM)
    decays = (DECAY_RATE, DECAY_RATE, DECAY_RATE, DECAY_RATE, 0.0, 0.0)
    rates = (LEARN_RATE, LEARN_RATE, LEARN_RATE, LEARN_RATE, VECTOR_RATE, VECTOR_RATE)
    results = [adam_update(params[number], firsts[number], seconds[number], grads[number], factor, decays[number], rates[number]) for number in range(6)]
    return (outputs.astype(jnp.bfloat16), source_grad.astype(jnp.bfloat16), grad_norm, results[0][0], results[1][0], results[2][0], results[3][0], results[4][0], results[5][0], results[0][1], results[1][1], results[2][1], results[3][1], results[4][1], results[5][1], results[0][2], results[1][2], results[2][2], results[3][2], results[4][2], results[5][2])
```

```python
import functools
import math

import jax
import jax.numpy as jnp
from jax import lax
from jax.experimental import pallas as pl
from jax.experimental.pallas import tpu as pltpu
from jax.sharding import PartitionSpec as P

HD = 64
STEP = 10
EPSILON = 1e-06
BETA_ONE = 0.9
BETA_TWO = 0.999
LEARN_RATE = 0.1
VECTOR_RATE = 0.6
DECAY_RATE = 0.01
ADAM_EPSILON = 1e-08
CLIP_NORM = 1.0

BF = jnp.bfloat16
F32 = jnp.float32
LOG2E = math.log2(math.e)
NEG = -1e30
SLOTS = 16


def dot_nn(a, b):
    return lax.dot_general(a, b, (((1,), (0,)), ((), ())), preferred_element_type=F32)


def dot_nt(a, b):
    return lax.dot_general(a, b, (((1,), (1,)), ((), ())), preferred_element_type=F32)


def dot_tn(a, b):
    return lax.dot_general(a, b, (((0,), (0,)), ((), ())), preferred_element_type=F32)


def norm_stats(values):
    average = jnp.mean(values, axis=-1, keepdims=True)
    centered = values - average
    variance = jnp.mean(centered * centered, axis=-1, keepdims=True)
    scale = lax.rsqrt(variance + EPSILON)
    return centered * scale, scale


def norm_back(grad, gain, unit, scale):
    inner = grad * gain
    mean_one = jnp.mean(inner, axis=-1, keepdims=True)
    mean_two = jnp.mean(inner * unit, axis=-1, keepdims=True)
    return scale * (inner - mean_one - unit * mean_two)


def row_sum(values):
    return jnp.sum(values, axis=0, keepdims=True)


def call(kernel, outs, args, scalars=0, scratch=(), flops=0):
    moved = sum(a.size * a.dtype.itemsize for a in args)
    moved += sum(math.prod(s) * jnp.dtype(d).itemsize for s, d in outs)
    return pl.pallas_call(
        kernel,
        out_shape=[jax.ShapeDtypeStruct(s, d) for s, d in outs],
        in_specs=[pl.BlockSpec(memory_space=pltpu.SMEM)] * scalars
        + [pl.BlockSpec(memory_space=pltpu.VMEM)] * (len(args) - scalars),
        out_specs=[pl.BlockSpec(memory_space=pltpu.VMEM)] * len(outs),
        scratch_shapes=list(scratch),
        cost_estimate=pl.CostEstimate(
            flops=flops, bytes_accessed=moved, transcendentals=0
        ),
        compiler_params=pltpu.CompilerParams(vmem_limit_bytes=48 << 20),
    )(*args)


def slot_of(kind, outer, inner):
    mid, z = inner // 4, inner % 4
    return (outer + 2 * mid if kind == 0 else 2 * outer + mid) + 4 * z


def assemble_kernel(kinds, me_ref, *refs):
    count = len(kinds)
    for number, kind in enumerate(kinds):
        target = refs[2 * count + number]
        block = target.shape[0] // SLOTS
        for outer in range(2):
            source = refs[2 * number + outer]
            for inner in range(8):
                place = lax.bitwise_xor(me_ref[0], slot_of(kind, outer, inner))
                start = pl.multiple_of(place * block, block)
                target[pl.ds(start, block), :] = source[inner]


def attn_forward_kernel(token_ref, mem_ref, qk_ref, vo_ref, bias_ref, part_ref, low_ref, qkv_ref, lse_ref, ctx_ref):
    seg = token_ref.shape[0]
    pad = mem_ref.shape[0]
    rows = seg + 2 * pad
    width = vo_ref.shape[1] // 2
    used = 10
    memory = mem_ref[...].astype(BF)
    low_ref[:seg, :] = token_ref[...]
    low_ref[seg : seg + pad, :] = memory
    low_ref[seg + pad :, :] = memory
    low = low_ref[...]
    qk = dot_nn(low, qk_ref[...])
    qkv_ref[:, :width] = (qk[:, :width] + bias_ref[:, :width]).astype(BF)
    qkv_ref[:, width : 2 * width] = qk[:, width:].astype(BF)
    v_all = dot_nn(low, vo_ref[:, :width])
    qkv_ref[:, 2 * width :] = (v_all + bias_ref[:, width : 2 * width]).astype(BF)
    key_at = lax.broadcasted_iota(jnp.int32, (1, rows), 1)
    dead = (key_at >= seg) & (((key_at - seg) & (pad - 1)) >= used)
    lane = lax.broadcasted_iota(jnp.int32, (rows, 128), 1)
    lse = jnp.zeros((rows, 128), F32)
    for pair in range(width // 128):
        at = pair * 128
        q = qkv_ref[:, at : at + 128]
        k = qkv_ref[:, width + at : width + at + 128]
        v = qkv_ref[:, 2 * width + at : 2 * width + at + 128]
        outs = []
        for head in range(2):
            mine = (lane < 64) if head == 0 else (lane >= 64)
            s = dot_nt(jnp.where(mine, q, jnp.zeros_like(q)), k) * (HD**-0.5 * LOG2E)
            s = jnp.where(dead, NEG, s)
            top = jnp.max(s, axis=1, keepdims=True)
            e = jnp.exp2(s - top)
            total = jnp.sum(e, axis=1, keepdims=True)
            p = (e * (1.0 / total)).astype(BF)
            outs.append(dot_nn(p, v))
            lse = jnp.where(lane == 2 * pair + head, top + jnp.log2(total), lse)
        ctx_ref[:, at : at + 128] = jnp.where(lane < 64, outs[0], outs[1]).astype(BF)
    lse_ref[...] = lse
    part_ref[...] = dot_nt(ctx_ref[...], vo_ref[:, width:]).astype(BF)


def ffn_forward_kernel(token_ref, mem_ref, own_ref, other_ref, up0_ref, up1_ref, down0_ref, down1_ref, bias_ref, shared_ref,
                       part_ref, first_ref, low_ref, act_ref, slope_ref, total_ref):
    seg = token_ref.shape[0]
    pad = mem_ref.shape[0]
    used = 10
    width = 384
    attn = own_ref[...].astype(F32) + other_ref[...].astype(F32) + shared_ref[used : used + 1, :]
    first_ref[:seg, :] = token_ref[...].astype(F32) + attn[:seg]
    first_ref[seg : seg + pad, :] = mem_ref[...] + attn[seg : seg + pad]
    first_ref[seg + pad :, :] = mem_ref[...] + attn[seg + pad :]
    unit, unused = norm_stats(first_ref[...])
    hidden = unit * shared_ref[used + 2 : used + 3, :] + shared_ref[used + 3 : used + 4, :]
    low_ref[...] = hidden.astype(BF)
    low = low_ref[...]
    for half, (up_ref, down_ref) in enumerate(((up0_ref, down0_ref), (up1_ref, down1_ref))):
        span = up_ref.shape[1]
        for piece in range(span // width):
            at = piece * width
            to = half * span + at
            u = dot_nn(low, up_ref[:, at : at + width]) + bias_ref[:, 2 * width + to : 2 * width + to + width]
            cdf = 0.5 + 0.5 * lax.erf(u * (0.5**0.5))
            density = jnp.exp2(u * u * (-0.5 * LOG2E)) * ((2.0 * math.pi) ** -0.5)
            active = (u * cdf).astype(BF)
            act_ref[:, to : to + width] = active
            slope_ref[:, to : to + width] = (cdf + u * density).astype(BF)
            add = dot_nt(active, down_ref[:, at : at + width])
            if to == 0:
                total_ref[...] = add
            else:
                total_ref[...] += add
    part_ref[...] = total_ref[...].astype(BF)


def close_rows(first_ref, own_ref, other_ref, shared_ref):
    used = 10
    unit, unused = norm_stats(first_ref[...])
    hidden = unit * shared_ref[used + 2 : used + 3, :] + shared_ref[used + 3 : used + 4, :]
    return hidden + (own_ref[...].astype(F32) + other_ref[...].astype(F32)) + shared_ref[used + 1 : used + 2, :]


def close_kernel(first_ref, own_ref, other_ref, shared_ref, alive_ref, out_ref, mem_ref, second_ref):
    used = 10
    seg = out_ref.shape[0]
    pad = mem_ref.shape[0]
    second = close_rows(first_ref, own_ref, other_ref, shared_ref)
    second_ref[...] = second
    unit, unused = norm_stats(second)
    result = unit * shared_ref[used + 4 : used + 5, :] + shared_ref[used + 5 : used + 6, :]
    out_ref[...] = (result[:seg] * alive_ref[...]).astype(BF)
    row = lax.broadcasted_iota(jnp.int32, (pad, result.shape[1]), 0)
    mem_ref[...] = jnp.where(row < used, result[seg + pad :], 0.0)


def ffn_backward_kernel(second_ref, cot_ref, dmem_ref, alive_ref, shared_ref, up0_ref, up1_ref, down0_ref, down1_ref, slope_ref,
                        part_ref, dsecond_ref, dlow_ref, du_ref, dbias_ref, dvec_ref, total_ref):
    used = 10
    seg = cot_ref.shape[0]
    pad = dmem_ref.shape[0]
    width = 384
    unit, scale = norm_stats(second_ref[...])
    dy = jnp.concatenate(
        [cot_ref[...].astype(F32) * alive_ref[...], jnp.zeros((pad, unit.shape[1]), F32), dmem_ref[...] * alive_ref[...]], axis=0
    )
    dsecond = norm_back(dy, shared_ref[used + 4 : used + 5, :], unit, scale)
    dsecond_ref[...] = dsecond
    dvec_ref[0:1, :] = row_sum(dsecond)
    dvec_ref[1:2, :] = row_sum(dy * unit)
    dvec_ref[2:3, :] = row_sum(dy)
    dvec_ref[3:, :] = jnp.zeros((dvec_ref.shape[0] - 3, unit.shape[1]), F32)
    dlow_ref[...] = dsecond.astype(BF)
    dlow = dlow_ref[...]
    for half, (up_ref, down_ref) in enumerate(((up0_ref, down0_ref), (up1_ref, down1_ref))):
        span = up_ref.shape[1]
        for piece in range(span // width):
            at = piece * width
            to = half * span + at
            dg = dot_nn(dlow, down_ref[:, at : at + width])
            du = dg * slope_ref[:, to : to + width].astype(F32)
            dbias_ref[:, to : to + width] = row_sum(du)
            du_low = du.astype(BF)
            du_ref[:, to : to + width] = du_low
            add = dot_nt(du_low, up_ref[:, at : at + width])
            if to == 0:
                total_ref[...] = add
            else:
                total_ref[...] += add
    part_ref[...] = total_ref[...].astype(BF)


def attn_backward_kernel(dsecond_ref, own_ref, other_ref, first_ref, shared_ref, qk_ref, vo_ref, qkv_ref, lse_ref,
                         part_ref, dfirst_ref, da_ref, dqkv_ref, dhead_ref, dvec_ref, dctx_ref):
    used = 10
    rows = first_ref.shape[0]
    width = vo_ref.shape[1] // 2
    pad = 16
    seg = rows - 2 * pad
    dhidden = dsecond_ref[...] + (own_ref[...].astype(F32) + other_ref[...].astype(F32))
    unit, scale = norm_stats(first_ref[...])
    dfirst = norm_back(dhidden, shared_ref[used + 2 : used + 3, :], unit, scale)
    dfirst_ref[...] = dfirst
    dvec_ref[0:1, :] = row_sum(dfirst)
    dvec_ref[1:2, :] = row_sum(dhidden * unit)
    dvec_ref[2:3, :] = row_sum(dhidden)
    dvec_ref[3:, :] = jnp.zeros((dvec_ref.shape[0] - 3, unit.shape[1]), F32)
    da_ref[...] = dfirst.astype(BF)
    dctx_ref[...] = dot_nn(da_ref[...], vo_ref[:, width:]).astype(BF)
    lse_t = jnp.transpose(lse_ref[...])
    key_at = lax.broadcasted_iota(jnp.int32, (rows, 1), 0)
    dead = (key_at >= seg) & (((key_at - seg) & (pad - 1)) >= used)
    lane = lax.broadcasted_iota(jnp.int32, (rows, 128), 1)
    sub = lax.broadcasted_iota(jnp.int32, (128, rows), 0)
    for pair in range(width // 128):
        at = pair * 128
        q = qkv_ref[:, at : at + 128]
        k = qkv_ref[:, width + at : width + at + 128]
        v = qkv_ref[:, 2 * width + at : 2 * width + at + 128]
        dc = dctx_ref[:, at : at + 128]
        dq_t, dk, dv = [], None, None
        for head in range(2):
            mine = (lane < 64) if head == 0 else (lane >= 64)
            q_one = jnp.where(mine, q, jnp.zeros_like(q))
            dc_one = jnp.where(mine, dc, jnp.zeros_like(dc))
            s_t = dot_nt(k, q_one) * (HD**-0.5 * LOG2E)
            number = 2 * pair + head
            p_t = jnp.where(dead, 0.0, jnp.exp2(s_t - lse_t[number : number + 1, :]))
            dp_t = dot_nt(v, dc_one)
            dv_one = dot_nn(p_t.astype(BF), dc_one)
            inner = row_sum(p_t * dp_t)
            ds_t = (p_t * (dp_t - inner)).astype(BF)
            dk_one = dot_nn(ds_t, q_one)
            dq_t.append(dot_tn(k, ds_t))
            dv = dv_one if dv is None else dv + dv_one
            dk = dk_one if dk is None else dk + dk_one
        dq = jnp.transpose(jnp.where(sub < 64, dq_t[0], dq_t[1])) * (HD**-0.5)
        dk = dk * (HD**-0.5)
        dhead_ref[:, at : at + 128] = row_sum(dq)
        dhead_ref[:, width + at : width + at + 128] = row_sum(dv)
        dqkv_ref[:, at : at + 128] = dq.astype(BF)
        dqkv_ref[:, width + at : width + at + 128] = dk.astype(BF)
        dqkv_ref[:, 2 * width + at : 2 * width + at + 128] = dv.astype(BF)
    part = dot_nt(dqkv_ref[:, : 2 * width], qk_ref[...]) + dot_nt(dqkv_ref[:, 2 * width :], vo_ref[:, :width])
    part_ref[...] = part.astype(BF)


def input_grad_kernel(dfirst_ref, own_ref, other_ref, grad_ref, dmem_ref):
    seg = grad_ref.shape[0]
    pad = dmem_ref.shape[0]
    dx = dfirst_ref[...] + (own_ref[...].astype(F32) + other_ref[...].astype(F32))
    grad_ref[...] = dx[:seg].astype(BF)
    dmem_ref[...] = dx[seg : seg + pad] + dx[seg + pad :]


def weight_grad_kernel(plan, kinds, me_ref, *refs):
    outs = refs[-2 * len(kinds) - 1 : -1]
    total_ref = refs[-1]
    block = total_ref.shape[0] // SLOTS
    for number, (kind, pieces) in enumerate(zip(kinds, plan)):
        at = 0
        for left, right, start, size in pieces:
            total = None
            for one, two in zip(left, right):
                add = dot_tn(refs[one][...], refs[two][:, start : start + size])
                total = add if total is None else total + add
            total_ref[:, at : at + size] = total
            at += size
        for outer in range(2):
            target = outs[2 * number + outer]
            for inner in range(8):
                place = lax.bitwise_xor(me_ref[0], slot_of(kind, outer, inner))
                begin = pl.multiple_of(place * block, block)
                target[inner] = total_ref[pl.ds(begin, block), :].astype(BF)


def exchange(values, axis, size, flip):
    return lax.ppermute(values, axis, [(i, i ^ flip) for i in range(size)])


def gather_part(own, kind, size):
    if size != SLOTS:
        full = lax.all_gather(own, "dp", axis=0, tiled=True)
        full = full.reshape(4, 2, 2, full.shape[0] // SLOTS, full.shape[1])
        full = full.transpose((2, 1, 0, 3, 4) if kind == 0 else (1, 2, 0, 3, 4))
        full = full.reshape(2, 8, *full.shape[3:])
        return full[0], full[1]
    middle, last = (2, 1) if kind == 0 else (1, 2)
    line = jnp.stack([own] + [exchange(own, "dp", size, 4 * j) for j in (1, 2, 3)])
    low = jnp.concatenate([line, exchange(line, "dp", size, middle)])
    return low, exchange(low, "dp", size, last)


def scatter_part(keep, send, kind, size):
    if size != SLOTS:
        full = jnp.stack([keep, send]).reshape(2, 2, 4, *keep.shape[1:])
        full = full.transpose((2, 1, 0, 3, 4) if kind == 0 else (2, 0, 1, 3, 4))
        full = full.reshape(SLOTS * keep.shape[1], keep.shape[2])
        return lax.psum_scatter(full, "dp", scatter_dimension=0, tiled=True).astype(F32)
    first, middle = (1, 2) if kind == 0 else (2, 1)
    got = exchange(send, "dp", size, first)
    eight = (keep.astype(F32) + got.astype(F32)).astype(BF)
    got = exchange(eight[4:], "dp", size, middle)
    four = (eight[:4].astype(F32) + got.astype(F32)).astype(BF)
    others = [exchange(four[j], "dp", size, 4 * j) for j in (1, 2, 3)]
    return four[0].astype(F32) + others[0].astype(F32) + others[1].astype(F32) + others[2].astype(F32)


def sum_all(values, axis, size):
    if size & (size - 1):
        return lax.psum(values, axis)
    flip = 1
    while flip < size:
        values = values + exchange(values, axis, size, flip)
        flip *= 2
    return values


def adam_update(weight, first_old, second_old, gradient, factor, decay_rate, step_rate):
    clipped = gradient * factor
    first_new = BETA_ONE * first_old + (1.0 - BETA_ONE) * clipped
    second_new = BETA_TWO * second_old + (1.0 - BETA_TWO) * clipped * clipped
    first_hat = first_new / (1.0 - BETA_ONE**STEP)
    second_hat = second_new / (1.0 - BETA_TWO**STEP)
    weight_new = weight - step_rate * (
        first_hat / (jnp.sqrt(second_hat) + ADAM_EPSILON) + decay_rate * weight
    )
    return (weight_new, first_new, second_new)


def shards(
    size,
    pair,
    inputs,
    cotangent,
    seg_counts,
    qkv_weight,
    out_weight,
    up_weight,
    down_weight,
    head_bias,
    shared_params,
    qkv_first,
    out_first,
    up_first,
    down_first,
    bias_first,
    shared_first,
    qkv_second,
    out_second,
    up_second,
    down_second,
    bias_second,
    shared_second,
):
    unused, segments, seg, model = inputs.shape
    width = qkv_weight.shape[2]
    hidden = up_weight.shape[1]
    used = shared_params.shape[0] - 6
    pad = 16
    rows = seg + 2 * pad
    half = hidden // 2

    me = (lax.axis_index("dp") if size == SLOTS else jnp.int32(0)).astype(jnp.int32).reshape(1)
    qkv_low = qkv_weight.astype(BF)
    out_low = out_weight.T.astype(BF)
    up_low = up_weight.astype(BF)
    down_low = down_weight.T.astype(BF)
    own_parts = [
        jnp.concatenate([qkv_low[0], qkv_low[1]], axis=1),
        jnp.concatenate([qkv_low[2], out_low], axis=1),
        up_low[:, :half],
        up_low[:, half:],
        down_low[:, :half],
        down_low[:, half:],
    ]
    kinds = (0, 1)

    def gathered(number):
        pieces = []
        for kind in kinds:
            pieces += gather_part(own_parts[2 * number + kind], kind, size)
        return call(
            functools.partial(assemble_kernel, kinds),
            [((model, model), BF)] * 2,
            [me, *pieces],
            scalars=1,
        )

    w_qk, w_vo = gathered(0)
    w_up = gathered(1)
    w_down = gathered(2)

    memory = jnp.concatenate([shared_params[:used], jnp.zeros((pad - used, model), F32)], axis=0)
    dense = 2 * rows * model
    saved = []
    tokens_out = []
    for segment in range(segments):
        tokens = inputs[0, segment]
        alive = (segment < seg_counts).astype(F32).reshape(1, 1)
        part, low, qkv, lse, ctx = call(
            attn_forward_kernel,
            [((rows, model), BF), ((rows, model), BF), ((rows, 3 * width), BF), ((rows, 128), F32), ((rows, width), BF)],
            [tokens, memory, w_qk, w_vo, head_bias],
            flops=dense * 4 * width + 4 * rows * rows * width,
        )
        other = exchange(part, "head", pair, 1)
        ffn_part, first_in, h_low, active, slope = call(
            ffn_forward_kernel,
            [((rows, model), BF), ((rows, model), F32), ((rows, model), BF), ((rows, hidden), BF), ((rows, hidden), BF)],
            [tokens, memory, part, other, *w_up, *w_down, head_bias, shared_params],
            scratch=[pltpu.VMEM((rows, model), F32)],
            flops=dense * 2 * hidden,
        )
        other = exchange(ffn_part, "head", pair, 1)
        out_rows, memory, second_in = call(
            close_kernel,
            [((seg, model), BF), ((pad, model), F32), ((rows, model), F32)],
            [first_in, ffn_part, other, shared_params, alive],
        )
        tokens_out.append(out_rows)
        saved.append((alive, low, qkv, lse, ctx, first_in, h_low, active, slope, second_in))
    outputs = jnp.stack(tokens_out)[None]

    dmem = jnp.zeros((pad, model), F32)
    grads = [None] * segments
    stacks = [None] * segments
    dbias_sum, dvec_sum, dhead_sum = [], [], []
    for segment in reversed(range(segments)):
        alive, low, qkv, lse, ctx, first_in, h_low, active, slope, second_in = saved[segment]
        part, dsecond, df_low, du, dbias, dvec_two = call(
            ffn_backward_kernel,
            [((rows, model), BF), ((rows, model), F32), ((rows, model), BF), ((rows, hidden), BF), ((1, hidden), F32), ((8, model), F32)],
            [second_in, cotangent[0, segment], dmem, alive, shared_params, *w_up, *w_down, slope],
            scratch=[pltpu.VMEM((rows, model), F32)],
            flops=dense * 2 * hidden,
        )
        other = exchange(part, "head", pair, 1)
        part, dfirst, da, dqkv, dhead, dvec_one = call(
            attn_backward_kernel,
            [((rows, model), BF), ((rows, model), F32), ((rows, model), BF), ((rows, 3 * width), BF), ((1, 2 * width), F32), ((8, model), F32)],
            [dsecond, part, other, first_in, shared_params, w_qk, w_vo, qkv, lse],
            scratch=[pltpu.VMEM((rows, width), BF)],
            flops=dense * 4 * width + 10 * rows * rows * width,
        )
        other = exchange(part, "head", pair, 1)
        grads[segment], dmem = call(
            input_grad_kernel,
            [((seg, model), BF), ((pad, model), F32)],
            [dfirst, part, other],
        )
        stacks[segment] = (low, ctx, h_low, active, df_low, du, da, dqkv)
        dbias_sum.append(dbias)
        dhead_sum.append(dhead)
        dvec_sum.append(
            jnp.stack([dvec_one[0], dvec_two[0], dvec_one[1], dvec_one[2], dvec_two[1], dvec_two[2]])
        )
    input_grad = jnp.stack(grads)[None]

    count = len(stacks)

    def weight_grad(names, plan):
        operands = [stacks[s][n] for n in names for s in range(count)]
        at = {n: [1 + i * count - 1 + s for s in range(count)] for i, n in enumerate(names)}
        steps = [[(at[a], at[b], start, length) for a, b, start, length in pieces] for pieces in plan]
        result = call(
            functools.partial(weight_grad_kernel, steps, kinds),
            [((8, model // SLOTS, model), BF)] * 4,
            [me, *operands],
            scalars=1,
            scratch=[pltpu.VMEM((model, model), F32)],
            flops=count * dense * model * 2,
        )
        return [scatter_part(result[2 * i], result[2 * i + 1], kind, size) for i, kind in enumerate(kinds)]

    low, ctx, h_low, active, df_low, du, da, dqkv = range(8)
    g_down = weight_grad((df_low, active), [[(df_low, active, 0, half)], [(df_low, active, half, half)]])
    g_up = weight_grad((h_low, du), [[(h_low, du, 0, half)], [(h_low, du, half, half)]])
    g_qkvo = weight_grad(
        (low, dqkv, da, ctx),
        [[(low, dqkv, 0, 2 * width)], [(low, dqkv, 2 * width, width), (da, ctx, 0, width)]],
    )

    head_grad = jnp.concatenate([sum(dhead_sum), sum(dbias_sum)], axis=1)
    shared_grad = jnp.concatenate([dmem[:used], sum(dvec_sum)], axis=0)
    small = jnp.concatenate([shared_grad, head_grad.reshape(-1, model)], axis=0)
    small = sum_all(small, "dp", size)
    shared_grad = small[: used + 6]
    bias_grad = small[used + 6 :].reshape(1, -1)

    matrix_squares = sum(jnp.sum(g * g) for g in (*g_down, *g_up, *g_qkvo))
    squares = sum_all(jnp.full((8, 128), matrix_squares), "dp", size)
    squares = sum_all(squares + jnp.sum(bias_grad * bias_grad), "head", pair)
    squares_total = squares[0, 0] + jnp.sum(shared_grad * shared_grad)
    grad_norm = jnp.sqrt(squares_total)
    factor = CLIP_NORM / jnp.maximum(grad_norm, CLIP_NORM)

    qkv_grad = jnp.stack([g_qkvo[0][:, :width], g_qkvo[0][:, width:], g_qkvo[1][:, :width]])
    out_grad = g_qkvo[1][:, width:].T
    up_grad = jnp.concatenate(g_up, axis=1)
    down_grad = jnp.concatenate(g_down, axis=1).T
    qkv_result = adam_update(qkv_weight, qkv_first, qkv_second, qkv_grad, factor, DECAY_RATE, LEARN_RATE)
    out_result = adam_update(out_weight, out_first, out_second, out_grad, factor, DECAY_RATE, LEARN_RATE)
    up_result = adam_update(up_weight, up_first, up_second, up_grad, factor, DECAY_RATE, LEARN_RATE)
    down_result = adam_update(down_weight, down_first, down_second, down_grad, factor, DECAY_RATE, LEARN_RATE)
    bias_result = adam_update(head_bias, bias_first, bias_second, bias_grad, factor, 0.0, VECTOR_RATE)
    shared_result = adam_update(shared_params, shared_first, shared_second, shared_grad, factor, 0.0, VECTOR_RATE)
    results = (qkv_result, out_result, up_result, down_result, bias_result, shared_result)
    return (outputs, input_grad, grad_norm) + tuple(r[i] for i in range(3) for r in results)


def solution(mesh):
    weights = (P(None, "dp", "head"), P("head", "dp"), P("dp", "head"), P("head", "dp"), P("head", None), P())
    rows = P("dp", None, None, None)
    return jax.shard_map(
        functools.partial(shards, mesh.shape["dp"], mesh.shape["head"]),
        mesh=mesh,
        in_specs=(rows, rows, P("dp")) + weights * 3,
        out_specs=(rows, rows, P()) + weights * 3,
        check_vma=False,
    )
```

```python
import functools
import math

import jax
import jax.numpy as jnp
from jax import lax
from jax.experimental import pallas as pl
from jax.experimental.pallas import tpu as pltpu
from jax.sharding import PartitionSpec as P

HD = 64
STEP = 10
EPSILON = 1e-06
BETA_ONE = 0.9
BETA_TWO = 0.999
LEARN_RATE = 0.1
VECTOR_RATE = 0.6
DECAY_RATE = 0.01
ADAM_EPSILON = 1e-08
CLIP_NORM = 1.0

BF = jnp.bfloat16
F32 = jnp.float32
LOG2E = math.log2(math.e)
NEG = -1e30
SLOTS = 16
LOW, CTX, H_LOW, ACTIVE, DF_LOW, DU, DA, DQKV = range(8)


def dot_nn(a, b):
    return lax.dot_general(a, b, (((1,), (0,)), ((), ())), preferred_element_type=F32)


def dot_nt(a, b):
    return lax.dot_general(a, b, (((1,), (1,)), ((), ())), preferred_element_type=F32)


def dot_tn(a, b):
    return lax.dot_general(a, b, (((0,), (0,)), ((), ())), preferred_element_type=F32)


def norm_stats(values):
    average = jnp.mean(values, axis=-1, keepdims=True)
    centered = values - average
    variance = jnp.mean(centered * centered, axis=-1, keepdims=True)
    scale = lax.rsqrt(variance + EPSILON)
    return centered * scale, scale


def norm_back(grad, gain, unit, scale):
    inner = grad * gain
    mean_one = jnp.mean(inner, axis=-1, keepdims=True)
    mean_two = jnp.mean(inner * unit, axis=-1, keepdims=True)
    return scale * (inner - mean_one - unit * mean_two)


def row_sum(values):
    return jnp.sum(values, axis=0, keepdims=True)


def call(kernel, outs, args, scalars=0, scratch=(), flops=0):
    moved = sum(a.size * a.dtype.itemsize for a in args)
    moved += sum(math.prod(s) * jnp.dtype(d).itemsize for s, d in outs)
    return pl.pallas_call(
        kernel,
        out_shape=[jax.ShapeDtypeStruct(s, d) for s, d in outs],
        in_specs=[pl.BlockSpec(memory_space=pltpu.SMEM)] * scalars
        + [pl.BlockSpec(memory_space=pltpu.VMEM)] * (len(args) - scalars),
        out_specs=[pl.BlockSpec(memory_space=pltpu.VMEM)] * len(outs),
        scratch_shapes=list(scratch),
        cost_estimate=pl.CostEstimate(
            flops=flops, bytes_accessed=moved, transcendentals=0
        ),
        compiler_params=pltpu.CompilerParams(vmem_limit_bytes=16 << 20),
    )(*args)


def slot_of(kind, number):
    if kind[0] == "z":
        outer, mid, z = number // 8, number // 4 % 2, number % 4
        return (outer + 2 * mid if kind[1] == "a" else 2 * outer + mid) + 4 * z
    outer, z, inner = number // 8, number // 2 % 4, number % 2
    return (2 * outer + inner if kind[1] == "a" else outer + 2 * inner) + 4 * z


def assemble_kernel(kinds, counts, me_ref, *refs):
    at = sum(counts)
    begin = 0
    for part, (kind, count) in enumerate(zip(kinds, counts)):
        target = refs[at + part]
        block = target.shape[0] // SLOTS
        number = 0
        for source in refs[begin : begin + count]:
            for inner in range(source.shape[0]):
                place = lax.bitwise_xor(me_ref[0], slot_of(kind, number))
                start = pl.multiple_of(place * block, block)
                target[pl.ds(start, block), :] = source[inner]
                number += 1
        begin += count


def attn_forward_kernel(token_ref, mem_ref, qk_ref, vo_ref, bias_ref, part_ref, low_ref, qkv_ref, lse_ref, ctx_ref):
    seg = token_ref.shape[0]
    pad = mem_ref.shape[0]
    rows = seg + 2 * pad
    width = vo_ref.shape[1] // 2
    used = 10
    memory = mem_ref[...].astype(BF)
    low_ref[:seg, :] = token_ref[...]
    low_ref[seg : seg + pad, :] = memory
    low_ref[seg + pad :, :] = memory
    low = low_ref[...]
    qk = dot_nn(low, qk_ref[...])
    qkv_ref[:, :width] = (qk[:, :width] + bias_ref[:, :width]).astype(BF)
    qkv_ref[:, width : 2 * width] = qk[:, width:].astype(BF)
    v_all = dot_nn(low, vo_ref[:, :width])
    qkv_ref[:, 2 * width :] = (v_all + bias_ref[:, width : 2 * width]).astype(BF)
    key_at = lax.broadcasted_iota(jnp.int32, (1, rows), 1)
    dead = (key_at >= seg) & (((key_at - seg) & (pad - 1)) >= used)
    lane = lax.broadcasted_iota(jnp.int32, (rows, 128), 1)
    lse = jnp.zeros((rows, 128), F32)
    for pair in range(width // 128):
        at = pair * 128
        q = qkv_ref[:, at : at + 128]
        k = qkv_ref[:, width + at : width + at + 128]
        v = qkv_ref[:, 2 * width + at : 2 * width + at + 128]
        outs = []
        for head in range(2):
            mine = (lane < 64) if head == 0 else (lane >= 64)
            s = dot_nt(jnp.where(mine, q, jnp.zeros_like(q)), k) * (HD**-0.5 * LOG2E)
            s = jnp.where(dead, NEG, s)
            top = jnp.max(s, axis=1, keepdims=True)
            e = jnp.exp2(s - top)
            total = jnp.sum(e, axis=1, keepdims=True)
            p = (e * (1.0 / total)).astype(BF)
            outs.append(dot_nn(p, v))
            lse = jnp.where(lane == 2 * pair + head, top + jnp.log2(total), lse)
        ctx_ref[:, at : at + 128] = jnp.where(lane < 64, outs[0], outs[1]).astype(BF)
    lse_ref[...] = lse
    part_ref[...] = dot_nt(ctx_ref[...], vo_ref[:, width:]).astype(BF)


def ffn_forward_kernel(token_ref, mem_ref, own_ref, other_ref, up0_ref, up1_ref, down0_ref, down1_ref, bias_ref, shared_ref,
                       part_ref, first_ref, low_ref, act_ref, slope_ref, total_ref):
    seg = token_ref.shape[0]
    pad = mem_ref.shape[0]
    used = 10
    width = 384
    attn = own_ref[...].astype(F32) + other_ref[...].astype(F32) + shared_ref[used : used + 1, :]
    first_ref[:seg, :] = token_ref[...].astype(F32) + attn[:seg]
    first_ref[seg : seg + pad, :] = mem_ref[...] + attn[seg : seg + pad]
    first_ref[seg + pad :, :] = mem_ref[...] + attn[seg + pad :]
    unit, unused = norm_stats(first_ref[...])
    hidden = unit * shared_ref[used + 2 : used + 3, :] + shared_ref[used + 3 : used + 4, :]
    low_ref[...] = hidden.astype(BF)
    low = low_ref[...]
    for half, (up_ref, down_ref) in enumerate(((up0_ref, down0_ref), (up1_ref, down1_ref))):
        span = up_ref.shape[1]
        for piece in range(span // width):
            at = piece * width
            to = half * span + at
            u = dot_nn(low, up_ref[:, at : at + width]) + bias_ref[:, 2 * width + to : 2 * width + to + width]
            cdf = 0.5 + 0.5 * lax.erf(u * (0.5**0.5))
            density = jnp.exp2(u * u * (-0.5 * LOG2E)) * ((2.0 * math.pi) ** -0.5)
            active = (u * cdf).astype(BF)
            act_ref[:, to : to + width] = active
            slope_ref[:, to : to + width] = (cdf + u * density).astype(BF)
            add = dot_nt(active, down_ref[:, at : at + width])
            if to == 0:
                total_ref[...] = add
            else:
                total_ref[...] += add
    part_ref[...] = total_ref[...].astype(BF)


def close_rows(first_ref, own_ref, other_ref, shared_ref):
    used = 10
    unit, unused = norm_stats(first_ref[...])
    hidden = unit * shared_ref[used + 2 : used + 3, :] + shared_ref[used + 3 : used + 4, :]
    return hidden + (own_ref[...].astype(F32) + other_ref[...].astype(F32)) + shared_ref[used + 1 : used + 2, :]


def close_kernel(first_ref, own_ref, other_ref, shared_ref, alive_ref, out_ref, mem_ref, second_ref):
    used = 10
    seg = out_ref.shape[0]
    pad = mem_ref.shape[0]
    second = close_rows(first_ref, own_ref, other_ref, shared_ref)
    second_ref[...] = second
    unit, unused = norm_stats(second)
    result = unit * shared_ref[used + 4 : used + 5, :] + shared_ref[used + 5 : used + 6, :]
    out_ref[...] = (result[:seg] * alive_ref[...]).astype(BF)
    row = lax.broadcasted_iota(jnp.int32, (pad, result.shape[1]), 0)
    mem_ref[...] = jnp.where(row < used, result[seg + pad :], 0.0)


def ffn_backward_kernel(second_ref, cot_ref, dmem_ref, alive_ref, shared_ref, up0_ref, up1_ref, down0_ref, down1_ref, slope_ref,
                        part_ref, dsecond_ref, dlow_ref, du_ref, dbias_ref, dvec_ref, total_ref):
    used = 10
    seg = cot_ref.shape[0]
    pad = dmem_ref.shape[0]
    width = 384
    unit, scale = norm_stats(second_ref[...])
    dy = jnp.concatenate(
        [cot_ref[...].astype(F32) * alive_ref[...], jnp.zeros((pad, unit.shape[1]), F32), dmem_ref[...] * alive_ref[...]], axis=0
    )
    dsecond = norm_back(dy, shared_ref[used + 4 : used + 5, :], unit, scale)
    dsecond_ref[...] = dsecond
    dvec_ref[0:1, :] = row_sum(dsecond)
    dvec_ref[1:2, :] = row_sum(dy * unit)
    dvec_ref[2:3, :] = row_sum(dy)
    dvec_ref[3:, :] = jnp.zeros((dvec_ref.shape[0] - 3, unit.shape[1]), F32)
    dlow_ref[...] = dsecond.astype(BF)
    dlow = dlow_ref[...]
    for half, (up_ref, down_ref) in enumerate(((up0_ref, down0_ref), (up1_ref, down1_ref))):
        span = up_ref.shape[1]
        for piece in range(span // width):
            at = piece * width
            to = half * span + at
            dg = dot_nn(dlow, down_ref[:, at : at + width])
            du = dg * slope_ref[:, to : to + width].astype(F32)
            dbias_ref[:, to : to + width] = row_sum(du)
            du_low = du.astype(BF)
            du_ref[:, to : to + width] = du_low
            add = dot_nt(du_low, up_ref[:, at : at + width])
            if to == 0:
                total_ref[...] = add
            else:
                total_ref[...] += add
    part_ref[...] = total_ref[...].astype(BF)


def attn_backward_kernel(dsecond_ref, own_ref, other_ref, first_ref, shared_ref, qk_ref, vo_ref, qkv_ref, lse_ref,
                         part_ref, dfirst_ref, da_ref, dqkv_ref, dhead_ref, dvec_ref, dctx_ref):
    used = 10
    rows = first_ref.shape[0]
    width = vo_ref.shape[1] // 2
    pad = 16
    seg = rows - 2 * pad
    dhidden = dsecond_ref[...] + (own_ref[...].astype(F32) + other_ref[...].astype(F32))
    unit, scale = norm_stats(first_ref[...])
    dfirst = norm_back(dhidden, shared_ref[used + 2 : used + 3, :], unit, scale)
    dfirst_ref[...] = dfirst
    dvec_ref[0:1, :] = row_sum(dfirst)
    dvec_ref[1:2, :] = row_sum(dhidden * unit)
    dvec_ref[2:3, :] = row_sum(dhidden)
    dvec_ref[3:, :] = jnp.zeros((dvec_ref.shape[0] - 3, unit.shape[1]), F32)
    da_ref[...] = dfirst.astype(BF)
    dctx_ref[...] = dot_nn(da_ref[...], vo_ref[:, width:]).astype(BF)
    lse_t = jnp.transpose(lse_ref[...])
    key_at = lax.broadcasted_iota(jnp.int32, (rows, 1), 0)
    dead = (key_at >= seg) & (((key_at - seg) & (pad - 1)) >= used)
    lane = lax.broadcasted_iota(jnp.int32, (rows, 128), 1)
    sub = lax.broadcasted_iota(jnp.int32, (128, rows), 0)
    for pair in range(width // 128):
        at = pair * 128
        q = qkv_ref[:, at : at + 128]
        k = qkv_ref[:, width + at : width + at + 128]
        v = qkv_ref[:, 2 * width + at : 2 * width + at + 128]
        dc = dctx_ref[:, at : at + 128]
        dq_t, dk, dv = [], None, None
        for head in range(2):
            mine = (lane < 64) if head == 0 else (lane >= 64)
            q_one = jnp.where(mine, q, jnp.zeros_like(q))
            dc_one = jnp.where(mine, dc, jnp.zeros_like(dc))
            s_t = dot_nt(k, q_one) * (HD**-0.5 * LOG2E)
            number = 2 * pair + head
            p_t = jnp.where(dead, 0.0, jnp.exp2(s_t - lse_t[number : number + 1, :]))
            dp_t = dot_nt(v, dc_one)
            dv_one = dot_nn(p_t.astype(BF), dc_one)
            inner = row_sum(p_t * dp_t)
            ds_t = (p_t * (dp_t - inner)).astype(BF)
            dk_one = dot_nn(ds_t, q_one)
            dq_t.append(dot_tn(k, ds_t))
            dv = dv_one if dv is None else dv + dv_one
            dk = dk_one if dk is None else dk + dk_one
        dq = jnp.transpose(jnp.where(sub < 64, dq_t[0], dq_t[1])) * (HD**-0.5)
        dk = dk * (HD**-0.5)
        dhead_ref[:, at : at + 128] = row_sum(dq)
        dhead_ref[:, width + at : width + at + 128] = row_sum(dv)
        dqkv_ref[:, at : at + 128] = dq.astype(BF)
        dqkv_ref[:, width + at : width + at + 128] = dk.astype(BF)
        dqkv_ref[:, 2 * width + at : 2 * width + at + 128] = dv.astype(BF)
    part = dot_nt(dqkv_ref[:, : 2 * width], qk_ref[...]) + dot_nt(dqkv_ref[:, 2 * width :], vo_ref[:, :width])
    part_ref[...] = part.astype(BF)


def input_grad_kernel(dfirst_ref, own_ref, other_ref, grad_ref, dmem_ref):
    seg = grad_ref.shape[0]
    pad = dmem_ref.shape[0]
    dx = dfirst_ref[...] + (own_ref[...].astype(F32) + other_ref[...].astype(F32))
    grad_ref[...] = dx[:seg].astype(BF)
    dmem_ref[...] = dx[seg : seg + pad] + dx[seg + pad :]


def weight_grad_kernel(plan, kinds, sizes, me_ref, *refs):
    count = len(kinds) * len(sizes)
    outs = refs[-count - 1 : -1]
    total_ref = refs[-1]
    block = total_ref.shape[0] // SLOTS
    for part, (kind, pieces) in enumerate(zip(kinds, plan)):
        at = 0
        for left, right, start, size in pieces:
            total = None
            for one, two in zip(left, right):
                add = dot_tn(refs[one][...], refs[two][:, start : start + size])
                total = add if total is None else total + add
            total_ref[:, at : at + size] = total
            at += size
        number = 0
        for target in outs[part * len(sizes) : (part + 1) * len(sizes)]:
            for inner in range(target.shape[0]):
                place = lax.bitwise_xor(me_ref[0], slot_of(kind, number))
                begin = pl.multiple_of(place * block, block)
                target[inner] = total_ref[pl.ds(begin, block), :].astype(BF)
                number += 1


def exchange(values, axis, size, flip):
    return lax.ppermute(values, axis, [(i, i ^ flip) for i in range(size)])


def after(value, *others):
    return lax.optimization_barrier((value, *others))[0]


def add_low(*values):
    total = values[0].astype(F32)
    for value in values[1:]:
        total = total + value.astype(F32)
    return total


def canonical_split(full, kind, sizes):
    full = full.reshape(SLOTS, full.shape[0] // SLOTS, full.shape[1])
    full = jnp.stack([full[slot_of(kind, number)] for number in range(SLOTS)])
    ends = [sum(sizes[: i + 1]) for i in range(len(sizes))]
    return [full[end - size : end] for end, size in zip(ends, sizes)]


def canonical_join(pieces, kind):
    full = jnp.concatenate(pieces)
    order = [slot_of(kind, number) for number in range(SLOTS)]
    full = jnp.stack([full[order.index(d)] for d in range(SLOTS)])
    return full.reshape(-1, full.shape[-1])


def line_stage(own, size):
    return [own] + [exchange(own, "dp", size, 4 * j) for j in (1, 2, 3)]


def sum_all(values, axis, size):
    if size & (size - 1):
        return lax.psum(values, axis)
    flip = 1
    while flip < size:
        if flip * 4 <= size:
            near, far, both = [exchange(values, axis, size, flip * j) for j in (1, 2, 3)]
            values = (values + near) + (far + both)
            flip *= 4
        else:
            values = values + exchange(values, axis, size, flip)
            flip *= 2
    return values


def adam_update(weight, first_old, second_old, gradient, factor, decay_rate, step_rate):
    clipped = gradient * factor
    first_new = BETA_ONE * first_old + (1.0 - BETA_ONE) * clipped
    second_new = BETA_TWO * second_old + (1.0 - BETA_TWO) * clipped * clipped
    first_hat = first_new / (1.0 - BETA_ONE**STEP)
    second_hat = second_new / (1.0 - BETA_TWO**STEP)
    weight_new = weight - step_rate * (
        first_hat / (jnp.sqrt(second_hat) + ADAM_EPSILON) + decay_rate * weight
    )
    return (weight_new, first_new, second_new)


def shards(
    size,
    pair,
    inputs,
    cotangent,
    seg_counts,
    qkv_weight,
    out_weight,
    up_weight,
    down_weight,
    head_bias,
    shared_params,
    qkv_first,
    out_first,
    up_first,
    down_first,
    bias_first,
    shared_first,
    qkv_second,
    out_second,
    up_second,
    down_second,
    bias_second,
    shared_second,
):
    unused, segments, seg, model = inputs.shape
    width = qkv_weight.shape[2]
    hidden = up_weight.shape[1]
    used = shared_params.shape[0] - 6
    pad = 16
    rows = seg + 2 * pad
    half = hidden // 2

    me = (lax.axis_index("dp") if size == SLOTS else jnp.int32(0)).astype(jnp.int32).reshape(1)
    qkv_low = qkv_weight.astype(BF)
    out_low = out_weight.T.astype(BF)
    up_low = up_weight.astype(BF)
    down_low = down_weight.T.astype(BF)
    own = [
        jnp.stack([jnp.concatenate([qkv_low[0], qkv_low[1]], axis=1), jnp.concatenate([qkv_low[2], out_low], axis=1)]),
        jnp.stack([up_low[:, :half], up_low[:, half:]]),
        jnp.stack([down_low[:, :half], down_low[:, half:]]),
    ]

    def assembled(kinds, pieces):
        return call(
            functools.partial(assemble_kernel, kinds, [len(p) for p in pieces]),
            [((model, model), BF)] * 2,
            [me, *pieces[0], *pieces[1]],
            scalars=1,
        )

    z_first, z_mid = ("za", "zb"), ("xa", "xb")
    if size == SLOTS:

        def spread(lines):
            low_a = jnp.concatenate([lines[0], exchange(lines[0], "dp", size, 2)])
            low_b = jnp.concatenate([lines[1], exchange(lines[1], "dp", size, 1)])
            return low_a, low_b

        def finish(low_a, low_b):
            return exchange(low_a, "dp", size, 1), exchange(low_b, "dp", size, 2)

        pair_c = [jnp.stack([own[2][i], exchange(own[2][i], "dp", size, 1 + i)]) for i in range(2)]
        line_one = line_stage(own[0], size)
        line_two = line_stage(after(own[1], *line_one), size)
        low_one = spread([jnp.stack([v[i] for v in line_one]) for i in range(2)])
        line_three = line_stage(after(jnp.stack(pair_c), *line_two, *low_one), size)
        high_one = finish(*low_one)
        low_two = spread([after(jnp.stack([v[i] for v in line_two]), *high_one) for i in range(2)])
        high_two = finish(*low_two)
        low_c = [jnp.concatenate([v[i] for v in line_three]) for i in range(2)]
        low_c = [after(v, *high_two) for v in low_c]
        high_c = [exchange(low_c[i], "dp", size, 2 - i) for i in range(2)]
        high_one = [after(h, *low_two) for h in high_one]
        w_qk, w_vo = assembled(z_first, [[low_one[i], high_one[i]] for i in range(2)])
        w_up = assembled(z_first, [[low_two[i], high_two[i]] for i in range(2)])
        w_down = assembled(z_mid, [[low_c[i], high_c[i]] for i in range(2)])
    else:

        def whole(number, kinds, sizes):
            pieces = [lax.all_gather(own[number][i], "dp", axis=0, tiled=True) for i in range(2)]
            return assembled(kinds, [canonical_split(p, kind, sizes) for p, kind in zip(pieces, kinds)])

        w_qk, w_vo = whole(0, z_first, (8, 8))
        w_up = whole(1, z_first, (8, 8))
        w_down = whole(2, z_mid, (8, 8))

    memory = jnp.concatenate([shared_params[:used], jnp.zeros((pad - used, model), F32)], axis=0)
    dense = 2 * rows * model
    saved = []
    tokens_out = []
    for segment in range(segments):
        tokens = inputs[0, segment]
        alive = (segment < seg_counts).astype(F32).reshape(1, 1)
        part, low, qkv, lse, ctx = call(
            attn_forward_kernel,
            [((rows, model), BF), ((rows, model), BF), ((rows, 3 * width), BF), ((rows, 128), F32), ((rows, width), BF)],
            [tokens, memory, w_qk, w_vo, head_bias],
            flops=dense * 4 * width + 4 * rows * rows * width,
        )
        other = exchange(part, "head", pair, 1)
        ffn_part, first_in, h_low, active, slope = call(
            ffn_forward_kernel,
            [((rows, model), BF), ((rows, model), F32), ((rows, model), BF), ((rows, hidden), BF), ((rows, hidden), BF)],
            [tokens, memory, part, other, *w_up, *w_down, head_bias, shared_params],
            scratch=[pltpu.VMEM((rows, model), F32)],
            flops=dense * 2 * hidden,
        )
        other = exchange(ffn_part, "head", pair, 1)
        out_rows, memory, second_in = call(
            close_kernel,
            [((seg, model), BF), ((pad, model), F32), ((rows, model), F32)],
            [first_in, ffn_part, other, shared_params, alive],
        )
        tokens_out.append(out_rows)
        saved.append((alive, low, qkv, lse, ctx, first_in, h_low, active, slope, second_in))
    outputs = jnp.stack(tokens_out)[None]

    count = segments

    def weight_grad(names, plan):
        kinds, sizes = z_first, (8, 8)
        operands = [stacks[s][n] for n in names for s in range(count)]
        at = {n: [i * count + s for s in range(count)] for i, n in enumerate(names)}
        steps = [[(at[a], at[b], start, length) for a, b, start, length in pieces] for pieces in plan]
        result = call(
            functools.partial(weight_grad_kernel, steps, kinds, sizes),
            [((length, model // SLOTS, model), BF) for kind in kinds for length in sizes],
            [me, *operands],
            scalars=1,
            scratch=[pltpu.VMEM((model, model), F32)],
            flops=count * dense * model * 2,
        )
        return result[: len(sizes)], result[len(sizes) :]

    dmem = jnp.zeros((pad, model), F32)
    grads = [None] * segments
    stacks = [None] * segments
    dbias_sum, dvec_sum, dhead_sum = [], [], []
    for segment in reversed(range(segments)):
        alive, low, qkv, lse, ctx, first_in, h_low, active, slope, second_in = saved[segment]
        part, dsecond, df_low, du, dbias, dvec_two = call(
            ffn_backward_kernel,
            [((rows, model), BF), ((rows, model), F32), ((rows, model), BF), ((rows, hidden), BF), ((1, hidden), F32), ((8, model), F32)],
            [second_in, cotangent[0, segment], dmem, alive, shared_params, *w_up, *w_down, slope],
            scratch=[pltpu.VMEM((rows, model), F32)],
            flops=dense * 2 * hidden,
        )
        other = exchange(part, "head", pair, 1)
        stacks[segment] = (low, ctx, h_low, active, df_low, du)
        if segment == 0:
            dw_down = weight_grad((DF_LOW, ACTIVE), [[(DF_LOW, ACTIVE, 0, half)], [(DF_LOW, ACTIVE, half, half)]])
            dw_up = weight_grad((H_LOW, DU), [[(H_LOW, DU, 0, half)], [(H_LOW, DU, half, half)]])
            dsecond = after(dsecond, dw_up[0][0])
        part, dfirst, da, dqkv, dhead, dvec_one = call(
            attn_backward_kernel,
            [((rows, model), BF), ((rows, model), F32), ((rows, model), BF), ((rows, 3 * width), BF), ((1, 2 * width), F32), ((8, model), F32)],
            [dsecond, part, other, first_in, shared_params, w_qk, w_vo, qkv, lse],
            scratch=[pltpu.VMEM((rows, width), BF)],
            flops=dense * 4 * width + 10 * rows * rows * width,
        )
        other = exchange(part, "head", pair, 1)
        grads[segment], dmem = call(
            input_grad_kernel,
            [((seg, model), BF), ((pad, model), F32)],
            [dfirst, part, other],
        )
        stacks[segment] += (da, dqkv)
        dbias_sum.append(dbias)
        dhead_sum.append(dhead)
        dvec_sum.append(
            jnp.stack([dvec_one[0], dvec_two[0], dvec_one[1], dvec_one[2], dvec_two[1], dvec_two[2]])
        )
    input_grad = jnp.stack(grads)[None]

    def fallback(parts, kinds):
        full = [canonical_join(p, kind) for p, kind in zip(parts, kinds)]
        full = jnp.concatenate(full, axis=1)
        return lax.psum_scatter(full, "dp", scatter_dimension=0, tiled=True).astype(F32)

    flips = ((1, 2), (2, 1))

    def first_hop(parts):
        return [exchange(parts[i][1], "dp", size, flips[i][0]) for i in range(2)]

    def add_first(parts, got):
        return [add_low(parts[i][0], got[i]).astype(BF) for i in range(2)]

    def second_hop(eight):
        return [exchange(eight[i][4:], "dp", size, flips[i][1]) for i in range(2)]

    def add_second(eight, got):
        return jnp.concatenate([add_low(eight[i][:4], got[i]).astype(BF) for i in range(2)], axis=2)

    def line_sum(four):
        return add_low(four[0], *[exchange(four[j], "dp", size, 4 * j) for j in (1, 2, 3)])

    dw_qkvo = weight_grad(
        (LOW, DQKV, DA, CTX),
        [[(LOW, DQKV, 0, 2 * width)], [(LOW, DQKV, 2 * width, width), (DA, CTX, 0, width)]],
    )
    if size == SLOTS:
        got_down, got_up, got_qkvo = first_hop(dw_down), first_hop(dw_up), first_hop(dw_qkvo)
        eight_qkvo = add_first(dw_qkvo, got_qkvo)
        eight_down = add_first(dw_down, [after(g, dmem) for g in got_down])
        eight_up = add_first(dw_up, [after(g, dmem) for g in got_up])
        four_down = add_second(eight_down, second_hop(eight_down))
        four_up = add_second(eight_up, second_hop(eight_up))
        four_qkvo = add_second(eight_qkvo, second_hop(eight_qkvo))
        g_down, g_up, g_qkvo = line_sum(four_down), line_sum(four_up), line_sum(four_qkvo)
    else:
        g_down, g_up, g_qkvo = (fallback(d, z_first) for d in (dw_down, dw_up, dw_qkvo))

    head_grad = jnp.concatenate([sum(dhead_sum), sum(dbias_sum)], axis=1)
    shared_grad = jnp.concatenate([dmem[:used], sum(dvec_sum)], axis=0)
    small = jnp.concatenate([shared_grad, head_grad.reshape(-1, model)], axis=0)
    small = sum_all(small, "dp", size)
    shared_grad = small[: used + 6]
    bias_grad = small[used + 6 :].reshape(1, -1)

    matrix_squares = sum(jnp.sum(g * g) for g in (g_down, g_up, g_qkvo))
    squares = sum_all(jnp.full((8, 128), matrix_squares), "dp", size)
    squares = sum_all(squares + jnp.sum(bias_grad * bias_grad), "head", pair)
    squares_total = squares[0, 0] + jnp.sum(shared_grad * shared_grad)
    grad_norm = jnp.sqrt(squares_total)
    factor = CLIP_NORM / jnp.maximum(grad_norm, CLIP_NORM)

    qkv_grad = jnp.stack([g_qkvo[:, i * width : (i + 1) * width] for i in range(3)])
    out_grad = g_qkvo[:, 3 * width :].T
    up_grad = g_up
    down_grad = g_down.T
    qkv_result = adam_update(qkv_weight, qkv_first, qkv_second, qkv_grad, factor, DECAY_RATE, LEARN_RATE)
    out_result = adam_update(out_weight, out_first, out_second, out_grad, factor, DECAY_RATE, LEARN_RATE)
    up_result = adam_update(up_weight, up_first, up_second, up_grad, factor, DECAY_RATE, LEARN_RATE)
    down_result = adam_update(down_weight, down_first, down_second, down_grad, factor, DECAY_RATE, LEARN_RATE)
    bias_result = adam_update(head_bias, bias_first, bias_second, bias_grad, factor, 0.0, VECTOR_RATE)
    shared_result = adam_update(shared_params, shared_first, shared_second, shared_grad, factor, 0.0, VECTOR_RATE)
    results = (qkv_result, out_result, up_result, down_result, bias_result, shared_result)
    return (outputs, input_grad, grad_norm) + tuple(r[i] for i in range(3) for r in results)


def solution(mesh):
    weights = (P(None, "dp", "head"), P("head", "dp"), P("dp", "head"), P("head", "dp"), P("head", None), P())
    rows = P("dp", None, None, None)
    return jax.shard_map(
        functools.partial(shards, mesh.shape["dp"], mesh.shape["head"]),
        mesh=mesh,
        in_specs=(rows, rows, P("dp")) + weights * 3,
        out_specs=(rows, rows, P()) + weights * 3,
        check_vma=False,
    )
```

```python
import functools
import math

import jax
import jax.numpy as jnp
from jax import lax
from jax.experimental import pallas as pl
from jax.experimental.pallas import tpu as pltpu
from jax.sharding import PartitionSpec as P

HD = 64
STEP = 10
EPSILON = 1e-06
BETA_ONE = 0.9
BETA_TWO = 0.999
LEARN_RATE = 0.1
VECTOR_RATE = 0.6
DECAY_RATE = 0.01
ADAM_EPSILON = 1e-08
CLIP_NORM = 1.0

BF = jnp.bfloat16
F32 = jnp.float32
LOG2E = math.log2(math.e)
NEG = -1e30
SLOTS = 16
PAD = 16
USED = 10
WIDE = 384
CHUNK = 256
LOW, CTX, H_LOW, ACTIVE, DF_LOW, DU, DA, DQKV = range(8)


def dot_nn(a, b):
    return lax.dot_general(a, b, (((1,), (0,)), ((), ())), preferred_element_type=F32)


def dot_nt(a, b):
    return lax.dot_general(a, b, (((1,), (1,)), ((), ())), preferred_element_type=F32)


def dot_tn(a, b):
    return lax.dot_general(a, b, (((0,), (0,)), ((), ())), preferred_element_type=F32)


def norm_stats(values):
    average = jnp.mean(values, axis=-1, keepdims=True)
    centered = values - average
    variance = jnp.mean(centered * centered, axis=-1, keepdims=True)
    scale = lax.rsqrt(variance + EPSILON)
    return centered * scale, scale


def norm_back(grad, gain, unit, scale):
    inner = grad * gain
    mean_one = jnp.mean(inner, axis=-1, keepdims=True)
    mean_two = jnp.mean(inner * unit, axis=-1, keepdims=True)
    return scale * (inner - mean_one - unit * mean_two)


def row_sum(values):
    return jnp.sum(values, axis=0, keepdims=True)


def call(kernel, outs, args, scalars=0, scratch=()):
    return pl.pallas_call(
        kernel,
        out_shape=[jax.ShapeDtypeStruct(s, d) for s, d in outs],
        in_specs=[pl.BlockSpec(memory_space=pltpu.SMEM)] * scalars
        + [pl.BlockSpec(memory_space=pltpu.VMEM)] * (len(args) - scalars),
        out_specs=[pl.BlockSpec(memory_space=pltpu.VMEM)] * len(outs),
        scratch_shapes=list(scratch),
        cost_estimate=pl.CostEstimate(flops=0, bytes_accessed=0, transcendentals=0),
        compiler_params=pltpu.CompilerParams(vmem_limit_bytes=16 << 20),
    )(*args)


def slot_of(kind, number):
    if kind[0] == "z":
        outer, mid, z = number // 8, number // 4 % 2, number % 4
        return (outer + 2 * mid if kind[1] == "a" else 2 * outer + mid) + 4 * z
    outer, z, inner = number // 8, number // 2 % 4, number % 2
    return (2 * outer + inner if kind[1] == "a" else outer + 2 * inner) + 4 * z


def assemble_kernel(kinds, counts, joined, me_ref, *refs):
    at = sum(counts)
    begin = 0
    for part, (kind, count) in enumerate(zip(kinds, counts)):
        target = refs[at] if joined else refs[at + part]
        block = target.shape[0] // SLOTS
        number = 0
        for source in refs[begin : begin + count]:
            length = source.shape[2]
            column = part * length if joined else 0
            for inner in range(source.shape[0]):
                place = lax.bitwise_xor(me_ref[0], slot_of(kind, number))
                start = pl.multiple_of(place * block, block)
                target[pl.ds(start, block), column : column + length] = source[inner]
                number += 1
        begin += count


def attn_rows(low_ref, qk_ref, vo_ref, bias_ref, part_ref, qkv_ref, lse_ref, ctx_ref):
    rows = low_ref.shape[0]
    width = vo_ref.shape[1] // 2
    seg = rows - 2 * PAD
    low = low_ref[...]
    qk = dot_nn(low, qk_ref[...])
    qkv_ref[:, :width] = (qk[:, :width] + bias_ref[:, :width]).astype(BF)
    qkv_ref[:, width : 2 * width] = qk[:, width:].astype(BF)
    v_all = dot_nn(low, vo_ref[:, :width])
    qkv_ref[:, 2 * width :] = (v_all + bias_ref[:, width : 2 * width]).astype(BF)
    key_at = lax.broadcasted_iota(jnp.int32, (1, rows), 1)
    dead = (key_at >= seg) & (((key_at - seg) & (PAD - 1)) >= USED)
    lane = lax.broadcasted_iota(jnp.int32, (rows, 128), 1)
    lse_ref[...] = jnp.zeros_like(lse_ref)

    def heads(pair, carry):
        at = pl.multiple_of(pair * 128, 128)
        q = qkv_ref[:, pl.ds(at, 128)]
        k = qkv_ref[:, pl.ds(width + at, 128)]
        v = qkv_ref[:, pl.ds(2 * width + at, 128)]
        outs = []
        for head in range(2):
            mine = (lane < 64) if head == 0 else (lane >= 64)
            s = dot_nt(jnp.where(mine, q, jnp.zeros_like(q)), k) * (HD**-0.5 * LOG2E)
            s = jnp.where(dead, NEG, s)
            top = jnp.max(s, axis=1, keepdims=True)
            e = jnp.exp2(s - top)
            total = jnp.sum(e, axis=1, keepdims=True)
            p = (e * (1.0 / total)).astype(BF)
            outs.append(dot_nn(p, v))
            lse_ref[...] = jnp.where(lane == 2 * pair + head, top + jnp.log2(total), lse_ref[...])
        ctx_ref[:, pl.ds(at, 128)] = jnp.where(lane < 64, outs[0], outs[1]).astype(BF)
        return carry

    lax.fori_loop(0, width // 128, heads, 0)
    part_ref[...] = dot_nt(ctx_ref[...], vo_ref[:, width:]).astype(BF)


def attn_forward_kernel(token_ref, mem_ref, qk_ref, vo_ref, bias_ref, part_ref, low_ref, qkv_ref, lse_ref, ctx_ref):
    seg = token_ref.shape[0]
    memory = mem_ref[...].astype(BF)
    low_ref[:seg, :] = token_ref[...]
    low_ref[seg : seg + PAD, :] = memory
    low_ref[seg + PAD :, :] = memory
    attn_rows(low_ref, qk_ref, vo_ref, bias_ref, part_ref, qkv_ref, lse_ref, ctx_ref)


def close_rows(first_ref, own_ref, other_ref, shared_ref):
    unit, unused = norm_stats(first_ref[...])
    hidden = unit * shared_ref[USED + 2 : USED + 3, :] + shared_ref[USED + 3 : USED + 4, :]
    return hidden + (own_ref[...].astype(F32) + other_ref[...].astype(F32)) + shared_ref[USED + 1 : USED + 2, :]


def attn_next_kernel(first_ref, own_ref, other_ref, shared_ref, alive_ref, keep_ref, token_ref, qk_ref, vo_ref, bias_ref,
                     out_ref, mem_ref, second_ref, part_ref, low_ref, qkv_ref, lse_ref, ctx_ref):
    seg = token_ref.shape[0]
    second = close_rows(first_ref, own_ref, other_ref, shared_ref)
    second_ref[...] = second
    unit, unused = norm_stats(second)
    result = unit * shared_ref[USED + 4 : USED + 5, :] + shared_ref[USED + 5 : USED + 6, :]
    out_ref[...] = (result[:seg] * alive_ref[...]).astype(BF)
    row = lax.broadcasted_iota(jnp.int32, mem_ref.shape, 0)
    fresh = jnp.where(row < USED, result[seg + PAD :], 0.0)
    memory = jnp.where(alive_ref[...] > 0.0, fresh, keep_ref[...])
    mem_ref[...] = memory
    low_ref[:seg, :] = token_ref[...]
    low_ref[seg : seg + PAD, :] = memory.astype(BF)
    low_ref[seg + PAD :, :] = memory.astype(BF)
    attn_rows(low_ref, qk_ref, vo_ref, bias_ref, part_ref, qkv_ref, lse_ref, ctx_ref)


def ffn_forward_kernel(token_ref, mem_ref, own_ref, other_ref, up_ref, down_ref, bias_ref, shared_ref,
                       part_ref, first_ref, low_ref, act_ref, slope_ref, total_ref):
    seg = token_ref.shape[0]
    hidden_units = up_ref.shape[1]
    begin = bias_ref.shape[1] - hidden_units
    attn = own_ref[...].astype(F32) + other_ref[...].astype(F32) + shared_ref[USED : USED + 1, :]
    first_ref[:seg, :] = token_ref[...].astype(F32) + attn[:seg]
    first_ref[seg : seg + PAD, :] = mem_ref[...] + attn[seg : seg + PAD]
    first_ref[seg + PAD :, :] = mem_ref[...] + attn[seg + PAD :]
    unit, unused = norm_stats(first_ref[...])
    hidden = unit * shared_ref[USED + 2 : USED + 3, :] + shared_ref[USED + 3 : USED + 4, :]
    low_ref[...] = hidden.astype(BF)
    total_ref[...] = jnp.zeros_like(total_ref)

    def units(step, carry):
        for piece in range(2):
            at = pl.multiple_of(step * (2 * WIDE) + piece * WIDE, 128)
            u = dot_nn(low_ref[...], up_ref[:, pl.ds(at, WIDE)]) + bias_ref[:, pl.ds(begin + at, WIDE)]
            cdf = 0.5 + 0.5 * lax.erf(u * (0.5**0.5))
            density = jnp.exp2(u * u * (-0.5 * LOG2E)) * ((2.0 * math.pi) ** -0.5)
            active = (u * cdf).astype(BF)
            act_ref[:, pl.ds(at, WIDE)] = active
            slope_ref[:, pl.ds(at, WIDE)] = (cdf + u * density).astype(BF)
            total_ref[...] += dot_nt(active, down_ref[:, pl.ds(at, WIDE)])
        return carry

    lax.fori_loop(0, hidden_units // (2 * WIDE), units, 0)
    part_ref[...] = total_ref[...].astype(BF)


def ffn_backward_rows(second, dmem, cot_ref, alive_ref, shared_ref, up_ref, down_ref, slope_ref,
                      part_ref, dsecond_ref, dlow_ref, du_ref, dbias_ref, dvec_ref, total_ref):
    unit, scale = norm_stats(second)
    dy = jnp.concatenate(
        [cot_ref[...].astype(F32) * alive_ref[...], jnp.zeros((PAD, unit.shape[1]), F32), dmem * alive_ref[...]], axis=0
    )
    dsecond = norm_back(dy, shared_ref[USED + 4 : USED + 5, :], unit, scale)
    dsecond_ref[...] = dsecond
    dvec_ref[0:1, :] = row_sum(dsecond)
    dvec_ref[1:2, :] = row_sum(dy * unit)
    dvec_ref[2:3, :] = row_sum(dy)
    dvec_ref[3:, :] = jnp.zeros((dvec_ref.shape[0] - 3, unit.shape[1]), F32)
    dlow_ref[...] = dsecond.astype(BF)
    total_ref[...] = jnp.zeros_like(total_ref)

    def units(step, carry):
        for piece in range(2):
            at = pl.multiple_of(step * (2 * WIDE) + piece * WIDE, 128)
            du = dot_nn(dlow_ref[...], down_ref[:, pl.ds(at, WIDE)]) * slope_ref[:, pl.ds(at, WIDE)].astype(F32)
            dbias_ref[:, pl.ds(at, WIDE)] = row_sum(du)
            du_low = du.astype(BF)
            du_ref[:, pl.ds(at, WIDE)] = du_low
            total_ref[...] += dot_nt(du_low, up_ref[:, pl.ds(at, WIDE)])
        return carry

    lax.fori_loop(0, up_ref.shape[1] // (2 * WIDE), units, 0)
    part_ref[...] = total_ref[...].astype(BF)


def ffn_last_kernel(first_ref, own_ref, other_ref, cot_ref, dmem_ref, alive_ref, shared_ref, up_ref, down_ref, slope_ref,
                    out_ref, *outs):
    second = close_rows(first_ref, own_ref, other_ref, shared_ref)
    unit, unused = norm_stats(second)
    result = unit * shared_ref[USED + 4 : USED + 5, :] + shared_ref[USED + 5 : USED + 6, :]
    out_ref[...] = (result[: out_ref.shape[0]] * alive_ref[...]).astype(BF)
    ffn_backward_rows(second, dmem_ref[...], cot_ref, alive_ref, shared_ref, up_ref, down_ref, slope_ref, *outs)


def input_rows(dfirst_ref, own_ref, other_ref, grad_ref, live, keep):
    seg = grad_ref.shape[0]
    dx = dfirst_ref[...] + (own_ref[...].astype(F32) + other_ref[...].astype(F32))
    grad_ref[...] = (dx[:seg] * live).astype(BF)
    return jnp.where(live > 0.0, dx[seg : seg + PAD] + dx[seg + PAD :], keep)


def ffn_before_kernel(dfirst_ref, own_ref, other_ref, live_ref, keep_ref, second_ref, cot_ref, alive_ref, shared_ref, up_ref, down_ref,
                      slope_ref, grad_ref, dmem_ref, *outs):
    dmem = input_rows(dfirst_ref, own_ref, other_ref, grad_ref, live_ref[...], keep_ref[...])
    dmem_ref[...] = dmem
    ffn_backward_rows(second_ref[...], dmem, cot_ref, alive_ref, shared_ref, up_ref, down_ref, slope_ref, *outs)


def input_grad_kernel(dfirst_ref, own_ref, other_ref, live_ref, keep_ref, grad_ref, dmem_ref):
    dmem_ref[...] = input_rows(dfirst_ref, own_ref, other_ref, grad_ref, live_ref[...], keep_ref[...])


def attn_backward_kernel(dsecond_ref, own_ref, other_ref, first_ref, shared_ref, qk_ref, vo_ref, qkv_ref, lse_ref,
                         part_ref, dfirst_ref, da_ref, dqkv_ref, dhead_ref, dvec_ref, dctx_ref, lse_t_ref):
    rows = first_ref.shape[0]
    width = vo_ref.shape[1] // 2
    seg = rows - 2 * PAD
    dhidden = dsecond_ref[...] + (own_ref[...].astype(F32) + other_ref[...].astype(F32))
    unit, scale = norm_stats(first_ref[...])
    dfirst = norm_back(dhidden, shared_ref[USED + 2 : USED + 3, :], unit, scale)
    dfirst_ref[...] = dfirst
    dvec_ref[0:1, :] = row_sum(dfirst)
    dvec_ref[1:2, :] = row_sum(dhidden * unit)
    dvec_ref[2:3, :] = row_sum(dhidden)
    dvec_ref[3:, :] = jnp.zeros((dvec_ref.shape[0] - 3, unit.shape[1]), F32)
    da_ref[...] = dfirst.astype(BF)
    dctx_ref[...] = dot_nn(da_ref[...], vo_ref[:, width:]).astype(BF)
    lse_t_ref[...] = jnp.transpose(lse_ref[...])
    key_at = lax.broadcasted_iota(jnp.int32, (rows, 1), 0)
    dead = (key_at >= seg) & (((key_at - seg) & (PAD - 1)) >= USED)
    lane = lax.broadcasted_iota(jnp.int32, (rows, 128), 1)
    sub = lax.broadcasted_iota(jnp.int32, (128, rows), 0)

    def heads(pair, carry):
        at = pl.multiple_of(pair * 128, 128)
        q = qkv_ref[:, pl.ds(at, 128)]
        k = qkv_ref[:, pl.ds(width + at, 128)]
        v = qkv_ref[:, pl.ds(2 * width + at, 128)]
        dc = dctx_ref[:, pl.ds(at, 128)]
        dq_t, dk, dv = [], None, None
        for head in range(2):
            mine = (lane < 64) if head == 0 else (lane >= 64)
            q_one = jnp.where(mine, q, jnp.zeros_like(q))
            dc_one = jnp.where(mine, dc, jnp.zeros_like(dc))
            s_t = dot_nt(k, q_one) * (HD**-0.5 * LOG2E)
            lse_row = lse_t_ref[pl.ds(2 * pair + head, 1), :]
            p_t = jnp.where(dead, 0.0, jnp.exp2(s_t - lse_row))
            dp_t = dot_nt(v, dc_one)
            dv_one = dot_nn(p_t.astype(BF), dc_one)
            inner = row_sum(p_t * dp_t)
            ds_t = (p_t * (dp_t - inner)).astype(BF)
            dk_one = dot_nn(ds_t, q_one)
            dq_t.append(dot_tn(k, ds_t))
            dv = dv_one if dv is None else dv + dv_one
            dk = dk_one if dk is None else dk + dk_one
        dq = jnp.transpose(jnp.where(sub < 64, dq_t[0], dq_t[1])) * (HD**-0.5)
        dk = dk * (HD**-0.5)
        dhead_ref[:, pl.ds(at, 128)] = row_sum(dq)
        dhead_ref[:, pl.ds(width + at, 128)] = row_sum(dv)
        dqkv_ref[:, pl.ds(at, 128)] = dq.astype(BF)
        dqkv_ref[:, pl.ds(width + at, 128)] = dk.astype(BF)
        dqkv_ref[:, pl.ds(2 * width + at, 128)] = dv.astype(BF)
        return carry

    lax.fori_loop(0, width // 128, heads, 0)
    part = dot_nt(dqkv_ref[:, : 2 * width], qk_ref[...]) + dot_nt(dqkv_ref[:, 2 * width :], vo_ref[:, :width])
    part_ref[...] = part.astype(BF)


def grad_close_kernel(lines, *refs):
    count = 3 * lines
    outs = refs[-4:]
    squares = None
    for matrix in range(3):
        total = refs[matrix * lines][...].astype(F32)
        for other in refs[matrix * lines + 1 : (matrix + 1) * lines]:
            total = total + other[...].astype(F32)
        outs[matrix][...] = total
        square = jnp.sum(total * total, keepdims=True)
        squares = square if squares is None else squares + square
    dmem_ref = refs[count]
    dvec_one, dvec_two, dhead, dbias = (refs[count + 1 + i : -4 : 4] for i in range(4))
    small = outs[3]
    model = small.shape[1]

    def total_of(group, row):
        total = group[0][row : row + 1, :]
        for ref in group[1:]:
            total = total + ref[row : row + 1, :]
        return total

    small[:PAD, :] = dmem_ref[...]
    for place, (group, row) in enumerate(((dvec_one, 0), (dvec_two, 0), (dvec_one, 1), (dvec_one, 2), (dvec_two, 1), (dvec_two, 2))):
        small[USED + place : USED + place + 1, :] = total_of(group, row)
    at = USED + 6
    for group in (dhead, dbias):
        whole = total_of(group, 0)
        for piece in range(whole.shape[1] // model):
            small[at : at + 1, :] = whole[:, piece * model : (piece + 1) * model]
            at += 1
    small[at:, :] = jnp.broadcast_to(squares, (small.shape[0] - at, model))


def adam_kernel(plan, small_ref, own_ref, other_ref, *refs):
    count = len(plan)
    grads = refs[:3]
    olds, news = refs[3 : 3 + 3 * count], refs[4 + 3 * count :]
    norm_ref = refs[3 + 3 * count]
    shared = small_ref[: USED + 6, :]
    norm = jnp.sqrt((own_ref[:1, :1] + other_ref[:1, :1]) + jnp.sum(shared * shared, keepdims=True))
    norm_ref[...] = norm
    factor = CLIP_NORM / jnp.maximum(norm, CLIP_NORM)
    for number, (source, row, column, rate, decay) in enumerate(plan):
        weight_ref, first_ref, second_ref = olds[3 * number : 3 * number + 3]
        height, length = weight_ref.shape[-2:]
        for index in range(math.prod(weight_ref.shape[:-2])):
            here = (index,) if weight_ref.ndim == 3 else ()
            if source is None and height == 1:
                model = small_ref.shape[1]
                gradient = jnp.concatenate([small_ref[row + i : row + i + 1, :] for i in range(length // model)], axis=1)
            elif source is None:
                gradient = small_ref[row : row + height, :]
            else:
                gradient = grads[source][:, column + index * length : column + (index + 1) * length]
            clipped = gradient * factor
            first = BETA_ONE * first_ref[here + (...,)] + (1.0 - BETA_ONE) * clipped
            second = BETA_TWO * second_ref[here + (...,)] + (1.0 - BETA_TWO) * clipped * clipped
            first_hat = first / (1.0 - BETA_ONE**STEP)
            second_hat = second / (1.0 - BETA_TWO**STEP)
            weight = weight_ref[here + (...,)]
            news[3 * number][here + (...,)] = weight - rate * (first_hat / (jnp.sqrt(second_hat) + ADAM_EPSILON) + decay * weight)
            news[3 * number + 1][here + (...,)] = first
            news[3 * number + 2][here + (...,)] = second


def weight_grad_kernel(plan, kinds, sizes, me_ref, *refs):
    count = len(kinds) * len(sizes)
    outs = refs[-count - 1 : -1]
    total_ref = refs[-1]
    block = total_ref.shape[0] // SLOTS
    for part, (kind, pieces) in enumerate(zip(kinds, plan)):
        at = 0
        for left, right, start, size in pieces:

            def rows_of(step, carry, left=left, right=right, start=start, size=size, at=at):
                begin = pl.multiple_of(step * CHUNK, CHUNK)
                total = None
                for one, two in zip(left, right):
                    add = dot_tn(refs[one][:, pl.ds(begin, CHUNK)], refs[two][:, start : start + size])
                    total = add if total is None else total + add
                total_ref[pl.ds(begin, CHUNK), at : at + size] = total
                return carry

            lax.fori_loop(0, total_ref.shape[0] // CHUNK, rows_of, 0)
            at += size
        number = 0
        for target in outs[part * len(sizes) : (part + 1) * len(sizes)]:
            for inner in range(target.shape[0]):
                place = lax.bitwise_xor(me_ref[0], slot_of(kind, number))
                begin = pl.multiple_of(place * block, block)
                target[inner] = total_ref[pl.ds(begin, block), :].astype(BF)
                number += 1


def exchange(values, axis, size, flip):
    return lax.ppermute(values, axis, [(i, i ^ flip) for i in range(size)])


def after(value, *others):
    return lax.optimization_barrier((value, *others))[0]


def add_low(*values):
    total = values[0].astype(F32)
    for value in values[1:]:
        total = total + value.astype(F32)
    return total


def canonical_split(full, kind, sizes):
    full = full.reshape(SLOTS, full.shape[0] // SLOTS, full.shape[1])
    full = jnp.stack([full[slot_of(kind, number)] for number in range(SLOTS)])
    ends = [sum(sizes[: i + 1]) for i in range(len(sizes))]
    return [full[end - size : end] for end, size in zip(ends, sizes)]


def canonical_join(pieces, kind):
    full = jnp.concatenate(pieces)
    order = [slot_of(kind, number) for number in range(SLOTS)]
    full = jnp.stack([full[order.index(d)] for d in range(SLOTS)])
    return full.reshape(-1, full.shape[-1])


def line_stage(own, size):
    return [own] + [exchange(own, "dp", size, 4 * j) for j in (1, 2, 3)]


def sum_all(values, axis, size):
    if size & (size - 1):
        return lax.psum(values, axis)
    flip = 1
    while flip < size:
        if flip * 4 <= size:
            near, far, both = [exchange(values, axis, size, flip * j) for j in (1, 2, 3)]
            values = (values + near) + (far + both)
            flip *= 4
        else:
            values = values + exchange(values, axis, size, flip)
            flip *= 2
    return values


def shards(
    size,
    pair,
    inputs,
    cotangent,
    seg_counts,
    qkv_weight,
    out_weight,
    up_weight,
    down_weight,
    head_bias,
    shared_params,
    qkv_first,
    out_first,
    up_first,
    down_first,
    bias_first,
    shared_first,
    qkv_second,
    out_second,
    up_second,
    down_second,
    bias_second,
    shared_second,
):
    unused, segments, seg, model = inputs.shape
    width = qkv_weight.shape[2]
    hidden = up_weight.shape[1]
    used = shared_params.shape[0] - 6
    pad = 16
    rows = seg + 2 * pad
    half = hidden // 2

    me = (lax.axis_index("dp") if size == SLOTS else jnp.int32(0)).astype(jnp.int32).reshape(1)
    qkv_low = qkv_weight.astype(BF)
    out_low = out_weight.T.astype(BF)
    up_low = up_weight.astype(BF)
    down_low = down_weight.T.astype(BF)
    own = [
        jnp.stack([jnp.concatenate([qkv_low[0], qkv_low[1]], axis=1), jnp.concatenate([qkv_low[2], out_low], axis=1)]),
        jnp.stack([up_low[:, :half], up_low[:, half:]]),
        jnp.stack([down_low[:, :half], down_low[:, half:]]),
    ]

    def assembled(kinds, pieces, joined):
        return call(
            functools.partial(assemble_kernel, kinds, [len(p) for p in pieces], joined),
            [((model, 2 * model), BF)] if joined else [((model, model), BF)] * 2,
            [me, *pieces[0], *pieces[1]],
            scalars=1,
        )

    z_first, z_mid = ("za", "zb"), ("xa", "xb")
    if size == SLOTS:

        def spread(lines):
            low_a = jnp.concatenate([lines[0], exchange(lines[0], "dp", size, 2)])
            low_b = jnp.concatenate([lines[1], exchange(lines[1], "dp", size, 1)])
            return low_a, low_b

        def finish(low_a, low_b):
            return exchange(low_a, "dp", size, 1), exchange(low_b, "dp", size, 2)

        pair_c = [jnp.stack([own[2][i], exchange(own[2][i], "dp", size, 1 + i)]) for i in range(2)]
        line_one = line_stage(own[0], size)
        line_two = line_stage(after(own[1], *line_one), size)
        low_one = spread([jnp.stack([v[i] for v in line_one]) for i in range(2)])
        line_three = line_stage(after(jnp.stack(pair_c), *line_two, *low_one), size)
        high_one = finish(*low_one)
        low_two = spread([after(jnp.stack([v[i] for v in line_two]), *high_one) for i in range(2)])
        high_two = finish(*low_two)
        low_c = [jnp.concatenate([v[i] for v in line_three]) for i in range(2)]
        low_c = [after(v, *high_two) for v in low_c]
        high_c = [exchange(low_c[i], "dp", size, 2 - i) for i in range(2)]
        high_one = [after(h, *low_two) for h in high_one]
        w_qk, w_vo = assembled(z_first, [[low_one[i], high_one[i]] for i in range(2)], False)
        (w_up,) = assembled(z_first, [[low_two[i], high_two[i]] for i in range(2)], True)
        (w_down,) = assembled(z_mid, [[low_c[i], high_c[i]] for i in range(2)], True)
    else:

        def whole(number, kinds, sizes):
            pieces = [lax.all_gather(own[number][i], "dp", axis=0, tiled=True) for i in range(2)]
            return assembled(kinds, [canonical_split(p, kind, sizes) for p, kind in zip(pieces, kinds)], number > 0)

        w_qk, w_vo = whole(0, z_first, (8, 8))
        (w_up,) = whole(1, z_first, (8, 8))
        (w_down,) = whole(2, z_mid, (8, 8))

    memory = jnp.concatenate([shared_params[:used], jnp.zeros((pad - used, model), F32)], axis=0)
    alive = [(slot < seg_counts).astype(F32).reshape(1, 1) for slot in range(segments)]
    memories, tokens_out, saved = [memory], [], []
    attn_outs = [((rows, model), BF), ((rows, model), BF), ((rows, 3 * width), BF), ((rows, 128), F32), ((rows, width), BF)]
    for slot in range(segments):
        tokens = inputs[0, slot]
        if slot == 0:
            part, *attn = call(attn_forward_kernel, attn_outs, [tokens, memory, w_qk, w_vo, head_bias])
        else:
            out_rows, memory, second_in, part, *attn = call(
                attn_next_kernel,
                [((seg, model), BF), ((pad, model), F32), ((rows, model), F32)] + attn_outs,
                [saved[-1][4], ffn_part, other, shared_params, alive[slot - 1], memory, tokens, w_qk, w_vo, head_bias],
            )
            tokens_out.append(out_rows)
            saved[-1] += (second_in,)
        other = exchange(part, "head", pair, 1)
        ffn_part, first_in, h_low, active, slope = call(
            ffn_forward_kernel,
            [((rows, model), BF), ((rows, model), F32), ((rows, model), BF), ((rows, hidden), BF), ((rows, hidden), BF)],
            [tokens, memory, part, other, w_up, w_down, head_bias, shared_params],
            scratch=[pltpu.VMEM((rows, model), F32)],
        )
        other = exchange(ffn_part, "head", pair, 1)
        saved.append((*attn, first_in, h_low, active, slope))

    count = segments

    def weight_grad(names, plan, kinds):
        sizes = (8, 8)
        operands = [stacks[s][n] for n in names for s in range(count)]
        at = {n: [i * count + s for s in range(count)] for i, n in enumerate(names)}
        steps = [[(at[a], at[b], start, length) for a, b, start, length in pieces] for pieces in plan]
        result = call(
            functools.partial(weight_grad_kernel, steps, kinds, sizes),
            [((length, model // SLOTS, model), BF) for kind in kinds for length in sizes],
            [me, *operands],
            scalars=1,
            scratch=[pltpu.VMEM((model, model), F32)],
        )
        return result[: len(sizes)], result[len(sizes) :]

    dmem = jnp.zeros((pad, model), F32)
    grads = [None] * segments
    stacks = [None] * segments
    smalls = []
    ffn_outs = [((rows, model), BF), ((rows, model), F32), ((rows, model), BF), ((rows, hidden), BF), ((1, hidden), F32), ((8, model), F32)]
    for slot in reversed(range(segments)):
        low, qkv, lse, ctx, first_in, h_low, active, slope = saved[slot][:8]
        weights = [alive[slot], shared_params, w_up, w_down, slope]
        scratch = [pltpu.VMEM((rows, model), F32)]
        if slot == segments - 1:
            out_rows, part, dsecond, df_low, du, dbias, dvec_two = call(
                ffn_last_kernel,
                [((seg, model), BF)] + ffn_outs,
                [first_in, ffn_part, other, cotangent[0, slot], dmem, *weights],
                scratch=scratch,
            )
            tokens_out.append(out_rows)
        else:
            grads[slot + 1], dmem, part, dsecond, df_low, du, dbias, dvec_two = call(
                ffn_before_kernel,
                [((seg, model), BF), ((pad, model), F32)] + ffn_outs,
                [dfirst, part, other, alive[slot + 1], dmem, saved[slot][8], cotangent[0, slot], *weights],
                scratch=scratch,
            )
        other = exchange(part, "head", pair, 1)
        stacks[slot] = (low, ctx, h_low, active, df_low, du)
        if slot == 0:
            dw_down = weight_grad((DF_LOW, ACTIVE), [[(DF_LOW, ACTIVE, 0, half)], [(DF_LOW, ACTIVE, half, half)]], z_first)
            dw_up = weight_grad((H_LOW, DU), [[(H_LOW, DU, 0, half)], [(H_LOW, DU, half, half)]], z_first)
            dsecond = after(dsecond, dw_down[0][0], dw_up[0][0])
        part, dfirst, da, dqkv, dhead, dvec_one = call(
            attn_backward_kernel,
            [((rows, model), BF), ((rows, model), F32), ((rows, model), BF), ((rows, 3 * width), BF), ((1, 2 * width), F32), ((8, model), F32)],
            [dsecond, part, other, first_in, shared_params, w_qk, w_vo, qkv, lse],
            scratch=[pltpu.VMEM((rows, width), BF), pltpu.VMEM((128, rows), F32)],
        )
        other = exchange(part, "head", pair, 1)
        stacks[slot] += (da, dqkv)
        smalls += [dvec_one, dvec_two, dhead, dbias]
    grads[0], dmem = call(
        input_grad_kernel,
        [((seg, model), BF), ((pad, model), F32)],
        [dfirst, part, other, alive[0], dmem],
    )
    outputs = jnp.stack(tokens_out)[None]
    input_grad = jnp.stack(grads)[None]

    def fallback(parts, kinds):
        full = [canonical_join(p, kind) for p, kind in zip(parts, kinds)]
        full = jnp.concatenate(full, axis=1)
        return lax.psum_scatter(full, "dp", scatter_dimension=0, tiled=True).astype(F32)

    def hop(blocks, flips):
        return [exchange(block, "dp", size, flip) for block, flip in zip(blocks, flips)]

    def add_halves(keep, got):
        return [add_low(k, g).astype(BF) for k, g in zip(keep, got)]

    def line_hop(four):
        return [exchange(four[j], "dp", size, 4 * j) for j in (1, 2, 3)]

    x_first, y_first = (1, 2), (2, 1)
    if size == SLOTS:
        got_down, got_up = hop([p[1] for p in dw_down], x_first), hop([p[1] for p in dw_up], x_first)
        stacks[0] = stacks[0][:DQKV] + (after(stacks[0][DQKV], *got_down),)
    dw_qkvo = weight_grad(
        (LOW, DQKV, DA, CTX),
        [[(LOW, DQKV, 0, 2 * width)], [(LOW, DQKV, 2 * width, width), (DA, CTX, 0, width)]],
        z_first,
    )
    if size == SLOTS:
        dw_qkvo = [[after(v, *got_up) for v in part] for part in dw_qkvo]
        got_qkvo = hop([p[1] for p in dw_qkvo], x_first)
        keep = [jnp.stack([dw_down[i][0], dw_up[i][0]], axis=1) for i in range(2)]
        got = [jnp.stack([after(got_down[i], dw_qkvo[0][0]), got_up[i]], axis=1) for i in range(2)]
        both = add_halves(keep, got)
        got = hop([v[4:] for v in both], y_first)
        both = add_halves([v[:4] for v in both], [after(g, *got_qkvo) for g in got])
        last = add_halves([p[0] for p in dw_qkvo], got_qkvo)
        last = add_halves([v[:4] for v in last], hop([v[4:] for v in last], y_first))
        both = jnp.concatenate(both, axis=3)
        got = line_hop(both)
        last = jnp.concatenate(last, axis=2)
        sums = [[both[0, i], *[g[i] for g in got]] for i in range(2)]
        sums.append([last[0], *line_hop(last)])
    else:
        sums = [[fallback(p, z_first)] for p in (dw_down, dw_up, dw_qkvo)]
    height, wide = sums[0][0].shape
    *matrices, small = call(
        functools.partial(grad_close_kernel, len(sums[0])),
        [((height, wide), F32)] * 3 + [((24, model), F32)],
        [*sums[0], *sums[1], *sums[2], dmem, *smalls],
    )
    small = sum_all(small, "dp", size)
    bias_grad = small[used + 6 : used + 9]
    squares = jnp.full((8, 128), small[used + 9, 0] + jnp.sum(bias_grad * bias_grad))
    other = exchange(squares, "head", pair, 1)
    plan = (
        (2, 0, 0, LEARN_RATE, DECAY_RATE),
        (2, 0, 3 * width, LEARN_RATE, DECAY_RATE),
        (1, 0, 0, LEARN_RATE, DECAY_RATE),
        (0, 0, 0, LEARN_RATE, DECAY_RATE),
        (None, used + 6, 0, VECTOR_RATE, 0.0),
        (None, 0, 0, VECTOR_RATE, 0.0),
    )
    olds = (
        (qkv_weight, qkv_first, qkv_second),
        (out_weight.T, out_first.T, out_second.T),
        (up_weight, up_first, up_second),
        (down_weight.T, down_first.T, down_second.T),
        (head_bias, bias_first, bias_second),
        (shared_params, shared_first, shared_second),
    )
    grad_norm, *news = call(
        functools.partial(adam_kernel, plan),
        [((1, 1), F32)] + [(o.shape, F32) for old in olds for o in old],
        [small, squares, other, *matrices, *[o for old in olds for o in old]],
    )
    results = [news[3 * i : 3 * i + 3] for i in range(6)]
    for number in (1, 3):
        results[number] = [r.T for r in results[number]]
    return (outputs, input_grad, grad_norm[0, 0]) + tuple(r[i] for i in range(3) for r in results)


def solution(mesh):
    weights = (P(None, "dp", "head"), P("head", "dp"), P("dp", "head"), P("head", "dp"), P("head", None), P())
    rows = P("dp", None, None, None)
    return jax.shard_map(
        functools.partial(shards, mesh.shape["dp"], mesh.shape["head"]),
        mesh=mesh,
        in_specs=(rows, rows, P("dp")) + weights * 3,
        out_specs=(rows, rows, P()) + weights * 3,
        check_vma=False,
    )
```

```python
import functools
import math

import jax
import jax.numpy as jnp
from jax import lax
from jax.experimental import pallas as pl
from jax.experimental.pallas import tpu as pltpu
from jax.sharding import PartitionSpec as P

HD = 64
STEP = 10
EPSILON = 1e-06
BETA_ONE = 0.9
BETA_TWO = 0.999
LEARN_RATE = 0.1
VECTOR_RATE = 0.6
DECAY_RATE = 0.01
ADAM_EPSILON = 1e-08
CLIP_NORM = 1.0

BF = jnp.bfloat16
F32 = jnp.float32
LOG2E = math.log2(math.e)
NEG = -1e30
SLOTS = 16
PAD = 16
USED = 10
WIDE = 256
CHUNK = 256
LOW, CTX, H_LOW, ACTIVE, DF_LOW, DU, DA, DQKV = range(8)


def dot_nn(a, b):
    return lax.dot_general(a, b, (((1,), (0,)), ((), ())), preferred_element_type=F32)


def dot_nt(a, b):
    return lax.dot_general(a, b, (((1,), (1,)), ((), ())), preferred_element_type=F32)


def dot_tn(a, b):
    return lax.dot_general(a, b, (((0,), (0,)), ((), ())), preferred_element_type=F32)


def norm_stats(values):
    average = jnp.mean(values, axis=-1, keepdims=True)
    centered = values - average
    variance = jnp.mean(centered * centered, axis=-1, keepdims=True)
    scale = lax.rsqrt(variance + EPSILON)
    return centered * scale, scale


def norm_back(grad, gain, unit, scale):
    inner = grad * gain
    mean_one = jnp.mean(inner, axis=-1, keepdims=True)
    mean_two = jnp.mean(inner * unit, axis=-1, keepdims=True)
    return scale * (inner - mean_one - unit * mean_two)


def row_sum(values):
    return jnp.sum(values, axis=0, keepdims=True)


def call(kernel, outs, args, scalars=0, scratch=()):
    return pl.pallas_call(
        kernel,
        out_shape=[jax.ShapeDtypeStruct(s, d) for s, d in outs],
        in_specs=[pl.BlockSpec(memory_space=pltpu.SMEM)] * scalars
        + [pl.BlockSpec(memory_space=pltpu.VMEM)] * (len(args) - scalars),
        out_specs=[pl.BlockSpec(memory_space=pltpu.VMEM)] * len(outs),
        scratch_shapes=list(scratch),
        cost_estimate=pl.CostEstimate(flops=0, bytes_accessed=0, transcendentals=0),
        compiler_params=pltpu.CompilerParams(vmem_limit_bytes=16 << 20),
    )(*args)


def slot_of(kind, number):
    if kind[0] == "z":
        outer, mid, z = number // 8, number // 4 % 2, number % 4
        return (outer + 2 * mid if kind[1] == "a" else 2 * outer + mid) + 4 * z
    outer, z, inner = number // 8, number // 2 % 4, number % 2
    return (2 * outer + inner if kind[1] == "a" else outer + 2 * inner) + 4 * z


def assemble_kernel(kinds, counts, joined, me_ref, *refs):
    at = sum(counts)
    begin = 0
    for part, (kind, count) in enumerate(zip(kinds, counts)):
        target = refs[at] if joined else refs[at + part]
        block = target.shape[0] // SLOTS
        number = 0
        for source in refs[begin : begin + count]:
            length = source.shape[2]
            column = part * length if joined else 0
            for inner in range(source.shape[0]):
                place = lax.bitwise_xor(me_ref[0], slot_of(kind, number))
                start = pl.multiple_of(place * block, block)
                target[pl.ds(start, block), column : column + length] = source[inner]
                number += 1
        begin += count


def dead_rows(rows):
    at = lax.broadcasted_iota(jnp.int32, (rows, 128), 0) - (rows - 2 * PAD)
    return (at >= 0) & ((at & (PAD - 1)) >= USED)


def masked_scores(q, k, mine, dead, lane, head, dot):
    spare = lane == (127 if head == 0 else 0)
    zero = jnp.zeros_like(q)
    q_one = jnp.where(spare, jnp.ones_like(q), jnp.where(mine, q, zero))
    k_one = jnp.where(spare, jnp.where(dead, jnp.full_like(k, NEG), zero), k)
    return dot(q_one, k_one)


def attn_rows(low_ref, qk_ref, vo_ref, bias_ref, part_ref, qkv_ref, lse_ref, ctx_ref):
    rows = low_ref.shape[0]
    width = vo_ref.shape[1] // 2
    seg = rows - 2 * PAD
    low = low_ref[...]
    qk = dot_nn(low, qk_ref[...])
    qkv_ref[:, :width] = (qk[:, :width] + bias_ref[:, :width]).astype(BF)
    qkv_ref[:, width : 2 * width] = qk[:, width:].astype(BF)
    v_all = dot_nn(low, vo_ref[:, :width])
    qkv_ref[:, 2 * width :] = (v_all + bias_ref[:, width : 2 * width]).astype(BF)
    lane = lax.broadcasted_iota(jnp.int32, (rows, 128), 1)
    lse_ref[...] = jnp.zeros_like(lse_ref)
    dead = dead_rows(rows)

    def heads(pair, carry):
        at = pl.multiple_of(pair * 128, 128)
        q = qkv_ref[:, pl.ds(at, 128)]
        k = qkv_ref[:, pl.ds(width + at, 128)]
        v = qkv_ref[:, pl.ds(2 * width + at, 128)]
        outs = []
        for head in range(2):
            mine = (lane < 64) if head == 0 else (lane >= 64)
            s = masked_scores(q, k, mine, dead, lane, head, dot_nt) * (HD**-0.5 * LOG2E)
            top = jnp.max(s, axis=1, keepdims=True)
            e = jnp.exp2(s - top)
            total = jnp.sum(e, axis=1, keepdims=True)
            outs.append(dot_nn(e.astype(BF), v) * (1.0 / total))
            lse_ref[...] = jnp.where(lane == 2 * pair + head, top + jnp.log2(total), lse_ref[...])
        ctx_ref[:, pl.ds(at, 128)] = jnp.where(lane < 64, outs[0], outs[1]).astype(BF)
        return carry

    lax.fori_loop(0, width // 128, heads, 0)
    part_ref[...] = dot_nt(ctx_ref[...], vo_ref[:, width:]).astype(BF)


def attn_forward_kernel(token_ref, mem_ref, qk_ref, vo_ref, bias_ref, part_ref, low_ref, qkv_ref, lse_ref, ctx_ref):
    seg = token_ref.shape[0]
    memory = mem_ref[...].astype(BF)
    low_ref[:seg, :] = token_ref[...]
    low_ref[seg : seg + PAD, :] = memory
    low_ref[seg + PAD :, :] = memory
    attn_rows(low_ref, qk_ref, vo_ref, bias_ref, part_ref, qkv_ref, lse_ref, ctx_ref)


def close_rows(first_ref, own_ref, other_ref, shared_ref):
    unit, unused = norm_stats(first_ref[...])
    hidden = unit * shared_ref[USED + 2 : USED + 3, :] + shared_ref[USED + 3 : USED + 4, :]
    return hidden + (own_ref[...].astype(F32) + other_ref[...].astype(F32)) + shared_ref[USED + 1 : USED + 2, :]


def attn_next_kernel(first_ref, own_ref, other_ref, shared_ref, alive_ref, keep_ref, token_ref, qk_ref, vo_ref, bias_ref,
                     out_ref, mem_ref, second_ref, part_ref, low_ref, qkv_ref, lse_ref, ctx_ref):
    seg = token_ref.shape[0]
    second = close_rows(first_ref, own_ref, other_ref, shared_ref)
    second_ref[...] = second
    unit, unused = norm_stats(second)
    result = unit * shared_ref[USED + 4 : USED + 5, :] + shared_ref[USED + 5 : USED + 6, :]
    out_ref[...] = (result[:seg] * alive_ref[...]).astype(BF)
    row = lax.broadcasted_iota(jnp.int32, mem_ref.shape, 0)
    fresh = jnp.where(row < USED, result[seg + PAD :], 0.0)
    memory = jnp.where(alive_ref[...] > 0.0, fresh, keep_ref[...])
    mem_ref[...] = memory
    low_ref[:seg, :] = token_ref[...]
    low_ref[seg : seg + PAD, :] = memory.astype(BF)
    low_ref[seg + PAD :, :] = memory.astype(BF)
    attn_rows(low_ref, qk_ref, vo_ref, bias_ref, part_ref, qkv_ref, lse_ref, ctx_ref)


def ffn_forward_kernel(token_ref, mem_ref, own_ref, other_ref, up_ref, down_ref, bias_ref, shared_ref,
                       part_ref, first_ref, low_ref, act_ref, slope_ref):
    seg = token_ref.shape[0]
    hidden_units = up_ref.shape[1]
    begin = bias_ref.shape[1] - hidden_units
    attn = own_ref[...].astype(F32) + other_ref[...].astype(F32) + shared_ref[USED : USED + 1, :]
    first_ref[:seg, :] = token_ref[...].astype(F32) + attn[:seg]
    first_ref[seg : seg + PAD, :] = mem_ref[...] + attn[seg : seg + PAD]
    first_ref[seg + PAD :, :] = mem_ref[...] + attn[seg + PAD :]
    unit, unused = norm_stats(first_ref[...])
    hidden = unit * shared_ref[USED + 2 : USED + 3, :] + shared_ref[USED + 3 : USED + 4, :]
    low_ref[...] = hidden.astype(BF)

    def units(step, carry):
        for piece in range(2):
            at = pl.multiple_of(step * (2 * WIDE) + piece * WIDE, 128)
            u = dot_nn(low_ref[...], up_ref[:, pl.ds(at, WIDE)]) + bias_ref[:, pl.ds(begin + at, WIDE)]
            cdf = 0.5 + 0.5 * lax.erf(u * (0.5**0.5))
            density = jnp.exp2(u * u * (-0.5 * LOG2E)) * ((2.0 * math.pi) ** -0.5)
            active = (u * cdf).astype(BF)
            act_ref[:, pl.ds(at, WIDE)] = active
            slope_ref[:, pl.ds(at, WIDE)] = (cdf + u * density).astype(BF)
        return carry

    lax.fori_loop(0, hidden_units // (2 * WIDE), units, 0)
    part_ref[...] = dot_nt(act_ref[...], down_ref[...]).astype(BF)


def ffn_backward_rows(second, dmem, cot_ref, alive_ref, shared_ref, up_ref, down_ref, slope_ref,
                      part_ref, dsecond_ref, dlow_ref, du_ref, dbias_ref, dvec_ref):
    unit, scale = norm_stats(second)
    dy = jnp.concatenate(
        [cot_ref[...].astype(F32) * alive_ref[...], jnp.zeros((PAD, unit.shape[1]), F32), dmem * alive_ref[...]], axis=0
    )
    dsecond = norm_back(dy, shared_ref[USED + 4 : USED + 5, :], unit, scale)
    dsecond_ref[...] = dsecond
    dvec_ref[0:1, :] = row_sum(dsecond)
    dvec_ref[1:2, :] = row_sum(dy * unit)
    dvec_ref[2:3, :] = row_sum(dy)
    dvec_ref[3:, :] = jnp.zeros((dvec_ref.shape[0] - 3, unit.shape[1]), F32)
    dlow_ref[...] = dsecond.astype(BF)

    def units(step, carry):
        for piece in range(2):
            at = pl.multiple_of(step * (2 * WIDE) + piece * WIDE, 128)
            du = dot_nn(dlow_ref[...], down_ref[:, pl.ds(at, WIDE)]) * slope_ref[:, pl.ds(at, WIDE)].astype(F32)
            dbias_ref[:, pl.ds(at, WIDE)] = row_sum(du)
            du_low = du.astype(BF)
            du_ref[:, pl.ds(at, WIDE)] = du_low
        return carry

    lax.fori_loop(0, up_ref.shape[1] // (2 * WIDE), units, 0)
    part_ref[...] = dot_nt(du_ref[...], up_ref[...]).astype(BF)


def ffn_last_kernel(first_ref, own_ref, other_ref, cot_ref, dmem_ref, alive_ref, shared_ref, up_ref, down_ref, slope_ref,
                    out_ref, *outs):
    second = close_rows(first_ref, own_ref, other_ref, shared_ref)
    unit, unused = norm_stats(second)
    result = unit * shared_ref[USED + 4 : USED + 5, :] + shared_ref[USED + 5 : USED + 6, :]
    out_ref[...] = (result[: out_ref.shape[0]] * alive_ref[...]).astype(BF)
    ffn_backward_rows(second, dmem_ref[...], cot_ref, alive_ref, shared_ref, up_ref, down_ref, slope_ref, *outs)


def input_rows(dfirst_ref, own_ref, other_ref, grad_ref, live, keep):
    seg = grad_ref.shape[0]
    dx = dfirst_ref[...] + (own_ref[...].astype(F32) + other_ref[...].astype(F32))
    grad_ref[...] = (dx[:seg] * live).astype(BF)
    return jnp.where(live > 0.0, dx[seg : seg + PAD] + dx[seg + PAD :], keep)


def ffn_before_kernel(dfirst_ref, own_ref, other_ref, live_ref, keep_ref, second_ref, cot_ref, alive_ref, shared_ref, up_ref, down_ref,
                      slope_ref, grad_ref, dmem_ref, *outs):
    dmem = input_rows(dfirst_ref, own_ref, other_ref, grad_ref, live_ref[...], keep_ref[...])
    dmem_ref[...] = dmem
    ffn_backward_rows(second_ref[...], dmem, cot_ref, alive_ref, shared_ref, up_ref, down_ref, slope_ref, *outs)


def input_grad_kernel(dfirst_ref, own_ref, other_ref, live_ref, keep_ref, grad_ref, dmem_ref):
    dmem_ref[...] = input_rows(dfirst_ref, own_ref, other_ref, grad_ref, live_ref[...], keep_ref[...])


def attn_backward_kernel(dsecond_ref, own_ref, other_ref, first_ref, shared_ref, qk_ref, vo_ref, qkv_ref, lse_ref,
                         part_ref, dfirst_ref, da_ref, dqkv_ref, dhead_ref, dvec_ref, dctx_ref, lse_t_ref):
    rows = first_ref.shape[0]
    width = vo_ref.shape[1] // 2
    seg = rows - 2 * PAD
    dhidden = dsecond_ref[...] + (own_ref[...].astype(F32) + other_ref[...].astype(F32))
    unit, scale = norm_stats(first_ref[...])
    dfirst = norm_back(dhidden, shared_ref[USED + 2 : USED + 3, :], unit, scale)
    dfirst_ref[...] = dfirst
    dvec_ref[0:1, :] = row_sum(dfirst)
    dvec_ref[1:2, :] = row_sum(dhidden * unit)
    dvec_ref[2:3, :] = row_sum(dhidden)
    dvec_ref[3:, :] = jnp.zeros((dvec_ref.shape[0] - 3, unit.shape[1]), F32)
    da_ref[...] = dfirst.astype(BF)
    dctx_ref[...] = dot_nn(da_ref[...], vo_ref[:, width:]).astype(BF)
    lse_t_ref[...] = jnp.transpose(lse_ref[...])
    dead = dead_rows(rows)
    lane = lax.broadcasted_iota(jnp.int32, (rows, 128), 1)

    def heads(pair, carry):
        at = pl.multiple_of(pair * 128, 128)
        q = qkv_ref[:, pl.ds(at, 128)]
        k = qkv_ref[:, pl.ds(width + at, 128)]
        v = qkv_ref[:, pl.ds(2 * width + at, 128)]
        dc = dctx_ref[:, pl.ds(at, 128)]
        dq, dk, dv = None, None, None
        for head in range(2):
            mine = (lane < 64) if head == 0 else (lane >= 64)
            q_one = jnp.where(mine, q, jnp.zeros_like(q))
            dc_one = jnp.where(mine, dc, jnp.zeros_like(dc))
            s_t = masked_scores(q, k, mine, dead, lane, head, lambda a, b: dot_nt(b, a)) * (HD**-0.5 * LOG2E)
            lse_row = lse_t_ref[pl.ds(2 * pair + head, 1), :]
            p_t = jnp.exp2(s_t - lse_row)
            dp_t = dot_nt(v, dc_one)
            dv_one = dot_nn(p_t.astype(BF), dc_one)
            inner = row_sum(p_t * dp_t)
            ds_t = (p_t * (dp_t - inner)).astype(BF)
            dk_one = dot_nn(ds_t, q_one)
            dq_one = dot_tn(ds_t, jnp.where(mine, k, jnp.zeros_like(k)))
            dq = dq_one if dq is None else dq + dq_one
            dv = dv_one if dv is None else dv + dv_one
            dk = dk_one if dk is None else dk + dk_one
        dq = dq * (HD**-0.5)
        dk = dk * (HD**-0.5)
        dhead_ref[:, pl.ds(at, 128)] = row_sum(dq)
        dhead_ref[:, pl.ds(width + at, 128)] = row_sum(dv)
        dqkv_ref[:, pl.ds(at, 128)] = dq.astype(BF)
        dqkv_ref[:, pl.ds(width + at, 128)] = dk.astype(BF)
        dqkv_ref[:, pl.ds(2 * width + at, 128)] = dv.astype(BF)
        return carry

    lax.fori_loop(0, width // 128, heads, 0)
    part = dot_nt(dqkv_ref[:, : 2 * width], qk_ref[...]) + dot_nt(dqkv_ref[:, 2 * width :], vo_ref[:, :width])
    part_ref[...] = part.astype(BF)


def grad_close_kernel(lines, *refs):
    count = 3 * lines
    outs = refs[-4:]
    squares = None
    for matrix in range(3):
        total = refs[matrix * lines][...].astype(F32)
        for other in refs[matrix * lines + 1 : (matrix + 1) * lines]:
            total = total + other[...].astype(F32)
        outs[matrix][...] = total
        square = jnp.sum(total * total, keepdims=True)
        squares = square if squares is None else squares + square
    dmem_ref = refs[count]
    dvec_one, dvec_two, dhead, dbias = (refs[count + 1 + i : -4 : 4] for i in range(4))
    small = outs[3]
    model = small.shape[1]

    def total_of(group, row):
        total = group[0][row : row + 1, :]
        for ref in group[1:]:
            total = total + ref[row : row + 1, :]
        return total

    small[:PAD, :] = dmem_ref[...]
    for place, (group, row) in enumerate(((dvec_one, 0), (dvec_two, 0), (dvec_one, 1), (dvec_one, 2), (dvec_two, 1), (dvec_two, 2))):
        small[USED + place : USED + place + 1, :] = total_of(group, row)
    at = USED + 6
    for group in (dhead, dbias):
        whole = total_of(group, 0)
        for piece in range(whole.shape[1] // model):
            small[at : at + 1, :] = whole[:, piece * model : (piece + 1) * model]
            at += 1
    small[at:, :] = jnp.broadcast_to(squares, (small.shape[0] - at, model))


def adam_kernel(plan, small_ref, own_ref, other_ref, *refs):
    count = len(plan)
    grads = refs[:3]
    olds, news = refs[3 : 3 + 3 * count], refs[4 + 3 * count :]
    norm_ref = refs[3 + 3 * count]
    shared = small_ref[: USED + 6, :]
    norm = jnp.sqrt((own_ref[:1, :1] + other_ref[:1, :1]) + jnp.sum(shared * shared, keepdims=True))
    norm_ref[...] = norm
    factor = CLIP_NORM / jnp.maximum(norm, CLIP_NORM)
    for number, (source, row, column, rate, decay) in enumerate(plan):
        weight_ref, first_ref, second_ref = olds[3 * number : 3 * number + 3]
        height, length = weight_ref.shape[-2:]
        for index in range(math.prod(weight_ref.shape[:-2])):
            here = (index,) if weight_ref.ndim == 3 else ()
            if source is None and height == 1:
                model = small_ref.shape[1]
                gradient = jnp.concatenate([small_ref[row + i : row + i + 1, :] for i in range(length // model)], axis=1)
            elif source is None:
                gradient = small_ref[row : row + height, :]
            else:
                gradient = grads[source][:, column + index * length : column + (index + 1) * length]
            clipped = gradient * factor
            first = BETA_ONE * first_ref[here + (...,)] + (1.0 - BETA_ONE) * clipped
            second = BETA_TWO * second_ref[here + (...,)] + (1.0 - BETA_TWO) * clipped * clipped
            first_hat = first / (1.0 - BETA_ONE**STEP)
            second_hat = second / (1.0 - BETA_TWO**STEP)
            weight = weight_ref[here + (...,)]
            news[3 * number][here + (...,)] = weight - rate * (first_hat / (jnp.sqrt(second_hat) + ADAM_EPSILON) + decay * weight)
            news[3 * number + 1][here + (...,)] = first
            news[3 * number + 2][here + (...,)] = second


def weight_grad_kernel(plan, kinds, sizes, me_ref, *refs):
    count = len(kinds) * len(sizes)
    outs = refs[-count - 1 : -1]
    total_ref = refs[-1]
    block = total_ref.shape[0] // SLOTS
    for part, (kind, pieces) in enumerate(zip(kinds, plan)):
        at = 0
        for left, right, start, size in pieces:

            def rows_of(step, carry, left=left, right=right, start=start, size=size, at=at):
                begin = pl.multiple_of(step * CHUNK, CHUNK)
                total = None
                for one, two in zip(left, right):
                    add = dot_tn(refs[one][:, pl.ds(begin, CHUNK)], refs[two][:, start : start + size])
                    total = add if total is None else total + add
                total_ref[pl.ds(begin, CHUNK), at : at + size] = total
                return carry

            lax.fori_loop(0, total_ref.shape[0] // CHUNK, rows_of, 0)
            at += size
        number = 0
        for target in outs[part * len(sizes) : (part + 1) * len(sizes)]:
            for inner in range(target.shape[0]):
                place = lax.bitwise_xor(me_ref[0], slot_of(kind, number))
                begin = pl.multiple_of(place * block, block)
                target[inner] = total_ref[pl.ds(begin, block), :].astype(BF)
                number += 1


def exchange(values, axis, size, flip):
    return lax.ppermute(values, axis, [(i, i ^ flip) for i in range(size)])


def after(value, *others):
    return lax.optimization_barrier((value, *others))[0]


def add_low(*values):
    total = values[0].astype(F32)
    for value in values[1:]:
        total = total + value.astype(F32)
    return total


def canonical_split(full, kind, sizes):
    full = full.reshape(SLOTS, full.shape[0] // SLOTS, full.shape[1])
    full = jnp.stack([full[slot_of(kind, number)] for number in range(SLOTS)])
    ends = [sum(sizes[: i + 1]) for i in range(len(sizes))]
    return [full[end - size : end] for end, size in zip(ends, sizes)]


def canonical_join(pieces, kind):
    full = jnp.concatenate(pieces)
    order = [slot_of(kind, number) for number in range(SLOTS)]
    full = jnp.stack([full[order.index(d)] for d in range(SLOTS)])
    return full.reshape(-1, full.shape[-1])


def line_stage(own, size):
    return [own] + [exchange(own, "dp", size, 4 * j) for j in (1, 2, 3)]


def sum_all(values, axis, size):
    if size & (size - 1):
        return lax.psum(values, axis)
    flip = 1
    while flip < size:
        if flip * 4 <= size:
            near, far, both = [exchange(values, axis, size, flip * j) for j in (1, 2, 3)]
            values = (values + near) + (far + both)
            flip *= 4
        else:
            values = values + exchange(values, axis, size, flip)
            flip *= 2
    return values


def shards(
    size,
    pair,
    inputs,
    cotangent,
    seg_counts,
    qkv_weight,
    out_weight,
    up_weight,
    down_weight,
    head_bias,
    shared_params,
    qkv_first,
    out_first,
    up_first,
    down_first,
    bias_first,
    shared_first,
    qkv_second,
    out_second,
    up_second,
    down_second,
    bias_second,
    shared_second,
):
    unused, segments, seg, model = inputs.shape
    width = qkv_weight.shape[2]
    hidden = up_weight.shape[1]
    used = shared_params.shape[0] - 6
    pad = 16
    rows = seg + 2 * pad
    half = hidden // 2

    me = (lax.axis_index("dp") if size == SLOTS else jnp.int32(0)).astype(jnp.int32).reshape(1)
    qkv_low = qkv_weight.astype(BF)
    out_low = out_weight.T.astype(BF)
    up_low = up_weight.astype(BF)
    down_low = down_weight.T.astype(BF)
    own = [
        jnp.stack([jnp.concatenate([qkv_low[0], qkv_low[1]], axis=1), jnp.concatenate([qkv_low[2], out_low], axis=1)]),
        jnp.stack([up_low[:, :half], up_low[:, half:]]),
        jnp.stack([down_low[:, :half], down_low[:, half:]]),
    ]

    def assembled(kinds, pieces, joined):
        return call(
            functools.partial(assemble_kernel, kinds, [len(p) for p in pieces], joined),
            [((model, 2 * model), BF)] if joined else [((model, model), BF)] * 2,
            [me, *pieces[0], *pieces[1]],
            scalars=1,
        )

    z_first, z_mid = ("za", "zb"), ("xa", "xb")
    if size == SLOTS:

        def spread(lines):
            low_a = jnp.concatenate([lines[0], exchange(lines[0], "dp", size, 2)])
            low_b = jnp.concatenate([lines[1], exchange(lines[1], "dp", size, 1)])
            return low_a, low_b

        def finish(low_a, low_b):
            return exchange(low_a, "dp", size, 1), exchange(low_b, "dp", size, 2)

        pair_c = [jnp.stack([own[2][i], exchange(own[2][i], "dp", size, 1 + i)]) for i in range(2)]
        line_one = line_stage(own[0], size)
        line_two = line_stage(after(own[1], *line_one), size)
        low_one = spread([jnp.stack([v[i] for v in line_one]) for i in range(2)])
        line_three = line_stage(after(jnp.stack(pair_c), *line_two, *low_one), size)
        high_one = finish(*low_one)
        low_two = spread([after(jnp.stack([v[i] for v in line_two]), *high_one) for i in range(2)])
        high_two = finish(*low_two)
        low_c = [jnp.concatenate([v[i] for v in line_three]) for i in range(2)]
        low_c = [after(v, *high_two) for v in low_c]
        high_c = [exchange(low_c[i], "dp", size, 2 - i) for i in range(2)]
        w_qk, w_vo = assembled(z_first, [[low_one[i], high_one[i]] for i in range(2)], False)
        (w_up,) = assembled(z_first, [[low_two[i], high_two[i]] for i in range(2)], True)
        (w_down,) = assembled(z_mid, [[low_c[i], high_c[i]] for i in range(2)], True)
    else:

        def whole(number, kinds, sizes):
            pieces = [lax.all_gather(own[number][i], "dp", axis=0, tiled=True) for i in range(2)]
            return assembled(kinds, [canonical_split(p, kind, sizes) for p, kind in zip(pieces, kinds)], number > 0)

        w_qk, w_vo = whole(0, z_first, (8, 8))
        (w_up,) = whole(1, z_first, (8, 8))
        (w_down,) = whole(2, z_mid, (8, 8))

    memory = jnp.concatenate([shared_params[:used], jnp.zeros((pad - used, model), F32)], axis=0)
    alive = [(slot < seg_counts).astype(F32).reshape(1, 1) for slot in range(segments)]
    memories, tokens_out, saved = [memory], [], []
    attn_outs = [((rows, model), BF), ((rows, model), BF), ((rows, 3 * width), BF), ((rows, 128), F32), ((rows, width), BF)]
    for slot in range(segments):
        tokens = inputs[0, slot]
        if slot == 0:
            part, *attn = call(attn_forward_kernel, attn_outs, [tokens, memory, w_qk, w_vo, head_bias])
        else:
            out_rows, memory, second_in, part, *attn = call(
                attn_next_kernel,
                [((seg, model), BF), ((pad, model), F32), ((rows, model), F32)] + attn_outs,
                [saved[-1][4], ffn_part, other, shared_params, alive[slot - 1], memory, tokens, w_qk, w_vo, head_bias],
            )
            tokens_out.append(out_rows)
            saved[-1] += (second_in,)
        other = exchange(part, "head", pair, 1)
        ffn_part, first_in, h_low, active, slope = call(
            ffn_forward_kernel,
            [((rows, model), BF), ((rows, model), F32), ((rows, model), BF), ((rows, hidden), BF), ((rows, hidden), BF)],
            [tokens, memory, part, other, w_up, w_down, head_bias, shared_params],
        )
        other = exchange(ffn_part, "head", pair, 1)
        saved.append((*attn, first_in, h_low, active, slope))

    count = segments

    def weight_grad(names, plan, kinds):
        sizes = (8, 8)
        operands = [stacks[s][n] for n in names for s in range(count)]
        at = {n: [i * count + s for s in range(count)] for i, n in enumerate(names)}
        steps = [[(at[a], at[b], start, length) for a, b, start, length in pieces] for pieces in plan]
        result = call(
            functools.partial(weight_grad_kernel, steps, kinds, sizes),
            [((length, model // SLOTS, model), BF) for kind in kinds for length in sizes],
            [me, *operands],
            scalars=1,
            scratch=[pltpu.VMEM((model, model), F32)],
        )
        return result[: len(sizes)], result[len(sizes) :]

    dmem = jnp.zeros((pad, model), F32)
    grads = [None] * segments
    stacks = [None] * segments
    smalls = []
    ffn_outs = [((rows, model), BF), ((rows, model), F32), ((rows, model), BF), ((rows, hidden), BF), ((1, hidden), F32), ((8, model), F32)]
    for slot in reversed(range(segments)):
        low, qkv, lse, ctx, first_in, h_low, active, slope = saved[slot][:8]
        weights = [alive[slot], shared_params, w_up, w_down, slope]
        if slot == segments - 1:
            out_rows, part, dsecond, df_low, du, dbias, dvec_two = call(
                ffn_last_kernel,
                [((seg, model), BF)] + ffn_outs,
                [first_in, ffn_part, other, cotangent[0, slot], dmem, *weights],
            )
            tokens_out.append(out_rows)
        else:
            grads[slot + 1], dmem, part, dsecond, df_low, du, dbias, dvec_two = call(
                ffn_before_kernel,
                [((seg, model), BF), ((pad, model), F32)] + ffn_outs,
                [dfirst, part, other, alive[slot + 1], dmem, saved[slot][8], cotangent[0, slot], *weights],
            )
        other = exchange(part, "head", pair, 1)
        stacks[slot] = (low, ctx, h_low, active, df_low, du)
        if slot == 0:
            dw_down = weight_grad((DF_LOW, ACTIVE), [[(DF_LOW, ACTIVE, 0, half)], [(DF_LOW, ACTIVE, half, half)]], z_first)
            dw_up = weight_grad((H_LOW, DU), [[(H_LOW, DU, 0, half)], [(H_LOW, DU, half, half)]], z_first)
            dsecond = after(dsecond, dw_down[0][0], dw_up[0][0])
        part, dfirst, da, dqkv, dhead, dvec_one = call(
            attn_backward_kernel,
            [((rows, model), BF), ((rows, model), F32), ((rows, model), BF), ((rows, 3 * width), BF), ((1, 2 * width), F32), ((8, model), F32)],
            [dsecond, part, other, first_in, shared_params, w_qk, w_vo, qkv, lse],
            scratch=[pltpu.VMEM((rows, width), BF), pltpu.VMEM((128, rows), F32)],
        )
        other = exchange(part, "head", pair, 1)
        stacks[slot] += (da, dqkv)
        smalls += [dvec_one, dvec_two, dhead, dbias]
    grads[0], dmem = call(
        input_grad_kernel,
        [((seg, model), BF), ((pad, model), F32)],
        [dfirst, part, other, alive[0], dmem],
    )
    outputs = jnp.stack(tokens_out)[None]
    input_grad = jnp.stack(grads)[None]

    def fallback(parts, kinds):
        full = [canonical_join(p, kind) for p, kind in zip(parts, kinds)]
        full = jnp.concatenate(full, axis=1)
        return lax.psum_scatter(full, "dp", scatter_dimension=0, tiled=True).astype(F32)

    def hop(blocks, flips):
        return [exchange(block, "dp", size, flip) for block, flip in zip(blocks, flips)]

    def add_halves(keep, got):
        return [add_low(k, g).astype(BF) for k, g in zip(keep, got)]

    def line_hop(four):
        return [exchange(four[j], "dp", size, 4 * j) for j in (1, 2, 3)]

    x_first, y_first = (1, 2), (2, 1)
    if size == SLOTS:
        got_down, got_up = hop([p[1] for p in dw_down], x_first), hop([p[1] for p in dw_up], x_first)
        down = add_halves([p[0] for p in dw_down], [after(g, stacks[0][DQKV]) for g in got_down])
        stacks[0] = stacks[0][:DQKV] + (after(stacks[0][DQKV], *down),)
        got_down = hop([v[4:] for v in down], y_first)
    dw_qkvo = weight_grad(
        (LOW, DQKV, DA, CTX),
        [[(LOW, DQKV, 0, 2 * width)], [(LOW, DQKV, 2 * width, width), (DA, CTX, 0, width)]],
        z_first,
    )
    if size == SLOTS:
        dw_qkvo = [[after(v, *got_up, *got_down) for v in part] for part in dw_qkvo]
        got_qkvo = hop([p[1] for p in dw_qkvo], x_first)
        down = jnp.concatenate(add_halves([v[:4] for v in down], [after(g, dw_qkvo[0][0]) for g in got_down]), axis=2)
        got_down = line_hop(down)
        up = add_halves([p[0] for p in dw_up], [after(g, down) for g in got_up])
        got_up = hop([v[4:] for v in up], y_first)
        last = add_halves([p[0] for p in dw_qkvo], [after(g, *got_down) for g in got_qkvo])
        up = jnp.concatenate(add_halves([v[:4] for v in up], [after(g, *got_qkvo) for g in got_up]), axis=2)
        last = jnp.concatenate(add_halves([v[:4] for v in last], hop([v[4:] for v in last], y_first)), axis=2)
        sums = [[down[0], *got_down], [up[0], *line_hop(up)], [last[0], *line_hop(last)]]
    else:
        sums = [[fallback(p, z_first)] for p in (dw_down, dw_up, dw_qkvo)]
    height, wide = sums[0][0].shape
    *matrices, small = call(
        functools.partial(grad_close_kernel, len(sums[0])),
        [((height, wide), F32)] * 3 + [((24, model), F32)],
        [*sums[0], *sums[1], *sums[2], dmem, *smalls],
    )
    small = sum_all(small, "dp", size)
    bias_grad = small[used + 6 : used + 9]
    squares = jnp.full((8, 128), small[used + 9, 0] + jnp.sum(bias_grad * bias_grad))
    other = exchange(squares, "head", pair, 1)
    plan = (
        (2, 0, 0, LEARN_RATE, DECAY_RATE),
        (2, 0, 3 * width, LEARN_RATE, DECAY_RATE),
        (1, 0, 0, LEARN_RATE, DECAY_RATE),
        (0, 0, 0, LEARN_RATE, DECAY_RATE),
        (None, used + 6, 0, VECTOR_RATE, 0.0),
        (None, 0, 0, VECTOR_RATE, 0.0),
    )
    olds = (
        (qkv_weight, qkv_first, qkv_second),
        (out_weight.T, out_first.T, out_second.T),
        (up_weight, up_first, up_second),
        (down_weight.T, down_first.T, down_second.T),
        (head_bias, bias_first, bias_second),
        (shared_params, shared_first, shared_second),
    )
    grad_norm, *news = call(
        functools.partial(adam_kernel, plan),
        [((1, 1), F32)] + [(o.shape, F32) for old in olds for o in old],
        [small, squares, other, *matrices, *[o for old in olds for o in old]],
    )
    results = [news[3 * i : 3 * i + 3] for i in range(6)]
    for number in (1, 3):
        results[number] = [r.T for r in results[number]]
    return (outputs, input_grad, grad_norm[0, 0]) + tuple(r[i] for i in range(3) for r in results)


def solution(mesh):
    weights = (P(None, "dp", "head"), P("head", "dp"), P("dp", "head"), P("head", "dp"), P("head", None), P())
    rows = P("dp", None, None, None)
    return jax.shard_map(
        functools.partial(shards, mesh.shape["dp"], mesh.shape["head"]),
        mesh=mesh,
        in_specs=(rows, rows, P("dp")) + weights * 3,
        out_specs=(rows, rows, P()) + weights * 3,
        check_vma=False,
    )
```

```python
import functools
import math

import jax
import jax.numpy as jnp
from jax import lax
from jax.experimental import pallas as pl
from jax.experimental.pallas import tpu as pltpu
from jax.sharding import PartitionSpec as P

HD = 64
STEP = 10
EPSILON = 1e-06
BETA_ONE = 0.9
BETA_TWO = 0.999
LEARN_RATE = 0.1
VECTOR_RATE = 0.6
DECAY_RATE = 0.01
ADAM_EPSILON = 1e-08
CLIP_NORM = 1.0

BF = jnp.bfloat16
F32 = jnp.float32
LOG2E = math.log2(math.e)
NEG = -1e30
SLOTS = 16
PAD = 16
USED = 10
WIDE = 256
CHUNK = 256
LOW, CTX, H_LOW, ACTIVE, DF_LOW, DU, DA, DQKV = range(8)


def dot_nn(a, b):
    return lax.dot_general(a, b, (((1,), (0,)), ((), ())), preferred_element_type=F32)


def dot_nt(a, b):
    return lax.dot_general(a, b, (((1,), (1,)), ((), ())), preferred_element_type=F32)


def dot_tn(a, b):
    return lax.dot_general(a, b, (((0,), (0,)), ((), ())), preferred_element_type=F32)


def norm_stats(values):
    average = jnp.mean(values, axis=-1, keepdims=True)
    centered = values - average
    variance = jnp.mean(centered * centered, axis=-1, keepdims=True)
    scale = lax.rsqrt(variance + EPSILON)
    return centered * scale, scale


def norm_back(grad, gain, unit, scale):
    inner = grad * gain
    mean_one = jnp.mean(inner, axis=-1, keepdims=True)
    mean_two = jnp.mean(inner * unit, axis=-1, keepdims=True)
    return scale * (inner - mean_one - unit * mean_two)


def row_sum(values):
    return jnp.sum(values, axis=0, keepdims=True)


def call(kernel, outs, args, scalars=0, scratch=()):
    return pl.pallas_call(
        kernel,
        out_shape=[jax.ShapeDtypeStruct(s, d) for s, d in outs],
        in_specs=[pl.BlockSpec(memory_space=pltpu.SMEM)] * scalars
        + [pl.BlockSpec(memory_space=pltpu.VMEM)] * (len(args) - scalars),
        out_specs=[pl.BlockSpec(memory_space=pltpu.VMEM)] * len(outs),
        scratch_shapes=list(scratch),
        cost_estimate=pl.CostEstimate(flops=0, bytes_accessed=0, transcendentals=0),
        compiler_params=pltpu.CompilerParams(vmem_limit_bytes=16 << 20),
    )(*args)


def slot_of(kind, number):
    if kind[0] == "z":
        outer, mid, z = number // 8, number // 4 % 2, number % 4
        return (outer + 2 * mid if kind[1] == "a" else 2 * outer + mid) + 4 * z
    outer, z, inner = number // 8, number // 2 % 4, number % 2
    return (2 * outer + inner if kind[1] == "a" else outer + 2 * inner) + 4 * z


def assemble_kernel(kinds, counts, joined, me_ref, *refs):
    at = sum(counts)
    begin = 0
    for part, (kind, count) in enumerate(zip(kinds, counts)):
        target = refs[at] if joined else refs[at + part]
        block = target.shape[0] // SLOTS
        number = 0
        for source in refs[begin : begin + count]:
            length = source.shape[2]
            column = part * length if joined else 0
            for inner in range(source.shape[0]):
                place = lax.bitwise_xor(me_ref[0], slot_of(kind, number))
                start = pl.multiple_of(place * block, block)
                target[pl.ds(start, block), column : column + length] = source[inner]
                number += 1
        begin += count


def dead_rows(rows):
    at = lax.broadcasted_iota(jnp.int32, (rows, 128), 0) - (rows - 2 * PAD)
    return (at >= 0) & ((at & (PAD - 1)) >= USED)


def masked_scores(q, k, mine, dead, lane, head, dot):
    spare = lane == (127 if head == 0 else 0)
    zero = jnp.zeros_like(q)
    q_one = jnp.where(spare, jnp.ones_like(q), jnp.where(mine, q, zero))
    k_one = jnp.where(spare, jnp.where(dead, jnp.full_like(k, NEG), zero), k)
    return dot(q_one, k_one)


def attn_rows(low_ref, qk_ref, vo_ref, bias_ref, part_ref, qkv_ref, lse_ref, ctx_ref):
    rows = low_ref.shape[0]
    width = vo_ref.shape[1] // 2
    seg = rows - 2 * PAD
    low = low_ref[...]
    qk = dot_nn(low, qk_ref[...])
    qkv_ref[:, :width] = (qk[:, :width] + bias_ref[:, :width]).astype(BF)
    qkv_ref[:, width : 2 * width] = qk[:, width:].astype(BF)
    v_all = dot_nn(low, vo_ref[:, :width])
    qkv_ref[:, 2 * width :] = (v_all + bias_ref[:, width : 2 * width]).astype(BF)
    lane = lax.broadcasted_iota(jnp.int32, (rows, 128), 1)
    lse_ref[...] = jnp.zeros_like(lse_ref)
    dead = dead_rows(rows)

    def heads(pair, carry):
        at = pl.multiple_of(pair * 128, 128)
        q = qkv_ref[:, pl.ds(at, 128)]
        k = qkv_ref[:, pl.ds(width + at, 128)]
        v = qkv_ref[:, pl.ds(2 * width + at, 128)]
        outs = []
        for head in range(2):
            mine = (lane < 64) if head == 0 else (lane >= 64)
            s = masked_scores(q, k, mine, dead, lane, head, dot_nt) * (HD**-0.5 * LOG2E)
            top = jnp.max(s, axis=1, keepdims=True)
            e = jnp.exp2(s - top)
            total = jnp.sum(e, axis=1, keepdims=True)
            outs.append(dot_nn(e.astype(BF), v) * (1.0 / total))
            lse_ref[...] = jnp.where(lane == 2 * pair + head, top + jnp.log2(total), lse_ref[...])
        ctx_ref[:, pl.ds(at, 128)] = jnp.where(lane < 64, outs[0], outs[1]).astype(BF)
        return carry

    lax.fori_loop(0, width // 128, heads, 0)
    part_ref[...] = dot_nt(ctx_ref[...], vo_ref[:, width:]).astype(BF)


def attn_forward_kernel(token_ref, mem_ref, qk_ref, vo_ref, bias_ref, part_ref, low_ref, qkv_ref, lse_ref, ctx_ref):
    seg = token_ref.shape[0]
    memory = mem_ref[...].astype(BF)
    low_ref[:seg, :] = token_ref[...]
    low_ref[seg : seg + PAD, :] = memory
    low_ref[seg + PAD :, :] = memory
    attn_rows(low_ref, qk_ref, vo_ref, bias_ref, part_ref, qkv_ref, lse_ref, ctx_ref)


def close_rows(first_ref, own_ref, other_ref, shared_ref):
    unit, unused = norm_stats(first_ref[...])
    hidden = unit * shared_ref[USED + 2 : USED + 3, :] + shared_ref[USED + 3 : USED + 4, :]
    return hidden + (own_ref[...].astype(F32) + other_ref[...].astype(F32)) + shared_ref[USED + 1 : USED + 2, :]


def attn_next_kernel(first_ref, own_ref, other_ref, shared_ref, alive_ref, keep_ref, token_ref, qk_ref, vo_ref, bias_ref,
                     out_ref, mem_ref, second_ref, part_ref, low_ref, qkv_ref, lse_ref, ctx_ref):
    seg = token_ref.shape[0]
    second = close_rows(first_ref, own_ref, other_ref, shared_ref)
    second_ref[...] = second
    unit, unused = norm_stats(second)
    result = unit * shared_ref[USED + 4 : USED + 5, :] + shared_ref[USED + 5 : USED + 6, :]
    out_ref[...] = (result[:seg] * alive_ref[...]).astype(BF)
    row = lax.broadcasted_iota(jnp.int32, mem_ref.shape, 0)
    fresh = jnp.where(row < USED, result[seg + PAD :], 0.0)
    memory = jnp.where(alive_ref[...] > 0.0, fresh, keep_ref[...])
    mem_ref[...] = memory
    low_ref[:seg, :] = token_ref[...]
    low_ref[seg : seg + PAD, :] = memory.astype(BF)
    low_ref[seg + PAD :, :] = memory.astype(BF)
    attn_rows(low_ref, qk_ref, vo_ref, bias_ref, part_ref, qkv_ref, lse_ref, ctx_ref)


def ffn_forward_kernel(token_ref, mem_ref, own_ref, other_ref, up_ref, down_ref, bias_ref, shared_ref,
                       part_ref, first_ref, low_ref, act_ref, slope_ref):
    seg = token_ref.shape[0]
    hidden_units = up_ref.shape[1]
    begin = bias_ref.shape[1] - hidden_units
    attn = own_ref[...].astype(F32) + other_ref[...].astype(F32) + shared_ref[USED : USED + 1, :]
    first_ref[:seg, :] = token_ref[...].astype(F32) + attn[:seg]
    first_ref[seg : seg + PAD, :] = mem_ref[...] + attn[seg : seg + PAD]
    first_ref[seg + PAD :, :] = mem_ref[...] + attn[seg + PAD :]
    unit, unused = norm_stats(first_ref[...])
    hidden = unit * shared_ref[USED + 2 : USED + 3, :] + shared_ref[USED + 3 : USED + 4, :]
    low_ref[...] = hidden.astype(BF)

    def units(step, carry):
        for piece in range(2):
            at = pl.multiple_of(step * (2 * WIDE) + piece * WIDE, 128)
            u = dot_nn(low_ref[...], up_ref[:, pl.ds(at, WIDE)]) + bias_ref[:, pl.ds(begin + at, WIDE)]
            cdf = 0.5 + 0.5 * lax.erf(u * (0.5**0.5))
            density = jnp.exp2(u * u * (-0.5 * LOG2E)) * ((2.0 * math.pi) ** -0.5)
            active = (u * cdf).astype(BF)
            act_ref[:, pl.ds(at, WIDE)] = active
            slope_ref[:, pl.ds(at, WIDE)] = (cdf + u * density).astype(BF)
        return carry

    lax.fori_loop(0, hidden_units // (2 * WIDE), units, 0)
    part_ref[...] = dot_nt(act_ref[...], down_ref[...]).astype(BF)


def ffn_backward_rows(second, dmem, cot_ref, alive_ref, shared_ref, up_ref, down_ref, slope_ref,
                      part_ref, dsecond_ref, dlow_ref, du_ref, dbias_ref, dvec_ref):
    unit, scale = norm_stats(second)
    dy = jnp.concatenate(
        [cot_ref[...].astype(F32) * alive_ref[...], jnp.zeros((PAD, unit.shape[1]), F32), dmem * alive_ref[...]], axis=0
    )
    dsecond = norm_back(dy, shared_ref[USED + 4 : USED + 5, :], unit, scale)
    dsecond_ref[...] = dsecond
    dvec_ref[0:1, :] = row_sum(dsecond)
    dvec_ref[1:2, :] = row_sum(dy * unit)
    dvec_ref[2:3, :] = row_sum(dy)
    dvec_ref[3:, :] = jnp.zeros((dvec_ref.shape[0] - 3, unit.shape[1]), F32)
    dlow_ref[...] = dsecond.astype(BF)

    def units(step, carry):
        for piece in range(2):
            at = pl.multiple_of(step * (2 * WIDE) + piece * WIDE, 128)
            du = dot_nn(dlow_ref[...], down_ref[:, pl.ds(at, WIDE)]) * slope_ref[:, pl.ds(at, WIDE)].astype(F32)
            dbias_ref[:, pl.ds(at, WIDE)] = row_sum(du)
            du_low = du.astype(BF)
            du_ref[:, pl.ds(at, WIDE)] = du_low
        return carry

    lax.fori_loop(0, up_ref.shape[1] // (2 * WIDE), units, 0)
    part_ref[...] = dot_nt(du_ref[...], up_ref[...]).astype(BF)


def ffn_last_kernel(before, *refs):
    first_ref, own_ref, other_ref, cot_ref, dmem_ref, alive_ref, shared_ref, up_ref, down_ref, slope_ref, out_ref, *outs = refs[before:]
    for slot in range(before):
        out_ref[slot] = refs[slot][...]
    second = close_rows(first_ref, own_ref, other_ref, shared_ref)
    unit, unused = norm_stats(second)
    result = unit * shared_ref[USED + 4 : USED + 5, :] + shared_ref[USED + 5 : USED + 6, :]
    out_ref[before] = (result[: out_ref.shape[1]] * alive_ref[...]).astype(BF)
    ffn_backward_rows(second, dmem_ref[...], cot_ref, alive_ref, shared_ref, up_ref, down_ref, slope_ref, *outs)


def input_rows(dfirst_ref, own_ref, other_ref, grad_ref, here, live, keep):
    seg = grad_ref.shape[-2]
    dx = dfirst_ref[...] + (own_ref[...].astype(F32) + other_ref[...].astype(F32))
    grad_ref[here] = (dx[:seg] * live).astype(BF)
    return jnp.where(live > 0.0, dx[seg : seg + PAD] + dx[seg + PAD :], keep)


def ffn_before_kernel(dfirst_ref, own_ref, other_ref, live_ref, keep_ref, second_ref, cot_ref, alive_ref, shared_ref, up_ref, down_ref,
                      slope_ref, grad_ref, dmem_ref, *outs):
    dmem = input_rows(dfirst_ref, own_ref, other_ref, grad_ref, ..., live_ref[...], keep_ref[...])
    dmem_ref[...] = dmem
    ffn_backward_rows(second_ref[...], dmem, cot_ref, alive_ref, shared_ref, up_ref, down_ref, slope_ref, *outs)


def input_grad_kernel(dfirst_ref, own_ref, other_ref, live_ref, keep_ref, *refs):
    *later, grad_ref, dmem_ref = refs
    for slot, ref in enumerate(later):
        grad_ref[slot + 1] = ref[...]
    dmem_ref[...] = input_rows(dfirst_ref, own_ref, other_ref, grad_ref, 0, live_ref[...], keep_ref[...])


def attn_backward_kernel(dsecond_ref, own_ref, other_ref, first_ref, shared_ref, qk_ref, vo_ref, qkv_ref, lse_ref,
                         part_ref, dfirst_ref, da_ref, dqkv_ref, dhead_ref, dvec_ref, dctx_ref, lse_t_ref):
    rows = first_ref.shape[0]
    width = vo_ref.shape[1] // 2
    seg = rows - 2 * PAD
    dhidden = dsecond_ref[...] + (own_ref[...].astype(F32) + other_ref[...].astype(F32))
    unit, scale = norm_stats(first_ref[...])
    dfirst = norm_back(dhidden, shared_ref[USED + 2 : USED + 3, :], unit, scale)
    dfirst_ref[...] = dfirst
    dvec_ref[0:1, :] = row_sum(dfirst)
    dvec_ref[1:2, :] = row_sum(dhidden * unit)
    dvec_ref[2:3, :] = row_sum(dhidden)
    dvec_ref[3:, :] = jnp.zeros((dvec_ref.shape[0] - 3, unit.shape[1]), F32)
    da_ref[...] = dfirst.astype(BF)
    dctx_ref[...] = dot_nn(da_ref[...], vo_ref[:, width:]).astype(BF)
    lse_t_ref[...] = jnp.transpose(lse_ref[...])
    dead = dead_rows(rows)
    lane = lax.broadcasted_iota(jnp.int32, (rows, 128), 1)

    def heads(pair, carry):
        at = pl.multiple_of(pair * 128, 128)
        q = qkv_ref[:, pl.ds(at, 128)]
        k = qkv_ref[:, pl.ds(width + at, 128)]
        v = qkv_ref[:, pl.ds(2 * width + at, 128)]
        dc = dctx_ref[:, pl.ds(at, 128)]
        dq, dk, dv = None, None, None
        for head in range(2):
            mine = (lane < 64) if head == 0 else (lane >= 64)
            q_one = jnp.where(mine, q, jnp.zeros_like(q))
            dc_one = jnp.where(mine, dc, jnp.zeros_like(dc))
            s_t = masked_scores(q, k, mine, dead, lane, head, lambda a, b: dot_nt(b, a)) * (HD**-0.5 * LOG2E)
            lse_row = lse_t_ref[pl.ds(2 * pair + head, 1), :]
            p_t = jnp.exp2(s_t - lse_row)
            dp_t = dot_nt(v, dc_one)
            dv_one = dot_nn(p_t.astype(BF), dc_one)
            inner = row_sum(p_t * dp_t)
            ds_t = (p_t * (dp_t - inner)).astype(BF)
            dk_one = dot_nn(ds_t, q_one)
            dq_one = dot_tn(ds_t, jnp.where(mine, k, jnp.zeros_like(k)))
            dq = dq_one if dq is None else dq + dq_one
            dv = dv_one if dv is None else dv + dv_one
            dk = dk_one if dk is None else dk + dk_one
        dq = dq * (HD**-0.5)
        dk = dk * (HD**-0.5)
        dhead_ref[:, pl.ds(at, 128)] = row_sum(dq)
        dhead_ref[:, pl.ds(width + at, 128)] = row_sum(dv)
        dqkv_ref[:, pl.ds(at, 128)] = dq.astype(BF)
        dqkv_ref[:, pl.ds(width + at, 128)] = dk.astype(BF)
        dqkv_ref[:, pl.ds(2 * width + at, 128)] = dv.astype(BF)
        return carry

    lax.fori_loop(0, width // 128, heads, 0)
    part = dot_nt(dqkv_ref[:, : 2 * width], qk_ref[...]) + dot_nt(dqkv_ref[:, 2 * width :], vo_ref[:, :width])
    part_ref[...] = part.astype(BF)


def grad_close_kernel(lines, *refs):
    count = 3 * lines
    outs = refs[-4:]
    squares = None
    for matrix in range(3):
        total = refs[matrix * lines][...].astype(F32)
        for other in refs[matrix * lines + 1 : (matrix + 1) * lines]:
            total = total + other[...].astype(F32)
        outs[matrix][...] = total
        square = jnp.sum(total * total, keepdims=True)
        squares = square if squares is None else squares + square
    dmem_ref = refs[count]
    dvec_one, dvec_two, dhead, dbias = (refs[count + 1 + i : -4 : 4] for i in range(4))
    small = outs[3]
    model = small.shape[1]

    def total_of(group, row):
        total = group[0][row : row + 1, :]
        for ref in group[1:]:
            total = total + ref[row : row + 1, :]
        return total

    small[:PAD, :] = dmem_ref[...]
    for place, (group, row) in enumerate(((dvec_one, 0), (dvec_two, 0), (dvec_one, 1), (dvec_one, 2), (dvec_two, 1), (dvec_two, 2))):
        small[USED + place : USED + place + 1, :] = total_of(group, row)
    at = USED + 6
    for group in (dhead, dbias):
        whole = total_of(group, 0)
        for piece in range(whole.shape[1] // model):
            small[at : at + 1, :] = whole[:, piece * model : (piece + 1) * model]
            at += 1
    small[at:, :] = jnp.broadcast_to(squares, (small.shape[0] - at, model))


def adam_kernel(plan, small_ref, other_ref, *refs):
    count = len(plan)
    grads = refs[:3]
    olds, news = refs[3 : 3 + 3 * count], refs[4 + 3 * count :]
    norm_ref = refs[3 + 3 * count]
    shared = small_ref[: USED + 6, :]
    halves = []
    for ref in (small_ref, other_ref):
        biases = ref[USED + 6 : USED + 9, :]
        halves.append(ref[USED + 9 : USED + 10, :1] + jnp.sum(biases * biases, keepdims=True))
    norm = jnp.sqrt((halves[0] + halves[1]) + jnp.sum(shared * shared, keepdims=True))
    norm_ref[...] = norm
    factor = CLIP_NORM / jnp.maximum(norm, CLIP_NORM)
    for number, (source, row, column, rate, decay) in enumerate(plan):
        weight_ref, first_ref, second_ref = olds[3 * number : 3 * number + 3]
        height, length = weight_ref.shape[-2:]
        for index in range(math.prod(weight_ref.shape[:-2])):
            here = (index,) if weight_ref.ndim == 3 else ()
            if source is None and height == 1:
                model = small_ref.shape[1]
                gradient = jnp.concatenate([small_ref[row + i : row + i + 1, :] for i in range(length // model)], axis=1)
            elif source is None:
                gradient = small_ref[row : row + height, :]
            else:
                gradient = grads[source][:, column + index * length : column + (index + 1) * length]
            clipped = gradient * factor
            first = BETA_ONE * first_ref[here + (...,)] + (1.0 - BETA_ONE) * clipped
            second = BETA_TWO * second_ref[here + (...,)] + (1.0 - BETA_TWO) * clipped * clipped
            first_hat = first / (1.0 - BETA_ONE**STEP)
            second_hat = second / (1.0 - BETA_TWO**STEP)
            weight = weight_ref[here + (...,)]
            news[3 * number][here + (...,)] = weight - rate * (first_hat / (jnp.sqrt(second_hat) + ADAM_EPSILON) + decay * weight)
            news[3 * number + 1][here + (...,)] = first
            news[3 * number + 2][here + (...,)] = second


def weight_start_kernel(left_ref, right_ref, total_ref):
    def rows_of(step, carry):
        begin = pl.multiple_of(step * CHUNK, CHUNK)
        total_ref[pl.ds(begin, CHUNK), :] = dot_tn(left_ref[:, pl.ds(begin, CHUNK)], right_ref[...])
        return carry

    lax.fori_loop(0, total_ref.shape[0] // CHUNK, rows_of, 0)


def weight_grad_kernel(plan, kinds, sizes, base, me_ref, *refs):
    count = len(kinds) * len(sizes)
    outs = refs[-count - 1 : -1]
    total_ref = refs[-1]
    block = total_ref.shape[0] // SLOTS
    for part, (kind, pieces) in enumerate(zip(kinds, plan)):
        at = 0
        for left, right, start, size in pieces:

            def rows_of(step, carry, left=left, right=right, start=start, size=size, at=at):
                begin = pl.multiple_of(step * CHUNK, CHUNK)
                total = None if base is None else refs[base][pl.ds(begin, CHUNK), start : start + size]
                for one, two in zip(left, right):
                    add = dot_tn(refs[one][:, pl.ds(begin, CHUNK)], refs[two][:, start : start + size])
                    total = add if total is None else total + add
                total_ref[pl.ds(begin, CHUNK), at : at + size] = total
                return carry

            lax.fori_loop(0, total_ref.shape[0] // CHUNK, rows_of, 0)
            at += size
        number = 0
        for target in outs[part * len(sizes) : (part + 1) * len(sizes)]:
            for inner in range(target.shape[0]):
                place = lax.bitwise_xor(me_ref[0], slot_of(kind, number))
                begin = pl.multiple_of(place * block, block)
                target[inner] = total_ref[pl.ds(begin, block), :].astype(BF)
                number += 1


def exchange(values, axis, size, flip):
    return lax.ppermute(values, axis, [(i, i ^ flip) for i in range(size)])


def after(value, *others):
    return lax.optimization_barrier((value, *others))[0]


def add_low(*values):
    total = values[0].astype(F32)
    for value in values[1:]:
        total = total + value.astype(F32)
    return total


def canonical_split(full, kind, sizes):
    full = full.reshape(SLOTS, full.shape[0] // SLOTS, full.shape[1])
    full = jnp.stack([full[slot_of(kind, number)] for number in range(SLOTS)])
    ends = [sum(sizes[: i + 1]) for i in range(len(sizes))]
    return [full[end - size : end] for end, size in zip(ends, sizes)]


def canonical_join(pieces, kind):
    full = jnp.concatenate(pieces)
    order = [slot_of(kind, number) for number in range(SLOTS)]
    full = jnp.stack([full[order.index(d)] for d in range(SLOTS)])
    return full.reshape(-1, full.shape[-1])


def line_stage(own, size):
    return [own] + [exchange(own, "dp", size, 4 * j) for j in (1, 2, 3)]


def sum_all(values, axis, size):
    if size & (size - 1):
        return lax.psum(values, axis)
    flip = 1
    while flip < size:
        if flip * 4 <= size:
            near, far, both = [exchange(values, axis, size, flip * j) for j in (1, 2, 3)]
            values = (values + near) + (far + both)
            flip *= 4
        else:
            values = values + exchange(values, axis, size, flip)
            flip *= 2
    return values


def shards(
    size,
    pair,
    inputs,
    cotangent,
    seg_counts,
    qkv_weight,
    out_weight,
    up_weight,
    down_weight,
    head_bias,
    shared_params,
    qkv_first,
    out_first,
    up_first,
    down_first,
    bias_first,
    shared_first,
    qkv_second,
    out_second,
    up_second,
    down_second,
    bias_second,
    shared_second,
):
    unused, segments, seg, model = inputs.shape
    width = qkv_weight.shape[2]
    hidden = up_weight.shape[1]
    used = shared_params.shape[0] - 6
    pad = 16
    rows = seg + 2 * pad
    half = hidden // 2

    me = (lax.axis_index("dp") if size == SLOTS else jnp.int32(0)).astype(jnp.int32).reshape(1)
    qkv_low = qkv_weight.astype(BF)
    out_low = out_weight.T.astype(BF)
    up_low = up_weight.astype(BF)
    down_low = down_weight.T.astype(BF)
    own = [
        jnp.stack([jnp.concatenate([qkv_low[0], qkv_low[1]], axis=1), jnp.concatenate([qkv_low[2], out_low], axis=1)]),
        jnp.stack([up_low[:, :half], up_low[:, half:]]),
        jnp.stack([down_low[:, :half], down_low[:, half:]]),
    ]

    def assembled(kinds, pieces, joined):
        return call(
            functools.partial(assemble_kernel, kinds, [len(p) for p in pieces], joined),
            [((model, 2 * model), BF)] if joined else [((model, model), BF)] * 2,
            [me, *pieces[0], *pieces[1]],
            scalars=1,
        )

    z_first, z_mid = ("za", "zb"), ("xa", "xb")
    if size == SLOTS:

        def spread(lines):
            low_a = jnp.concatenate([lines[0], exchange(lines[0], "dp", size, 2)])
            low_b = jnp.concatenate([lines[1], exchange(lines[1], "dp", size, 1)])
            return low_a, low_b

        def finish(low_a, low_b):
            return exchange(low_a, "dp", size, 1), exchange(low_b, "dp", size, 2)

        pair_c = [jnp.stack([own[2][i], exchange(own[2][i], "dp", size, 1 + i)]) for i in range(2)]
        line_one = line_stage(own[0], size)
        line_two = line_stage(after(own[1], *line_one), size)
        low_one = spread([jnp.stack([v[i] for v in line_one]) for i in range(2)])
        line_three = line_stage(after(jnp.stack(pair_c), *line_two, *low_one), size)
        high_one = finish(*low_one)
        low_two = spread([after(jnp.stack([v[i] for v in line_two]), *high_one) for i in range(2)])
        high_two = finish(*low_two)
        low_c = [jnp.concatenate([v[i] for v in line_three]) for i in range(2)]
        low_c = [after(v, *high_two) for v in low_c]
        high_c = [exchange(low_c[i], "dp", size, 2 - i) for i in range(2)]
        w_qk, w_vo = assembled(z_first, [[low_one[i], high_one[i]] for i in range(2)], False)
        (w_up,) = assembled(z_first, [[low_two[i], high_two[i]] for i in range(2)], True)
        (w_down,) = assembled(z_mid, [[low_c[i], high_c[i]] for i in range(2)], True)
    else:

        def whole(number, kinds, sizes):
            pieces = [lax.all_gather(own[number][i], "dp", axis=0, tiled=True) for i in range(2)]
            return assembled(kinds, [canonical_split(p, kind, sizes) for p, kind in zip(pieces, kinds)], number > 0)

        w_qk, w_vo = whole(0, z_first, (8, 8))
        (w_up,) = whole(1, z_first, (8, 8))
        (w_down,) = whole(2, z_mid, (8, 8))

    memory = jnp.concatenate([shared_params[:used], jnp.zeros((pad - used, model), F32)], axis=0)
    alive = [(slot < seg_counts).astype(F32).reshape(1, 1) for slot in range(segments)]
    memories, tokens_out, saved = [memory], [], []
    attn_outs = [((rows, model), BF), ((rows, model), BF), ((rows, 3 * width), BF), ((rows, 128), F32), ((rows, width), BF)]
    for slot in range(segments):
        tokens = inputs[0, slot]
        if slot == 0:
            part, *attn = call(attn_forward_kernel, attn_outs, [tokens, memory, w_qk, w_vo, head_bias])
        else:
            out_rows, memory, second_in, part, *attn = call(
                attn_next_kernel,
                [((seg, model), BF), ((pad, model), F32), ((rows, model), F32)] + attn_outs,
                [saved[-1][4], ffn_part, other, shared_params, alive[slot - 1], memory, tokens, w_qk, w_vo, head_bias],
            )
            tokens_out.append(out_rows)
            saved[-1] += (second_in,)
        other = exchange(part, "head", pair, 1)
        ffn_part, first_in, h_low, active, slope = call(
            ffn_forward_kernel,
            [((rows, model), BF), ((rows, model), F32), ((rows, model), BF), ((rows, hidden), BF), ((rows, hidden), BF)],
            [tokens, memory, part, other, w_up, w_down, head_bias, shared_params],
        )
        other = exchange(ffn_part, "head", pair, 1)
        saved.append((*attn, first_in, h_low, active, slope))

    count = segments

    def weight_grad(names, plan, kinds, base=None):
        sizes = (8, 8)
        slots = range(count) if base is None else (0,)
        operands = [stacks[s][n] for n in names for s in slots]
        at = {n: [i * len(slots) + j for j in range(len(slots))] for i, n in enumerate(names)}
        steps = [[(at[a], at[b], start, length) for a, b, start, length in pieces] for pieces in plan]
        result = call(
            functools.partial(weight_grad_kernel, steps, kinds, sizes, None if base is None else len(operands)),
            [((length, model // SLOTS, model), BF) for kind in kinds for length in sizes],
            [me, *operands] + ([] if base is None else [base]),
            scalars=1,
            scratch=[pltpu.VMEM((model, model), F32)],
        )
        return result[: len(sizes)], result[len(sizes) :]

    dmem = jnp.zeros((pad, model), F32)
    grads = [None] * segments
    stacks = [None] * segments
    smalls, base = [], None
    ffn_outs = [((rows, model), BF), ((rows, model), F32), ((rows, model), BF), ((rows, hidden), BF), ((1, hidden), F32), ((8, model), F32)]
    for slot in reversed(range(segments)):
        low, qkv, lse, ctx, first_in, h_low, active, slope = saved[slot][:8]
        weights = [alive[slot], shared_params, w_up, w_down, slope]
        if slot == segments - 1:
            outputs, part, dsecond, df_low, du, dbias, dvec_two = call(
                functools.partial(ffn_last_kernel, slot),
                [((segments, seg, model), BF)] + ffn_outs,
                [*tokens_out, first_in, ffn_part, other, cotangent[0, slot], dmem, *weights],
            )
        else:
            grads[slot + 1], dmem, part, dsecond, df_low, du, dbias, dvec_two = call(
                ffn_before_kernel,
                [((seg, model), BF), ((pad, model), F32)] + ffn_outs,
                [dfirst, part, other, alive[slot + 1], dmem, saved[slot][8], cotangent[0, slot], *weights],
            )
        other = exchange(part, "head", pair, 1)
        stacks[slot] = (low, ctx, h_low, active, df_low, du)
        if slot == 0:
            dw_down = weight_grad((DF_LOW, ACTIVE), [[(DF_LOW, ACTIVE, 0, half)], [(DF_LOW, ACTIVE, half, half)]], z_first, base)
            dw_up = weight_grad((H_LOW, DU), [[(H_LOW, DU, 0, half)], [(H_LOW, DU, half, half)]], z_first)
            dsecond = after(dsecond, dw_down[0][0], dw_up[0][0])
        elif segments == 2:
            (base,) = call(weight_start_kernel, [((model, hidden), F32)], [df_low, active])
            dsecond = after(dsecond, base)
        part, dfirst, da, dqkv, dhead, dvec_one = call(
            attn_backward_kernel,
            [((rows, model), BF), ((rows, model), F32), ((rows, model), BF), ((rows, 3 * width), BF), ((1, 2 * width), F32), ((8, model), F32)],
            [dsecond, part, other, first_in, shared_params, w_qk, w_vo, qkv, lse],
            scratch=[pltpu.VMEM((rows, width), BF), pltpu.VMEM((128, rows), F32)],
        )
        other = exchange(part, "head", pair, 1)
        stacks[slot] += (da, dqkv)
        smalls += [dvec_one, dvec_two, dhead, dbias]
    input_grad, dmem = call(
        input_grad_kernel,
        [((segments, seg, model), BF), ((pad, model), F32)],
        [dfirst, part, other, alive[0], dmem, *grads[1:]],
    )

    def fallback(parts, kinds):
        full = [canonical_join(p, kind) for p, kind in zip(parts, kinds)]
        full = jnp.concatenate(full, axis=1)
        return lax.psum_scatter(full, "dp", scatter_dimension=0, tiled=True).astype(F32)

    def hop(blocks, flips):
        return [exchange(block, "dp", size, flip) for block, flip in zip(blocks, flips)]

    def add_halves(keep, got):
        return [add_low(k, g).astype(BF) for k, g in zip(keep, got)]

    def line_hop(four):
        return [exchange(four[j], "dp", size, 4 * j) for j in (1, 2, 3)]

    x_first, y_first = (1, 2), (2, 1)
    if size == SLOTS:
        got_down, got_up = hop([p[1] for p in dw_down], x_first), hop([p[1] for p in dw_up], x_first)
        down = add_halves([p[0] for p in dw_down], [after(g, stacks[0][DQKV]) for g in got_down])
        got_down = hop([v[4:] for v in down], y_first)
        up = add_halves([p[0] for p in dw_up], [after(g, *down) for g in got_up])
        stacks[0] = stacks[0][:DQKV] + (after(stacks[0][DQKV], *up),)
        got_up = hop([v[4:] for v in up], y_first)
    dw_qkvo = weight_grad(
        (LOW, DQKV, DA, CTX),
        [[(LOW, DQKV, 0, 2 * width)], [(LOW, DQKV, 2 * width, width), (DA, CTX, 0, width)]],
        z_first,
    )
    if size == SLOTS:
        got_down = [after(g, dw_qkvo[0][0]) for g in got_down]
        down = jnp.concatenate(add_halves([v[:4] for v in down], got_down), axis=2)
        got_down = line_hop(down)
        dw_qkvo = [[after(v, *got_up) for v in part] for part in dw_qkvo]
        got_qkvo = hop([p[1] for p in dw_qkvo], x_first)
        up = jnp.concatenate(add_halves([v[:4] for v in up], got_up), axis=2)
        got_up = line_hop(up)
        last = add_halves([p[0] for p in dw_qkvo], [after(g, *got_down, *got_up) for g in got_qkvo])
        got_qkvo = hop([v[4:] for v in last], y_first)
        last = jnp.concatenate(add_halves([v[:4] for v in last], got_qkvo), axis=2)
        sums = [[down[0], *got_down], [up[0], *got_up], [last[0], *line_hop(last)]]
    else:
        sums = [[fallback(p, z_first)] for p in (dw_down, dw_up, dw_qkvo)]
    height, wide = sums[0][0].shape
    *matrices, small = call(
        functools.partial(grad_close_kernel, len(sums[0])),
        [((height, wide), F32)] * 3 + [((24, model), F32)],
        [*sums[0], *sums[1], *sums[2], dmem, *smalls],
    )
    small = sum_all(small, "dp", size)
    other = exchange(small, "head", pair, 1)
    plan = (
        (2, 0, 0, LEARN_RATE, DECAY_RATE),
        (2, 0, 3 * width, LEARN_RATE, DECAY_RATE),
        (1, 0, 0, LEARN_RATE, DECAY_RATE),
        (0, 0, 0, LEARN_RATE, DECAY_RATE),
        (None, used + 6, 0, VECTOR_RATE, 0.0),
        (None, 0, 0, VECTOR_RATE, 0.0),
    )
    olds = (
        (qkv_weight, qkv_first, qkv_second),
        (out_weight.T, out_first.T, out_second.T),
        (up_weight, up_first, up_second),
        (down_weight.T, down_first.T, down_second.T),
        (head_bias, bias_first, bias_second),
        (shared_params, shared_first, shared_second),
    )
    grad_norm, *news = call(
        functools.partial(adam_kernel, plan),
        [((1, 1), F32)] + [(o.shape, F32) for old in olds for o in old],
        [small, other, *matrices, *[o for old in olds for o in old]],
    )
    results = [news[3 * i : 3 * i + 3] for i in range(6)]
    for number in (1, 3):
        results[number] = [r.T for r in results[number]]
    return (outputs[None], input_grad[None], grad_norm[0, 0]) + tuple(r[i] for i in range(3) for r in results)


def solution(mesh):
    weights = (P(None, "dp", "head"), P("head", "dp"), P("dp", "head"), P("head", "dp"), P("head", None), P())
    rows = P("dp", None, None, None)
    return jax.shard_map(
        functools.partial(shards, mesh.shape["dp"], mesh.shape["head"]),
        mesh=mesh,
        in_specs=(rows, rows, P("dp")) + weights * 3,
        out_specs=(rows, rows, P()) + weights * 3,
        check_vma=False,
    )
```

```python
import functools
import math

import jax
import jax.numpy as jnp
from jax import lax
from jax.experimental import pallas as pl
from jax.experimental.pallas import tpu as pltpu
from jax.sharding import PartitionSpec as P

HD = 64
STEP = 10
EPSILON = 1e-06
BETA_ONE = 0.9
BETA_TWO = 0.999
LEARN_RATE = 0.1
VECTOR_RATE = 0.6
DECAY_RATE = 0.01
ADAM_EPSILON = 1e-08
CLIP_NORM = 1.0

BF = jnp.bfloat16
F32 = jnp.float32
LOG2E = math.log2(math.e)
NEG = -1e30
SLOTS = 16
PAD = 16
USED = 10
WIDE = 256
CHUNK = 256
LOW, CTX, H_LOW, ACTIVE, DF_LOW, DU, DA, DQKV = range(8)


def dot_nn(a, b):
    return lax.dot_general(a, b, (((1,), (0,)), ((), ())), preferred_element_type=F32)


def dot_nt(a, b):
    return lax.dot_general(a, b, (((1,), (1,)), ((), ())), preferred_element_type=F32)


def dot_tn(a, b):
    return lax.dot_general(a, b, (((0,), (0,)), ((), ())), preferred_element_type=F32)


def norm_stats(values):
    average = jnp.mean(values, axis=-1, keepdims=True)
    centered = values - average
    variance = jnp.mean(centered * centered, axis=-1, keepdims=True)
    scale = lax.rsqrt(variance + EPSILON)
    return centered * scale, scale


def norm_back(grad, gain, unit, scale):
    inner = grad * gain
    mean_one = jnp.mean(inner, axis=-1, keepdims=True)
    mean_two = jnp.mean(inner * unit, axis=-1, keepdims=True)
    return scale * (inner - mean_one - unit * mean_two)


def row_sum(values):
    return jnp.sum(values, axis=0, keepdims=True)


def call(kernel, outs, args, scalars=0, scratch=()):
    return pl.pallas_call(
        kernel,
        out_shape=[jax.ShapeDtypeStruct(s, d) for s, d in outs],
        in_specs=[pl.BlockSpec(memory_space=pltpu.SMEM)] * scalars
        + [pl.BlockSpec(memory_space=pltpu.VMEM)] * (len(args) - scalars),
        out_specs=[pl.BlockSpec(memory_space=pltpu.VMEM)] * len(outs),
        scratch_shapes=list(scratch),
        cost_estimate=pl.CostEstimate(flops=0, bytes_accessed=0, transcendentals=0),
        compiler_params=pltpu.CompilerParams(vmem_limit_bytes=16 << 20),
    )(*args)


def slot_of(kind, number):
    if kind[0] == "z":
        outer, mid, z = number // 8, number // 4 % 2, number % 4
        return (outer + 2 * mid if kind[1] == "a" else 2 * outer + mid) + 4 * z
    outer, z, inner = number // 8, number // 2 % 4, number % 2
    return (2 * outer + inner if kind[1] == "a" else outer + 2 * inner) + 4 * z


def own_first_kernel(qkv_ref, out_ref, own_ref):
    width = out_ref.shape[1]
    for part in range(2):
        own_ref[part, :, :width] = qkv_ref[2 * part].astype(BF)
    own_ref[0, :, width:] = qkv_ref[1].astype(BF)
    own_ref[1, :, width:] = out_ref[...].astype(BF)


def own_next_kernel(up_ref, down_ref, up_own_ref, *down_own_refs):
    half = up_ref.shape[1] // 2
    for part in range(2):
        up_own_ref[part] = up_ref[:, part * half : (part + 1) * half].astype(BF)
        down_own_refs[part][...] = down_ref[:, part * half : (part + 1) * half].astype(BF)


def line_kernel(*refs):
    for part, target in enumerate(refs[4:]):
        for place, source in enumerate(refs[:4]):
            target[place] = source[part]


def assemble_kernel(kinds, counts, joined, me_ref, *refs):
    at = sum(counts)
    begin = 0
    for part, (kind, count) in enumerate(zip(kinds, counts)):
        target = refs[at] if joined else refs[at + part]
        block = target.shape[0] // SLOTS
        number = 0
        for source in refs[begin : begin + count]:
            length = source.shape[2]
            column = part * length if joined else 0
            for inner in range(source.shape[0]):
                place = lax.bitwise_xor(me_ref[0], slot_of(kind, number))
                start = pl.multiple_of(place * block, block)
                target[pl.ds(start, block), column : column + length] = source[inner]
                number += 1
        begin += count


def dead_rows(rows):
    at = lax.broadcasted_iota(jnp.int32, (rows, 128), 0) - (rows - 2 * PAD)
    return (at >= 0) & ((at & (PAD - 1)) >= USED)


def masked_scores(q, k, mine, dead, lane, head, dot):
    spare = lane == (127 if head == 0 else 0)
    zero = jnp.zeros_like(q)
    q_one = jnp.where(spare, jnp.ones_like(q), jnp.where(mine, q, zero))
    k_one = jnp.where(spare, jnp.where(dead, jnp.full_like(k, NEG), zero), k)
    return dot(q_one, k_one)


def attn_rows(low_ref, qk_ref, vo_ref, bias_ref, part_ref, qkv_ref, lse_ref, ctx_ref):
    rows = low_ref.shape[0]
    width = vo_ref.shape[1] // 2
    seg = rows - 2 * PAD
    low = low_ref[...]
    qk = dot_nn(low, qk_ref[...])
    qkv_ref[:, :width] = (qk[:, :width] + bias_ref[:, :width]).astype(BF)
    qkv_ref[:, width : 2 * width] = qk[:, width:].astype(BF)
    v_all = dot_nn(low, vo_ref[:, :width])
    qkv_ref[:, 2 * width :] = (v_all + bias_ref[:, width : 2 * width]).astype(BF)
    lane = lax.broadcasted_iota(jnp.int32, (rows, 128), 1)
    lse_ref[...] = jnp.zeros_like(lse_ref)
    dead = dead_rows(rows)

    def heads(pair, carry):
        at = pl.multiple_of(pair * 128, 128)
        q = qkv_ref[:, pl.ds(at, 128)]
        k = qkv_ref[:, pl.ds(width + at, 128)]
        v = qkv_ref[:, pl.ds(2 * width + at, 128)]
        outs = []
        for head in range(2):
            mine = (lane < 64) if head == 0 else (lane >= 64)
            s = masked_scores(q, k, mine, dead, lane, head, dot_nt) * (HD**-0.5 * LOG2E)
            top = jnp.max(s, axis=1, keepdims=True)
            e = jnp.exp2(s - top)
            total = jnp.sum(e, axis=1, keepdims=True)
            outs.append(dot_nn(e.astype(BF), v) * (1.0 / total))
            lse_ref[...] = jnp.where(lane == 2 * pair + head, top + jnp.log2(total), lse_ref[...])
        ctx_ref[:, pl.ds(at, 128)] = jnp.where(lane < 64, outs[0], outs[1]).astype(BF)
        return carry

    lax.fori_loop(0, width // 128, heads, 0)
    part_ref[...] = dot_nt(ctx_ref[...], vo_ref[:, width:]).astype(BF)


def attn_forward_kernel(token_ref, mem_ref, qk_ref, vo_ref, bias_ref, part_ref, low_ref, qkv_ref, lse_ref, ctx_ref):
    seg = token_ref.shape[0]
    memory = mem_ref[...].astype(BF)
    low_ref[:seg, :] = token_ref[...]
    low_ref[seg : seg + PAD, :] = memory
    low_ref[seg + PAD :, :] = memory
    attn_rows(low_ref, qk_ref, vo_ref, bias_ref, part_ref, qkv_ref, lse_ref, ctx_ref)


def close_rows(first_ref, own_ref, other_ref, shared_ref):
    unit, unused = norm_stats(first_ref[...])
    hidden = unit * shared_ref[USED + 2 : USED + 3, :] + shared_ref[USED + 3 : USED + 4, :]
    return hidden + (own_ref[...].astype(F32) + other_ref[...].astype(F32)) + shared_ref[USED + 1 : USED + 2, :]


def attn_next_kernel(first_ref, own_ref, other_ref, shared_ref, alive_ref, keep_ref, token_ref, qk_ref, vo_ref, bias_ref,
                     out_ref, mem_ref, second_ref, part_ref, low_ref, qkv_ref, lse_ref, ctx_ref):
    seg = token_ref.shape[0]
    second = close_rows(first_ref, own_ref, other_ref, shared_ref)
    second_ref[...] = second
    unit, unused = norm_stats(second)
    result = unit * shared_ref[USED + 4 : USED + 5, :] + shared_ref[USED + 5 : USED + 6, :]
    out_ref[...] = (result[:seg] * alive_ref[...]).astype(BF)
    row = lax.broadcasted_iota(jnp.int32, mem_ref.shape, 0)
    fresh = jnp.where(row < USED, result[seg + PAD :], 0.0)
    memory = jnp.where(alive_ref[...] > 0.0, fresh, keep_ref[...])
    mem_ref[...] = memory
    low_ref[:seg, :] = token_ref[...]
    low_ref[seg : seg + PAD, :] = memory.astype(BF)
    low_ref[seg + PAD :, :] = memory.astype(BF)
    attn_rows(low_ref, qk_ref, vo_ref, bias_ref, part_ref, qkv_ref, lse_ref, ctx_ref)


def ffn_forward_kernel(token_ref, mem_ref, own_ref, other_ref, up_ref, down_ref, bias_ref, shared_ref,
                       part_ref, first_ref, low_ref, act_ref, slope_ref):
    seg = token_ref.shape[0]
    hidden_units = up_ref.shape[1]
    begin = bias_ref.shape[1] - hidden_units
    attn = own_ref[...].astype(F32) + other_ref[...].astype(F32) + shared_ref[USED : USED + 1, :]
    first_ref[:seg, :] = token_ref[...].astype(F32) + attn[:seg]
    first_ref[seg : seg + PAD, :] = mem_ref[...] + attn[seg : seg + PAD]
    first_ref[seg + PAD :, :] = mem_ref[...] + attn[seg + PAD :]
    unit, unused = norm_stats(first_ref[...])
    hidden = unit * shared_ref[USED + 2 : USED + 3, :] + shared_ref[USED + 3 : USED + 4, :]
    low_ref[...] = hidden.astype(BF)

    def units(step, carry):
        for piece in range(2):
            at = pl.multiple_of(step * (2 * WIDE) + piece * WIDE, 128)
            u = dot_nn(low_ref[...], up_ref[:, pl.ds(at, WIDE)]) + bias_ref[:, pl.ds(begin + at, WIDE)]
            cdf = 0.5 + 0.5 * lax.erf(u * (0.5**0.5))
            density = jnp.exp2(u * u * (-0.5 * LOG2E)) * ((2.0 * math.pi) ** -0.5)
            active = (u * cdf).astype(BF)
            act_ref[:, pl.ds(at, WIDE)] = active
            slope_ref[:, pl.ds(at, WIDE)] = (cdf + u * density).astype(BF)
        return carry

    lax.fori_loop(0, hidden_units // (2 * WIDE), units, 0)
    part_ref[...] = dot_nt(act_ref[...], down_ref[...]).astype(BF)


def ffn_backward_rows(second, dmem, cot_ref, alive_ref, shared_ref, up_ref, down_ref, slope_ref,
                      part_ref, dsecond_ref, dlow_ref, du_ref, dbias_ref, dvec_ref):
    unit, scale = norm_stats(second)
    dy = jnp.concatenate(
        [cot_ref[...].astype(F32) * alive_ref[...], jnp.zeros((PAD, unit.shape[1]), F32), dmem * alive_ref[...]], axis=0
    )
    dsecond = norm_back(dy, shared_ref[USED + 4 : USED + 5, :], unit, scale)
    dsecond_ref[...] = dsecond
    dvec_ref[0:1, :] = row_sum(dsecond)
    dvec_ref[1:2, :] = row_sum(dy * unit)
    dvec_ref[2:3, :] = row_sum(dy)
    dvec_ref[3:, :] = jnp.zeros((dvec_ref.shape[0] - 3, unit.shape[1]), F32)
    dlow_ref[...] = dsecond.astype(BF)

    def units(step, carry):
        for piece in range(2):
            at = pl.multiple_of(step * (2 * WIDE) + piece * WIDE, 128)
            du = dot_nn(dlow_ref[...], down_ref[:, pl.ds(at, WIDE)]) * slope_ref[:, pl.ds(at, WIDE)].astype(F32)
            dbias_ref[:, pl.ds(at, WIDE)] = row_sum(du)
            du_low = du.astype(BF)
            du_ref[:, pl.ds(at, WIDE)] = du_low
        return carry

    lax.fori_loop(0, up_ref.shape[1] // (2 * WIDE), units, 0)
    part_ref[...] = dot_nt(du_ref[...], up_ref[...]).astype(BF)


def ffn_last_kernel(before, *refs):
    first_ref, own_ref, other_ref, cot_ref, dmem_ref, alive_ref, shared_ref, up_ref, down_ref, slope_ref, out_ref, *outs = refs[before:]
    for slot in range(before):
        out_ref[slot] = refs[slot][...]
    second = close_rows(first_ref, own_ref, other_ref, shared_ref)
    unit, unused = norm_stats(second)
    result = unit * shared_ref[USED + 4 : USED + 5, :] + shared_ref[USED + 5 : USED + 6, :]
    out_ref[before] = (result[: out_ref.shape[1]] * alive_ref[...]).astype(BF)
    ffn_backward_rows(second, dmem_ref[...], cot_ref, alive_ref, shared_ref, up_ref, down_ref, slope_ref, *outs)


def input_rows(dfirst_ref, own_ref, other_ref, grad_ref, here, live, keep):
    seg = grad_ref.shape[-2]
    dx = dfirst_ref[...] + (own_ref[...].astype(F32) + other_ref[...].astype(F32))
    grad_ref[here] = (dx[:seg] * live).astype(BF)
    return jnp.where(live > 0.0, dx[seg : seg + PAD] + dx[seg + PAD :], keep)


def ffn_before_kernel(dfirst_ref, own_ref, other_ref, live_ref, keep_ref, second_ref, cot_ref, alive_ref, shared_ref, up_ref, down_ref,
                      slope_ref, grad_ref, dmem_ref, *outs):
    dmem = input_rows(dfirst_ref, own_ref, other_ref, grad_ref, ..., live_ref[...], keep_ref[...])
    dmem_ref[...] = dmem
    ffn_backward_rows(second_ref[...], dmem, cot_ref, alive_ref, shared_ref, up_ref, down_ref, slope_ref, *outs)


def input_grad_kernel(dfirst_ref, own_ref, other_ref, live_ref, keep_ref, *refs):
    *later, grad_ref, dmem_ref = refs
    for slot, ref in enumerate(later):
        grad_ref[slot + 1] = ref[...]
    dmem_ref[...] = input_rows(dfirst_ref, own_ref, other_ref, grad_ref, 0, live_ref[...], keep_ref[...])


def attn_backward_kernel(dsecond_ref, own_ref, other_ref, first_ref, shared_ref, qk_ref, vo_ref, qkv_ref, lse_ref,
                         part_ref, dfirst_ref, da_ref, dqkv_ref, dhead_ref, dvec_ref, dctx_ref, lse_t_ref):
    rows = first_ref.shape[0]
    width = vo_ref.shape[1] // 2
    seg = rows - 2 * PAD
    dhidden = dsecond_ref[...] + (own_ref[...].astype(F32) + other_ref[...].astype(F32))
    unit, scale = norm_stats(first_ref[...])
    dfirst = norm_back(dhidden, shared_ref[USED + 2 : USED + 3, :], unit, scale)
    dfirst_ref[...] = dfirst
    dvec_ref[0:1, :] = row_sum(dfirst)
    dvec_ref[1:2, :] = row_sum(dhidden * unit)
    dvec_ref[2:3, :] = row_sum(dhidden)
    dvec_ref[3:, :] = jnp.zeros((dvec_ref.shape[0] - 3, unit.shape[1]), F32)
    da_ref[...] = dfirst.astype(BF)
    dctx_ref[...] = dot_nn(da_ref[...], vo_ref[:, width:]).astype(BF)
    lse_t_ref[...] = jnp.transpose(lse_ref[...])
    dead = dead_rows(rows)
    lane = lax.broadcasted_iota(jnp.int32, (rows, 128), 1)

    def heads(pair, carry):
        at = pl.multiple_of(pair * 128, 128)
        q = qkv_ref[:, pl.ds(at, 128)]
        k = qkv_ref[:, pl.ds(width + at, 128)]
        v = qkv_ref[:, pl.ds(2 * width + at, 128)]
        dc = dctx_ref[:, pl.ds(at, 128)]
        dq, dk, dv = None, None, None
        for head in range(2):
            mine = (lane < 64) if head == 0 else (lane >= 64)
            q_one = jnp.where(mine, q, jnp.zeros_like(q))
            dc_one = jnp.where(mine, dc, jnp.zeros_like(dc))
            s_t = masked_scores(q, k, mine, dead, lane, head, lambda a, b: dot_nt(b, a)) * (HD**-0.5 * LOG2E)
            lse_row = lse_t_ref[pl.ds(2 * pair + head, 1), :]
            p_t = jnp.exp2(s_t - lse_row)
            dp_t = dot_nt(v, dc_one)
            dv_one = dot_nn(p_t.astype(BF), dc_one)
            inner = row_sum(p_t * dp_t)
            ds_t = (p_t * (dp_t - inner)).astype(BF)
            dk_one = dot_nn(ds_t, q_one)
            dq_one = dot_tn(ds_t, jnp.where(mine, k, jnp.zeros_like(k)))
            dq = dq_one if dq is None else dq + dq_one
            dv = dv_one if dv is None else dv + dv_one
            dk = dk_one if dk is None else dk + dk_one
        dq = dq * (HD**-0.5)
        dk = dk * (HD**-0.5)
        dhead_ref[:, pl.ds(at, 128)] = row_sum(dq)
        dhead_ref[:, pl.ds(width + at, 128)] = row_sum(dv)
        dqkv_ref[:, pl.ds(at, 128)] = dq.astype(BF)
        dqkv_ref[:, pl.ds(width + at, 128)] = dk.astype(BF)
        dqkv_ref[:, pl.ds(2 * width + at, 128)] = dv.astype(BF)
        return carry

    lax.fori_loop(0, width // 128, heads, 0)
    part = dot_nt(dqkv_ref[:, : 2 * width], qk_ref[...]) + dot_nt(dqkv_ref[:, 2 * width :], vo_ref[:, :width])
    part_ref[...] = part.astype(BF)


def grad_close_kernel(lines, *refs):
    count = 3 * lines
    outs = refs[-4:]
    squares = None
    for matrix in range(3):
        total = refs[matrix * lines][...].astype(F32)
        for other in refs[matrix * lines + 1 : (matrix + 1) * lines]:
            total = total + other[...].astype(F32)
        outs[matrix][...] = total
        square = jnp.sum(total * total, keepdims=True)
        squares = square if squares is None else squares + square
    dmem_ref = refs[count]
    dvec_one, dvec_two, dhead, dbias = (refs[count + 1 + i : -4 : 4] for i in range(4))
    small = outs[3]
    model = small.shape[1]

    def total_of(group, row):
        total = group[0][row : row + 1, :]
        for ref in group[1:]:
            total = total + ref[row : row + 1, :]
        return total

    small[:PAD, :] = dmem_ref[...]
    for place, (group, row) in enumerate(((dvec_one, 0), (dvec_two, 0), (dvec_one, 1), (dvec_one, 2), (dvec_two, 1), (dvec_two, 2))):
        small[USED + place : USED + place + 1, :] = total_of(group, row)
    at = USED + 6
    for group in (dhead, dbias):
        whole = total_of(group, 0)
        for piece in range(whole.shape[1] // model):
            small[at : at + 1, :] = whole[:, piece * model : (piece + 1) * model]
            at += 1
    small[at:, :] = jnp.broadcast_to(squares, (small.shape[0] - at, model))


def adam_kernel(plan, small_ref, other_ref, *refs):
    count = len(plan)
    grads = refs[:3]
    olds, news = refs[3 : 3 + 3 * count], refs[4 + 3 * count :]
    norm_ref = refs[3 + 3 * count]
    shared = small_ref[: USED + 6, :]
    halves = []
    for ref in (small_ref, other_ref):
        biases = ref[USED + 6 : USED + 9, :]
        halves.append(ref[USED + 9 : USED + 10, :1] + jnp.sum(biases * biases, keepdims=True))
    norm = jnp.sqrt((halves[0] + halves[1]) + jnp.sum(shared * shared, keepdims=True))
    norm_ref[...] = norm
    factor = CLIP_NORM / jnp.maximum(norm, CLIP_NORM)
    for number, (source, row, column, rate, decay) in enumerate(plan):
        weight_ref, first_ref, second_ref = olds[3 * number : 3 * number + 3]
        height, length = weight_ref.shape[-2:]
        for index in range(math.prod(weight_ref.shape[:-2])):
            here = (index,) if weight_ref.ndim == 3 else ()
            if source is None and height == 1:
                model = small_ref.shape[1]
                gradient = jnp.concatenate([small_ref[row + i : row + i + 1, :] for i in range(length // model)], axis=1)
            elif source is None:
                gradient = small_ref[row : row + height, :]
            else:
                gradient = grads[source][:, column + index * length : column + (index + 1) * length]
            clipped = gradient * factor
            first = BETA_ONE * first_ref[here + (...,)] + (1.0 - BETA_ONE) * clipped
            second = BETA_TWO * second_ref[here + (...,)] + (1.0 - BETA_TWO) * clipped * clipped
            first_hat = first / (1.0 - BETA_ONE**STEP)
            second_hat = second / (1.0 - BETA_TWO**STEP)
            weight = weight_ref[here + (...,)]
            news[3 * number][here + (...,)] = weight - rate * (first_hat / (jnp.sqrt(second_hat) + ADAM_EPSILON) + decay * weight)
            news[3 * number + 1][here + (...,)] = first
            news[3 * number + 2][here + (...,)] = second


def weight_start_kernel(left_ref, right_ref, total_ref):
    def rows_of(step, carry):
        begin = pl.multiple_of(step * CHUNK, CHUNK)
        total_ref[pl.ds(begin, CHUNK), :] = dot_tn(left_ref[:, pl.ds(begin, CHUNK)], right_ref[...])
        return carry

    lax.fori_loop(0, total_ref.shape[0] // CHUNK, rows_of, 0)


def weight_grad_kernel(plan, kinds, sizes, base, me_ref, *refs):
    count = len(kinds) * len(sizes)
    outs = refs[-count - 1 : -1]
    total_ref = refs[-1]
    block = total_ref.shape[0] // SLOTS
    for part, (kind, pieces) in enumerate(zip(kinds, plan)):
        at = 0
        for left, right, start, size in pieces:

            def rows_of(step, carry, left=left, right=right, start=start, size=size, at=at):
                begin = pl.multiple_of(step * CHUNK, CHUNK)
                total = None if base is None else refs[base][pl.ds(begin, CHUNK), start : start + size]
                for one, two in zip(left, right):
                    add = dot_tn(refs[one][:, pl.ds(begin, CHUNK)], refs[two][:, start : start + size])
                    total = add if total is None else total + add
                total_ref[pl.ds(begin, CHUNK), at : at + size] = total
                return carry

            lax.fori_loop(0, total_ref.shape[0] // CHUNK, rows_of, 0)
            at += size
        number = 0
        for target in outs[part * len(sizes) : (part + 1) * len(sizes)]:
            for inner in range(target.shape[0]):
                place = lax.bitwise_xor(me_ref[0], slot_of(kind, number))
                begin = pl.multiple_of(place * block, block)
                target[inner] = total_ref[pl.ds(begin, block), :].astype(BF)
                number += 1


def exchange(values, axis, size, flip):
    return lax.ppermute(values, axis, [(i, i ^ flip) for i in range(size)])


def after(value, *others):
    return lax.optimization_barrier((value, *others))[0]


def add_low(*values):
    total = values[0].astype(F32)
    for value in values[1:]:
        total = total + value.astype(F32)
    return total


def canonical_split(full, kind, sizes):
    full = full.reshape(SLOTS, full.shape[0] // SLOTS, full.shape[1])
    full = jnp.stack([full[slot_of(kind, number)] for number in range(SLOTS)])
    ends = [sum(sizes[: i + 1]) for i in range(len(sizes))]
    return [full[end - size : end] for end, size in zip(ends, sizes)]


def canonical_join(pieces, kind):
    full = jnp.concatenate(pieces)
    order = [slot_of(kind, number) for number in range(SLOTS)]
    full = jnp.stack([full[order.index(d)] for d in range(SLOTS)])
    return full.reshape(-1, full.shape[-1])


def line_stage(own, size):
    return [own] + [exchange(own, "dp", size, 4 * j) for j in (1, 2, 3)]


def sum_all(values, axis, size):
    if size & (size - 1):
        return lax.psum(values, axis)
    flip = 1
    while flip < size:
        if flip * 4 <= size:
            near, far, both = [exchange(values, axis, size, flip * j) for j in (1, 2, 3)]
            values = (values + near) + (far + both)
            flip *= 4
        else:
            values = values + exchange(values, axis, size, flip)
            flip *= 2
    return values


def shards(
    size,
    pair,
    inputs,
    cotangent,
    seg_counts,
    qkv_weight,
    out_weight,
    up_weight,
    down_weight,
    head_bias,
    shared_params,
    qkv_first,
    out_first,
    up_first,
    down_first,
    bias_first,
    shared_first,
    qkv_second,
    out_second,
    up_second,
    down_second,
    bias_second,
    shared_second,
):
    unused, segments, seg, model = inputs.shape
    width = qkv_weight.shape[2]
    hidden = up_weight.shape[1]
    used = shared_params.shape[0] - 6
    pad = 16
    rows = seg + 2 * pad
    half = hidden // 2

    me = (lax.axis_index("dp") if size == SLOTS else jnp.int32(0)).astype(jnp.int32).reshape(1)
    block = qkv_weight.shape[1]
    (own_qkvo,) = call(own_first_kernel, [((2, block, 2 * width), BF)], [qkv_weight, out_weight.T])
    own_up, *own_down = call(
        own_next_kernel,
        [((2, block, half), BF), ((block, half), BF), ((block, half), BF)],
        [up_weight, down_weight.T],
    )
    own = [own_qkvo, own_up, own_down]

    def assembled(kinds, pieces, joined):
        return call(
            functools.partial(assemble_kernel, kinds, [len(p) for p in pieces], joined),
            [((model, 2 * model), BF)] if joined else [((model, model), BF)] * 2,
            [me, *pieces[0], *pieces[1]],
            scalars=1,
        )

    z_first, z_mid = ("za", "zb"), ("xa", "xb")
    if size == SLOTS:

        def spread(lines):
            low_a = jnp.concatenate([lines[0], exchange(lines[0], "dp", size, 2)])
            low_b = jnp.concatenate([lines[1], exchange(lines[1], "dp", size, 1)])
            return low_a, low_b

        def finish(low_a, low_b):
            return exchange(low_a, "dp", size, 1), exchange(low_b, "dp", size, 2)

        pair_c = [jnp.stack([own[2][i], exchange(own[2][i], "dp", size, 1 + i)]) for i in range(2)]
        line_one = line_stage(own[0], size)
        line_two = line_stage(after(own[1], *line_one), size)
        low_one = spread(call(line_kernel, [((4, *line_one[0].shape[1:]), BF)] * 2, line_one))
        line_three = line_stage(after(jnp.stack(pair_c), *line_two, *low_one), size)
        high_one = finish(*low_one)
        low_two = spread([after(jnp.stack([v[i] for v in line_two]), *high_one) for i in range(2)])
        high_two = finish(*low_two)
        low_c = [jnp.concatenate([v[i] for v in line_three]) for i in range(2)]
        low_c = [after(v, *high_two) for v in low_c]
        high_c = [exchange(low_c[i], "dp", size, 2 - i) for i in range(2)]
        w_qk, w_vo = assembled(z_first, [[low_one[i], high_one[i]] for i in range(2)], False)
        (w_up,) = assembled(z_first, [[low_two[i], high_two[i]] for i in range(2)], True)
        (w_down,) = assembled(z_mid, [[low_c[i], high_c[i]] for i in range(2)], True)
    else:

        def whole(number, kinds, sizes):
            pieces = [lax.all_gather(own[number][i], "dp", axis=0, tiled=True) for i in range(2)]
            return assembled(kinds, [canonical_split(p, kind, sizes) for p, kind in zip(pieces, kinds)], number > 0)

        w_qk, w_vo = whole(0, z_first, (8, 8))
        (w_up,) = whole(1, z_first, (8, 8))
        (w_down,) = whole(2, z_mid, (8, 8))

    memory = jnp.concatenate([shared_params[:used], jnp.zeros((pad - used, model), F32)], axis=0)
    alive = [(slot < seg_counts).astype(F32).reshape(1, 1) for slot in range(segments)]
    memories, tokens_out, saved = [memory], [], []
    attn_outs = [((rows, model), BF), ((rows, model), BF), ((rows, 3 * width), BF), ((rows, 128), F32), ((rows, width), BF)]
    for slot in range(segments):
        tokens = inputs[0, slot]
        if slot == 0:
            part, *attn = call(attn_forward_kernel, attn_outs, [tokens, memory, w_qk, w_vo, head_bias])
        else:
            out_rows, memory, second_in, part, *attn = call(
                attn_next_kernel,
                [((seg, model), BF), ((pad, model), F32), ((rows, model), F32)] + attn_outs,
                [saved[-1][4], ffn_part, other, shared_params, alive[slot - 1], memory, tokens, w_qk, w_vo, head_bias],
            )
            tokens_out.append(out_rows)
            saved[-1] += (second_in,)
        other = exchange(part, "head", pair, 1)
        ffn_part, first_in, h_low, active, slope = call(
            ffn_forward_kernel,
            [((rows, model), BF), ((rows, model), F32), ((rows, model), BF), ((rows, hidden), BF), ((rows, hidden), BF)],
            [tokens, memory, part, other, w_up, w_down, head_bias, shared_params],
        )
        other = exchange(ffn_part, "head", pair, 1)
        saved.append((*attn, first_in, h_low, active, slope))

    count = segments

    def weight_grad(names, plan, kinds, base=None):
        sizes = (8, 8)
        slots = range(count) if base is None else (0,)
        operands = [stacks[s][n] for n in names for s in slots]
        at = {n: [i * len(slots) + j for j in range(len(slots))] for i, n in enumerate(names)}
        steps = [[(at[a], at[b], start, length) for a, b, start, length in pieces] for pieces in plan]
        result = call(
            functools.partial(weight_grad_kernel, steps, kinds, sizes, None if base is None else len(operands)),
            [((length, model // SLOTS, model), BF) for kind in kinds for length in sizes],
            [me, *operands] + ([] if base is None else [base]),
            scalars=1,
            scratch=[pltpu.VMEM((model, model), F32)],
        )
        return result[: len(sizes)], result[len(sizes) :]

    dmem = jnp.zeros((pad, model), F32)
    grads = [None] * segments
    stacks = [None] * segments
    smalls, base = [], None
    ffn_outs = [((rows, model), BF), ((rows, model), F32), ((rows, model), BF), ((rows, hidden), BF), ((1, hidden), F32), ((8, model), F32)]
    for slot in reversed(range(segments)):
        low, qkv, lse, ctx, first_in, h_low, active, slope = saved[slot][:8]
        weights = [alive[slot], shared_params, w_up, w_down, slope]
        if slot == segments - 1:
            outputs, part, dsecond, df_low, du, dbias, dvec_two = call(
                functools.partial(ffn_last_kernel, slot),
                [((segments, seg, model), BF)] + ffn_outs,
                [*tokens_out, first_in, ffn_part, other, cotangent[0, slot], dmem, *weights],
            )
        else:
            grads[slot + 1], dmem, part, dsecond, df_low, du, dbias, dvec_two = call(
                ffn_before_kernel,
                [((seg, model), BF), ((pad, model), F32)] + ffn_outs,
                [dfirst, part, other, alive[slot + 1], dmem, saved[slot][8], cotangent[0, slot], *weights],
            )
        other = exchange(part, "head", pair, 1)
        stacks[slot] = (low, ctx, h_low, active, df_low, du)
        if slot == 0:
            dw_down = weight_grad((DF_LOW, ACTIVE), [[(DF_LOW, ACTIVE, 0, half)], [(DF_LOW, ACTIVE, half, half)]], z_first, base)
            dw_up = weight_grad((H_LOW, DU), [[(H_LOW, DU, 0, half)], [(H_LOW, DU, half, half)]], z_first)
            dsecond = after(dsecond, dw_down[0][0], dw_up[0][0])
        elif segments == 2:
            (base,) = call(weight_start_kernel, [((model, hidden), F32)], [df_low, active])
            dsecond = after(dsecond, base)
        part, dfirst, da, dqkv, dhead, dvec_one = call(
            attn_backward_kernel,
            [((rows, model), BF), ((rows, model), F32), ((rows, model), BF), ((rows, 3 * width), BF), ((1, 2 * width), F32), ((8, model), F32)],
            [dsecond, part, other, first_in, shared_params, w_qk, w_vo, qkv, lse],
            scratch=[pltpu.VMEM((rows, width), BF), pltpu.VMEM((128, rows), F32)],
        )
        other = exchange(part, "head", pair, 1)
        stacks[slot] += (da, dqkv)
        smalls += [dvec_one, dvec_two, dhead, dbias]
    input_grad, dmem = call(
        input_grad_kernel,
        [((segments, seg, model), BF), ((pad, model), F32)],
        [dfirst, part, other, alive[0], dmem, *grads[1:]],
    )

    def fallback(parts, kinds):
        full = [canonical_join(p, kind) for p, kind in zip(parts, kinds)]
        full = jnp.concatenate(full, axis=1)
        return lax.psum_scatter(full, "dp", scatter_dimension=0, tiled=True).astype(F32)

    def hop(blocks, flips):
        return [exchange(block, "dp", size, flip) for block, flip in zip(blocks, flips)]

    def add_halves(keep, got):
        return [add_low(k, g).astype(BF) for k, g in zip(keep, got)]

    def line_hop(four):
        return [exchange(four[j], "dp", size, 4 * j) for j in (1, 2, 3)]

    x_first, y_first = (1, 2), (2, 1)
    if size == SLOTS:
        got_down, got_up = hop([p[1] for p in dw_down], x_first), hop([p[1] for p in dw_up], x_first)
        down = add_halves([p[0] for p in dw_down], [after(g, stacks[0][DQKV]) for g in got_down])
        got_down = hop([v[4:] for v in down], y_first)
        up = add_halves([p[0] for p in dw_up], [after(g, *down) for g in got_up])
        stacks[0] = stacks[0][:DQKV] + (after(stacks[0][DQKV], *up),)
        got_up = hop([v[4:] for v in up], y_first)
    dw_qkvo = weight_grad(
        (LOW, DQKV, DA, CTX),
        [[(LOW, DQKV, 0, 2 * width)], [(LOW, DQKV, 2 * width, width), (DA, CTX, 0, width)]],
        z_first,
    )
    if size == SLOTS:
        got_down = [after(g, dw_qkvo[0][0]) for g in got_down]
        down = jnp.concatenate(add_halves([v[:4] for v in down], got_down), axis=2)
        got_down = line_hop(down)
        dw_qkvo = [[after(v, *got_up) for v in part] for part in dw_qkvo]
        got_qkvo = hop([p[1] for p in dw_qkvo], x_first)
        up = jnp.concatenate(add_halves([v[:4] for v in up], got_up), axis=2)
        got_up = line_hop(up)
        last = add_halves([p[0] for p in dw_qkvo], [after(g, *got_down, *got_up) for g in got_qkvo])
        got_qkvo = hop([v[4:] for v in last], y_first)
        last = jnp.concatenate(add_halves([v[:4] for v in last], got_qkvo), axis=2)
        sums = [[down[0], *got_down], [up[0], *got_up], [last[0], *line_hop(last)]]
    else:
        sums = [[fallback(p, z_first)] for p in (dw_down, dw_up, dw_qkvo)]
    height, wide = sums[0][0].shape
    *matrices, small = call(
        functools.partial(grad_close_kernel, len(sums[0])),
        [((height, wide), F32)] * 3 + [((24, model), F32)],
        [*sums[0], *sums[1], *sums[2], dmem, *smalls],
    )
    small = sum_all(small, "dp", size)
    other = exchange(small, "head", pair, 1)
    plan = (
        (2, 0, 0, LEARN_RATE, DECAY_RATE),
        (2, 0, 3 * width, LEARN_RATE, DECAY_RATE),
        (1, 0, 0, LEARN_RATE, DECAY_RATE),
        (0, 0, 0, LEARN_RATE, DECAY_RATE),
        (None, used + 6, 0, VECTOR_RATE, 0.0),
        (None, 0, 0, VECTOR_RATE, 0.0),
    )
    olds = (
        (qkv_weight, qkv_first, qkv_second),
        (out_weight.T, out_first.T, out_second.T),
        (up_weight, up_first, up_second),
        (down_weight.T, down_first.T, down_second.T),
        (head_bias, bias_first, bias_second),
        (shared_params, shared_first, shared_second),
    )
    grad_norm, *news = call(
        functools.partial(adam_kernel, plan),
        [((1, 1), F32)] + [(o.shape, F32) for old in olds for o in old],
        [small, other, *matrices, *[o for old in olds for o in old]],
    )
    results = [news[3 * i : 3 * i + 3] for i in range(6)]
    for number in (1, 3):
        results[number] = [r.T for r in results[number]]
    return (outputs[None], input_grad[None], grad_norm[0, 0]) + tuple(r[i] for i in range(3) for r in results)


def solution(mesh):
    weights = (P(None, "dp", "head"), P("head", "dp"), P("dp", "head"), P("head", "dp"), P("head", None), P())
    rows = P("dp", None, None, None)
    return jax.shard_map(
        functools.partial(shards, mesh.shape["dp"], mesh.shape["head"]),
        mesh=mesh,
        in_specs=(rows, rows, P("dp")) + weights * 3,
        out_specs=(rows, rows, P()) + weights * 3,
        check_vma=False,
    )
```

```python
import functools
import math

import jax
import jax.numpy as jnp
from jax import lax
from jax.experimental import pallas as pl
from jax.experimental.pallas import tpu as pltpu
from jax.sharding import PartitionSpec as P

HD = 64
STEP = 10
EPSILON = 1e-06
BETA_ONE = 0.9
BETA_TWO = 0.999
LEARN_RATE = 0.1
VECTOR_RATE = 0.6
DECAY_RATE = 0.01
ADAM_EPSILON = 1e-08
CLIP_NORM = 1.0

BF = jnp.bfloat16
F32 = jnp.float32
LOG2E = math.log2(math.e)
NEG = -1e30
SLOTS = 16
PAD = 16
USED = 10
WIDE = 256
CHUNK = 256
LOW, CTX, H_LOW, ACTIVE, DF_LOW, DU, DA, DQKV = range(8)


def dot_nn(a, b):
    return lax.dot_general(a, b, (((1,), (0,)), ((), ())), preferred_element_type=F32)


def dot_nt(a, b):
    return lax.dot_general(a, b, (((1,), (1,)), ((), ())), preferred_element_type=F32)


def dot_tn(a, b):
    return lax.dot_general(a, b, (((0,), (0,)), ((), ())), preferred_element_type=F32)


def norm_stats(values):
    average = jnp.mean(values, axis=-1, keepdims=True)
    centered = values - average
    variance = jnp.mean(centered * centered, axis=-1, keepdims=True)
    scale = lax.rsqrt(variance + EPSILON)
    return centered * scale, scale


def norm_back(grad, gain, unit, scale):
    inner = grad * gain
    mean_one = jnp.mean(inner, axis=-1, keepdims=True)
    mean_two = jnp.mean(inner * unit, axis=-1, keepdims=True)
    return scale * (inner - mean_one - unit * mean_two)


def row_sum(values):
    return jnp.sum(values, axis=0, keepdims=True)


def call(kernel, outs, args, scalars=0, scratch=()):
    return pl.pallas_call(
        kernel,
        out_shape=[jax.ShapeDtypeStruct(s, d) for s, d in outs],
        in_specs=[pl.BlockSpec(memory_space=pltpu.SMEM)] * scalars
        + [pl.BlockSpec(memory_space=pltpu.VMEM)] * (len(args) - scalars),
        out_specs=[pl.BlockSpec(memory_space=pltpu.VMEM)] * len(outs),
        scratch_shapes=list(scratch),
        cost_estimate=pl.CostEstimate(flops=0, bytes_accessed=0, transcendentals=0),
        compiler_params=pltpu.CompilerParams(vmem_limit_bytes=16 << 20),
    )(*args)


def slot_of(kind, number):
    if kind[0] == "z":
        outer, mid, z = number // 8, number // 4 % 2, number % 4
        return (outer + 2 * mid if kind[1] == "a" else 2 * outer + mid) + 4 * z
    outer, z, inner = number // 8, number // 2 % 4, number % 2
    return (2 * outer + inner if kind[1] == "a" else outer + 2 * inner) + 4 * z


def own_first_kernel(qkv_ref, out_ref, own_ref):
    width = out_ref.shape[1]
    for part in range(2):
        own_ref[part, :, :width] = qkv_ref[2 * part].astype(BF)
    own_ref[0, :, width:] = qkv_ref[1].astype(BF)
    own_ref[1, :, width:] = out_ref[...].astype(BF)


def own_next_kernel(up_ref, down_ref, up_own_ref, *down_own_refs):
    half = up_ref.shape[1] // 2
    for part in range(2):
        up_own_ref[part] = up_ref[:, part * half : (part + 1) * half].astype(BF)
        down_own_refs[part][...] = down_ref[:, part * half : (part + 1) * half].astype(BF)


def line_kernel(*refs):
    for part, target in enumerate(refs[4:]):
        for place, source in enumerate(refs[:4]):
            target[place] = source[part]


def assemble_kernel(kinds, counts, joined, me_ref, *refs):
    at = sum(counts)
    begin = 0
    for part, (kind, count) in enumerate(zip(kinds, counts)):
        target = refs[at] if joined else refs[at + part]
        block = target.shape[0] // SLOTS
        number = 0
        for source in refs[begin : begin + count]:
            length = source.shape[2]
            column = part * length if joined else 0
            for inner in range(source.shape[0]):
                place = lax.bitwise_xor(me_ref[0], slot_of(kind, number))
                start = pl.multiple_of(place * block, block)
                target[pl.ds(start, block), column : column + length] = source[inner]
                number += 1
        begin += count


def dead_rows(rows):
    at = lax.broadcasted_iota(jnp.int32, (rows, 128), 0) - (rows - 2 * PAD)
    return (at >= 0) & ((at & (PAD - 1)) >= USED)


def masked_scores(q, k, mine, dead, lane, head, dot):
    spare = lane == (127 if head == 0 else 0)
    zero = jnp.zeros_like(q)
    q_one = jnp.where(spare, jnp.ones_like(q), jnp.where(mine, q, zero))
    k_one = jnp.where(spare, jnp.where(dead, jnp.full_like(k, NEG), zero), k)
    return dot(q_one, k_one)


def attn_rows(low_ref, qk_ref, vo_ref, bias_ref, part_ref, qkv_ref, lse_ref, ctx_ref):
    rows = low_ref.shape[0]
    width = vo_ref.shape[1] // 2
    seg = rows - 2 * PAD
    low = low_ref[...]
    qk = dot_nn(low, qk_ref[...])
    qkv_ref[:, :width] = (qk[:, :width] + bias_ref[:, :width]).astype(BF)
    qkv_ref[:, width : 2 * width] = qk[:, width:].astype(BF)
    v_all = dot_nn(low, vo_ref[:, :width])
    qkv_ref[:, 2 * width :] = (v_all + bias_ref[:, width : 2 * width]).astype(BF)
    lane = lax.broadcasted_iota(jnp.int32, (rows, 128), 1)
    lse_ref[...] = jnp.zeros_like(lse_ref)
    dead = dead_rows(rows)

    def heads(pair, carry):
        at = pl.multiple_of(pair * 128, 128)
        q = qkv_ref[:, pl.ds(at, 128)]
        k = qkv_ref[:, pl.ds(width + at, 128)]
        v = qkv_ref[:, pl.ds(2 * width + at, 128)]
        outs = []
        for head in range(2):
            mine = (lane < 64) if head == 0 else (lane >= 64)
            s = masked_scores(q, k, mine, dead, lane, head, dot_nt) * (HD**-0.5 * LOG2E)
            top = jnp.max(s, axis=1, keepdims=True)
            e = jnp.exp2(s - top)
            total = jnp.sum(e, axis=1, keepdims=True)
            outs.append(dot_nn(e.astype(BF), v) * (1.0 / total))
            lse_ref[...] = jnp.where(lane == 2 * pair + head, top + jnp.log2(total), lse_ref[...])
        ctx_ref[:, pl.ds(at, 128)] = jnp.where(lane < 64, outs[0], outs[1]).astype(BF)
        return carry

    lax.fori_loop(0, width // 128, heads, 0)
    part_ref[...] = dot_nt(ctx_ref[...], vo_ref[:, width:]).astype(BF)


def attn_forward_kernel(token_ref, mem_ref, qk_ref, vo_ref, bias_ref, part_ref, low_ref, qkv_ref, lse_ref, ctx_ref):
    seg = token_ref.shape[0]
    memory = mem_ref[...].astype(BF)
    low_ref[:seg, :] = token_ref[...]
    low_ref[seg : seg + PAD, :] = memory
    low_ref[seg + PAD :, :] = memory
    attn_rows(low_ref, qk_ref, vo_ref, bias_ref, part_ref, qkv_ref, lse_ref, ctx_ref)


def close_rows(first_ref, own_ref, other_ref, shared_ref):
    unit, unused = norm_stats(first_ref[...])
    hidden = unit * shared_ref[USED + 2 : USED + 3, :] + shared_ref[USED + 3 : USED + 4, :]
    return hidden + (own_ref[...].astype(F32) + other_ref[...].astype(F32)) + shared_ref[USED + 1 : USED + 2, :]


def attn_next_kernel(first_ref, own_ref, other_ref, shared_ref, alive_ref, keep_ref, token_ref, qk_ref, vo_ref, bias_ref,
                     out_ref, mem_ref, second_ref, part_ref, low_ref, qkv_ref, lse_ref, ctx_ref):
    seg = token_ref.shape[0]
    second = close_rows(first_ref, own_ref, other_ref, shared_ref)
    second_ref[...] = second
    unit, unused = norm_stats(second)
    result = unit * shared_ref[USED + 4 : USED + 5, :] + shared_ref[USED + 5 : USED + 6, :]
    out_ref[...] = (result[:seg] * alive_ref[...]).astype(BF)
    row = lax.broadcasted_iota(jnp.int32, mem_ref.shape, 0)
    fresh = jnp.where(row < USED, result[seg + PAD :], 0.0)
    memory = jnp.where(alive_ref[...] > 0.0, fresh, keep_ref[...])
    mem_ref[...] = memory
    low_ref[:seg, :] = token_ref[...]
    low_ref[seg : seg + PAD, :] = memory.astype(BF)
    low_ref[seg + PAD :, :] = memory.astype(BF)
    attn_rows(low_ref, qk_ref, vo_ref, bias_ref, part_ref, qkv_ref, lse_ref, ctx_ref)


def ffn_forward_kernel(token_ref, mem_ref, own_ref, other_ref, up_ref, down_ref, bias_ref, shared_ref,
                       part_ref, first_ref, low_ref, act_ref, slope_ref):
    seg = token_ref.shape[0]
    hidden_units = up_ref.shape[1]
    begin = bias_ref.shape[1] - hidden_units
    attn = own_ref[...].astype(F32) + other_ref[...].astype(F32) + shared_ref[USED : USED + 1, :]
    first_ref[:seg, :] = token_ref[...].astype(F32) + attn[:seg]
    first_ref[seg : seg + PAD, :] = mem_ref[...] + attn[seg : seg + PAD]
    first_ref[seg + PAD :, :] = mem_ref[...] + attn[seg + PAD :]
    unit, unused = norm_stats(first_ref[...])
    hidden = unit * shared_ref[USED + 2 : USED + 3, :] + shared_ref[USED + 3 : USED + 4, :]
    low_ref[...] = hidden.astype(BF)

    def units(step, carry):
        for piece in range(2):
            at = pl.multiple_of(step * (2 * WIDE) + piece * WIDE, 128)
            u = dot_nn(low_ref[...], up_ref[:, pl.ds(at, WIDE)]) + bias_ref[:, pl.ds(begin + at, WIDE)]
            cdf = 0.5 + 0.5 * lax.erf(u * (0.5**0.5))
            density = jnp.exp2(u * u * (-0.5 * LOG2E)) * ((2.0 * math.pi) ** -0.5)
            active = (u * cdf).astype(BF)
            act_ref[:, pl.ds(at, WIDE)] = active
            slope_ref[:, pl.ds(at, WIDE)] = (cdf + u * density).astype(BF)
        return carry

    lax.fori_loop(0, hidden_units // (2 * WIDE), units, 0)
    part_ref[...] = dot_nt(act_ref[...], down_ref[...]).astype(BF)


def ffn_backward_rows(second, dmem, cot_ref, alive_ref, shared_ref, up_ref, down_ref, slope_ref,
                      part_ref, dsecond_ref, dlow_ref, du_ref, dbias_ref, dvec_ref):
    unit, scale = norm_stats(second)
    dy = jnp.concatenate(
        [cot_ref[...].astype(F32) * alive_ref[...], jnp.zeros((PAD, unit.shape[1]), F32), dmem * alive_ref[...]], axis=0
    )
    dsecond = norm_back(dy, shared_ref[USED + 4 : USED + 5, :], unit, scale)
    dsecond_ref[...] = dsecond
    dvec_ref[0:1, :] = row_sum(dsecond)
    dvec_ref[1:2, :] = row_sum(dy * unit)
    dvec_ref[2:3, :] = row_sum(dy)
    dvec_ref[3:, :] = jnp.zeros((dvec_ref.shape[0] - 3, unit.shape[1]), F32)
    dlow_ref[...] = dsecond.astype(BF)

    def units(step, carry):
        for piece in range(2):
            at = pl.multiple_of(step * (2 * WIDE) + piece * WIDE, 128)
            du = dot_nn(dlow_ref[...], down_ref[:, pl.ds(at, WIDE)]) * slope_ref[:, pl.ds(at, WIDE)].astype(F32)
            dbias_ref[:, pl.ds(at, WIDE)] = row_sum(du)
            du_low = du.astype(BF)
            du_ref[:, pl.ds(at, WIDE)] = du_low
        return carry

    lax.fori_loop(0, up_ref.shape[1] // (2 * WIDE), units, 0)
    part_ref[...] = dot_nt(du_ref[...], up_ref[...]).astype(BF)


def ffn_last_kernel(before, *refs):
    first_ref, own_ref, other_ref, cot_ref, dmem_ref, alive_ref, shared_ref, up_ref, down_ref, slope_ref, out_ref, *outs = refs[before:]
    for slot in range(before):
        out_ref[slot] = refs[slot][...]
    second = close_rows(first_ref, own_ref, other_ref, shared_ref)
    unit, unused = norm_stats(second)
    result = unit * shared_ref[USED + 4 : USED + 5, :] + shared_ref[USED + 5 : USED + 6, :]
    out_ref[before] = (result[: out_ref.shape[1]] * alive_ref[...]).astype(BF)
    ffn_backward_rows(second, dmem_ref[...], cot_ref, alive_ref, shared_ref, up_ref, down_ref, slope_ref, *outs)


def input_rows(dfirst_ref, own_ref, other_ref, grad_ref, here, live, keep):
    seg = grad_ref.shape[-2]
    dx = dfirst_ref[...] + (own_ref[...].astype(F32) + other_ref[...].astype(F32))
    grad_ref[here] = (dx[:seg] * live).astype(BF)
    return jnp.where(live > 0.0, dx[seg : seg + PAD] + dx[seg + PAD :], keep)


def ffn_before_kernel(dfirst_ref, own_ref, other_ref, live_ref, keep_ref, second_ref, cot_ref, alive_ref, shared_ref, up_ref, down_ref,
                      slope_ref, grad_ref, dmem_ref, *outs):
    dmem = input_rows(dfirst_ref, own_ref, other_ref, grad_ref, ..., live_ref[...], keep_ref[...])
    dmem_ref[...] = dmem
    ffn_backward_rows(second_ref[...], dmem, cot_ref, alive_ref, shared_ref, up_ref, down_ref, slope_ref, *outs)


def input_grad_kernel(dfirst_ref, own_ref, other_ref, live_ref, keep_ref, *refs):
    *later, grad_ref, dmem_ref = refs
    for slot, ref in enumerate(later):
        grad_ref[slot + 1] = ref[...]
    dmem_ref[...] = input_rows(dfirst_ref, own_ref, other_ref, grad_ref, 0, live_ref[...], keep_ref[...])


def attn_backward_kernel(dsecond_ref, own_ref, other_ref, first_ref, shared_ref, qk_ref, vo_ref, qkv_ref, lse_ref,
                         part_ref, dfirst_ref, da_ref, dqkv_ref, dhead_ref, dvec_ref, dctx_ref, lse_t_ref):
    rows = first_ref.shape[0]
    width = vo_ref.shape[1] // 2
    seg = rows - 2 * PAD
    dhidden = dsecond_ref[...] + (own_ref[...].astype(F32) + other_ref[...].astype(F32))
    unit, scale = norm_stats(first_ref[...])
    dfirst = norm_back(dhidden, shared_ref[USED + 2 : USED + 3, :], unit, scale)
    dfirst_ref[...] = dfirst
    dvec_ref[0:1, :] = row_sum(dfirst)
    dvec_ref[1:2, :] = row_sum(dhidden * unit)
    dvec_ref[2:3, :] = row_sum(dhidden)
    dvec_ref[3:, :] = jnp.zeros((dvec_ref.shape[0] - 3, unit.shape[1]), F32)
    da_ref[...] = dfirst.astype(BF)
    dctx_ref[...] = dot_nn(da_ref[...], vo_ref[:, width:]).astype(BF)
    lse_t_ref[...] = jnp.transpose(lse_ref[...])
    dead = dead_rows(rows)
    lane = lax.broadcasted_iota(jnp.int32, (rows, 128), 1)

    def heads(pair, carry):
        at = pl.multiple_of(pair * 128, 128)
        q = qkv_ref[:, pl.ds(at, 128)]
        k = qkv_ref[:, pl.ds(width + at, 128)]
        v = qkv_ref[:, pl.ds(2 * width + at, 128)]
        dc = dctx_ref[:, pl.ds(at, 128)]
        dq, dk, dv = None, None, None
        for head in range(2):
            mine = (lane < 64) if head == 0 else (lane >= 64)
            q_one = jnp.where(mine, q, jnp.zeros_like(q))
            dc_one = jnp.where(mine, dc, jnp.zeros_like(dc))
            s_t = masked_scores(q, k, mine, dead, lane, head, lambda a, b: dot_nt(b, a)) * (HD**-0.5 * LOG2E)
            lse_row = lse_t_ref[pl.ds(2 * pair + head, 1), :]
            p_t = jnp.exp2(s_t - lse_row)
            dp_t = dot_nt(v, dc_one)
            dv_one = dot_nn(p_t.astype(BF), dc_one)
            inner = row_sum(p_t * dp_t)
            ds_t = (p_t * (dp_t - inner)).astype(BF)
            dk_one = dot_nn(ds_t, q_one)
            dq_one = dot_tn(ds_t, jnp.where(mine, k, jnp.zeros_like(k)))
            dq = dq_one if dq is None else dq + dq_one
            dv = dv_one if dv is None else dv + dv_one
            dk = dk_one if dk is None else dk + dk_one
        dq = dq * (HD**-0.5)
        dk = dk * (HD**-0.5)
        dhead_ref[:, pl.ds(at, 128)] = row_sum(dq)
        dhead_ref[:, pl.ds(width + at, 128)] = row_sum(dv)
        dqkv_ref[:, pl.ds(at, 128)] = dq.astype(BF)
        dqkv_ref[:, pl.ds(width + at, 128)] = dk.astype(BF)
        dqkv_ref[:, pl.ds(2 * width + at, 128)] = dv.astype(BF)
        return carry

    lax.fori_loop(0, width // 128, heads, 0)
    part = dot_nt(dqkv_ref[:, : 2 * width], qk_ref[...]) + dot_nt(dqkv_ref[:, 2 * width :], vo_ref[:, :width])
    part_ref[...] = part.astype(BF)


def grad_close_kernel(lines, *refs):
    count = 3 * lines
    outs = refs[-4:]
    squares = None
    for matrix in range(3):
        total = refs[matrix * lines][...].astype(F32)
        for other in refs[matrix * lines + 1 : (matrix + 1) * lines]:
            total = total + other[...].astype(F32)
        outs[matrix][...] = total
        square = jnp.sum(total * total, keepdims=True)
        squares = square if squares is None else squares + square
    dmem_ref = refs[count]
    dvec_one, dvec_two, dhead, dbias = (refs[count + 1 + i : -4 : 4] for i in range(4))
    small = outs[3]
    model = small.shape[1]

    def total_of(group, row):
        total = group[0][row : row + 1, :]
        for ref in group[1:]:
            total = total + ref[row : row + 1, :]
        return total

    small[:PAD, :] = dmem_ref[...]
    for place, (group, row) in enumerate(((dvec_one, 0), (dvec_two, 0), (dvec_one, 1), (dvec_one, 2), (dvec_two, 1), (dvec_two, 2))):
        small[USED + place : USED + place + 1, :] = total_of(group, row)
    at = USED + 6
    for group in (dhead, dbias):
        whole = total_of(group, 0)
        for piece in range(whole.shape[1] // model):
            small[at : at + 1, :] = whole[:, piece * model : (piece + 1) * model]
            at += 1
    small[at:, :] = jnp.broadcast_to(squares, (small.shape[0] - at, model))


def adam_kernel(plan, small_ref, other_ref, *refs):
    count = len(plan)
    grads = refs[:3]
    olds, news = refs[3 : 3 + 3 * count], refs[4 + 3 * count :]
    norm_ref = refs[3 + 3 * count]
    shared = small_ref[: USED + 6, :]
    halves = []
    for ref in (small_ref, other_ref):
        biases = ref[USED + 6 : USED + 9, :]
        halves.append(ref[USED + 9 : USED + 10, :1] + jnp.sum(biases * biases, keepdims=True))
    norm = jnp.sqrt((halves[0] + halves[1]) + jnp.sum(shared * shared, keepdims=True))
    norm_ref[...] = norm
    factor = CLIP_NORM / jnp.maximum(norm, CLIP_NORM)
    for number, (source, row, column, rate, decay) in enumerate(plan):
        weight_ref, first_ref, second_ref = olds[3 * number : 3 * number + 3]
        height, length = weight_ref.shape[-2:]
        for index in range(math.prod(weight_ref.shape[:-2])):
            here = (index,) if weight_ref.ndim == 3 else ()
            if source is None and height == 1:
                model = small_ref.shape[1]
                gradient = jnp.concatenate([small_ref[row + i : row + i + 1, :] for i in range(length // model)], axis=1)
            elif source is None:
                gradient = small_ref[row : row + height, :]
            else:
                gradient = grads[source][:, column + index * length : column + (index + 1) * length]
            clipped = gradient * factor
            first = BETA_ONE * first_ref[here + (...,)] + (1.0 - BETA_ONE) * clipped
            second = BETA_TWO * second_ref[here + (...,)] + (1.0 - BETA_TWO) * clipped * clipped
            first_hat = first / (1.0 - BETA_ONE**STEP)
            second_hat = second / (1.0 - BETA_TWO**STEP)
            weight = weight_ref[here + (...,)]
            news[3 * number][here + (...,)] = weight - rate * (first_hat / (jnp.sqrt(second_hat) + ADAM_EPSILON) + decay * weight)
            news[3 * number + 1][here + (...,)] = first
            news[3 * number + 2][here + (...,)] = second


def weight_start_kernel(left_ref, right_ref, total_ref):
    def rows_of(step, carry):
        begin = pl.multiple_of(step * CHUNK, CHUNK)
        total_ref[pl.ds(begin, CHUNK), :] = dot_tn(left_ref[:, pl.ds(begin, CHUNK)], right_ref[...])
        return carry

    lax.fori_loop(0, total_ref.shape[0] // CHUNK, rows_of, 0)


def weight_grad_kernel(plan, kinds, sizes, base, me_ref, *refs):
    count = len(kinds) * len(sizes)
    outs = refs[-count - 1 : -1]
    total_ref = refs[-1]
    block = total_ref.shape[0] // SLOTS
    for part, (kind, pieces) in enumerate(zip(kinds, plan)):
        at = 0
        for left, right, start, size in pieces:

            def rows_of(step, carry, left=left, right=right, start=start, size=size, at=at):
                begin = pl.multiple_of(step * CHUNK, CHUNK)
                total = None if base is None else refs[base][pl.ds(begin, CHUNK), start : start + size]
                tokens = refs[left[0]].shape[0] - 2 * PAD
                operands = [(refs[a][:, pl.ds(begin, CHUNK)], refs[b][:, start : start + size]) for a, b in zip(left, right)]
                if len(operands) > 1:
                    tails = [jnp.concatenate([pair[i][tokens:] for pair in operands], axis=0) for i in range(2)]
                    operands = [(a[:tokens], b[:tokens]) for a, b in operands] + [tails]
                for one, two in operands:
                    add = dot_tn(one, two)
                    total = add if total is None else total + add
                total_ref[pl.ds(begin, CHUNK), at : at + size] = total
                return carry

            lax.fori_loop(0, total_ref.shape[0] // CHUNK, rows_of, 0)
            at += size
        number = 0
        for target in outs[part * len(sizes) : (part + 1) * len(sizes)]:
            for inner in range(target.shape[0]):
                place = lax.bitwise_xor(me_ref[0], slot_of(kind, number))
                begin = pl.multiple_of(place * block, block)
                target[inner] = total_ref[pl.ds(begin, block), :].astype(BF)
                number += 1


def exchange(values, axis, size, flip):
    return lax.ppermute(values, axis, [(i, i ^ flip) for i in range(size)])


def after(value, *others):
    return lax.optimization_barrier((value, *others))[0]


def add_low(*values):
    total = values[0].astype(F32)
    for value in values[1:]:
        total = total + value.astype(F32)
    return total


def canonical_split(full, kind, sizes):
    full = full.reshape(SLOTS, full.shape[0] // SLOTS, full.shape[1])
    full = jnp.stack([full[slot_of(kind, number)] for number in range(SLOTS)])
    ends = [sum(sizes[: i + 1]) for i in range(len(sizes))]
    return [full[end - size : end] for end, size in zip(ends, sizes)]


def canonical_join(pieces, kind):
    full = jnp.concatenate(pieces)
    order = [slot_of(kind, number) for number in range(SLOTS)]
    full = jnp.stack([full[order.index(d)] for d in range(SLOTS)])
    return full.reshape(-1, full.shape[-1])


def line_stage(own, size):
    return [own] + [exchange(own, "dp", size, 4 * j) for j in (1, 2, 3)]


def sum_all(values, axis, size):
    if size & (size - 1):
        return lax.psum(values, axis)
    flip = 1
    while flip < size:
        if flip * 4 <= size:
            near, far, both = [exchange(values, axis, size, flip * j) for j in (1, 2, 3)]
            values = (values + near) + (far + both)
            flip *= 4
        else:
            values = values + exchange(values, axis, size, flip)
            flip *= 2
    return values


def shards(
    size,
    pair,
    inputs,
    cotangent,
    seg_counts,
    qkv_weight,
    out_weight,
    up_weight,
    down_weight,
    head_bias,
    shared_params,
    qkv_first,
    out_first,
    up_first,
    down_first,
    bias_first,
    shared_first,
    qkv_second,
    out_second,
    up_second,
    down_second,
    bias_second,
    shared_second,
):
    unused, segments, seg, model = inputs.shape
    width = qkv_weight.shape[2]
    hidden = up_weight.shape[1]
    used = shared_params.shape[0] - 6
    pad = 16
    rows = seg + 2 * pad
    half = hidden // 2

    me = (lax.axis_index("dp") if size == SLOTS else jnp.int32(0)).astype(jnp.int32).reshape(1)
    block = qkv_weight.shape[1]
    (own_qkvo,) = call(own_first_kernel, [((2, block, 2 * width), BF)], [qkv_weight, out_weight.T])
    own_up, *own_down = call(
        own_next_kernel,
        [((2, block, half), BF), ((block, half), BF), ((block, half), BF)],
        [up_weight, down_weight.T],
    )
    own = [own_qkvo, own_up, own_down]

    def assembled(kinds, pieces, joined):
        return call(
            functools.partial(assemble_kernel, kinds, [len(p) for p in pieces], joined),
            [((model, 2 * model), BF)] if joined else [((model, model), BF)] * 2,
            [me, *pieces[0], *pieces[1]],
            scalars=1,
        )

    z_first, z_mid = ("za", "zb"), ("xa", "xb")
    if size == SLOTS:

        def spread(lines):
            low_a = jnp.concatenate([lines[0], exchange(lines[0], "dp", size, 2)])
            low_b = jnp.concatenate([lines[1], exchange(lines[1], "dp", size, 1)])
            return low_a, low_b

        def finish(low_a, low_b):
            return exchange(low_a, "dp", size, 1), exchange(low_b, "dp", size, 2)

        pair_c = [jnp.stack([own[2][i], exchange(own[2][i], "dp", size, 1 + i)]) for i in range(2)]
        line_one = line_stage(own[0], size)
        line_two = line_stage(after(own[1], *line_one), size)
        low_one = spread(call(line_kernel, [((4, *line_one[0].shape[1:]), BF)] * 2, line_one))
        line_three = line_stage(after(jnp.stack(pair_c), *line_two, *low_one), size)
        high_one = finish(*low_one)
        low_two = spread([after(jnp.stack([v[i] for v in line_two]), *high_one) for i in range(2)])
        high_two = finish(*low_two)
        low_c = [jnp.concatenate([v[i] for v in line_three]) for i in range(2)]
        low_c = [after(v, *high_two) for v in low_c]
        high_c = [exchange(low_c[i], "dp", size, 2 - i) for i in range(2)]
        w_qk, w_vo = assembled(z_first, [[low_one[i], high_one[i]] for i in range(2)], False)
        (w_up,) = assembled(z_first, [[low_two[i], high_two[i]] for i in range(2)], True)
        (w_down,) = assembled(z_mid, [[low_c[i], high_c[i]] for i in range(2)], True)
    else:

        def whole(number, kinds, sizes):
            pieces = [lax.all_gather(own[number][i], "dp", axis=0, tiled=True) for i in range(2)]
            return assembled(kinds, [canonical_split(p, kind, sizes) for p, kind in zip(pieces, kinds)], number > 0)

        w_qk, w_vo = whole(0, z_first, (8, 8))
        (w_up,) = whole(1, z_first, (8, 8))
        (w_down,) = whole(2, z_mid, (8, 8))

    memory = jnp.concatenate([shared_params[:used], jnp.zeros((pad - used, model), F32)], axis=0)
    alive = [(slot < seg_counts).astype(F32).reshape(1, 1) for slot in range(segments)]
    memories, tokens_out, saved = [memory], [], []
    attn_outs = [((rows, model), BF), ((rows, model), BF), ((rows, 3 * width), BF), ((rows, 128), F32), ((rows, width), BF)]
    for slot in range(segments):
        tokens = inputs[0, slot]
        if slot == 0:
            part, *attn = call(attn_forward_kernel, attn_outs, [tokens, memory, w_qk, w_vo, head_bias])
        else:
            out_rows, memory, second_in, part, *attn = call(
                attn_next_kernel,
                [((seg, model), BF), ((pad, model), F32), ((rows, model), F32)] + attn_outs,
                [saved[-1][4], ffn_part, other, shared_params, alive[slot - 1], memory, tokens, w_qk, w_vo, head_bias],
            )
            tokens_out.append(out_rows)
            saved[-1] += (second_in,)
        other = exchange(part, "head", pair, 1)
        ffn_part, first_in, h_low, active, slope = call(
            ffn_forward_kernel,
            [((rows, model), BF), ((rows, model), F32), ((rows, model), BF), ((rows, hidden), BF), ((rows, hidden), BF)],
            [tokens, memory, part, other, w_up, w_down, head_bias, shared_params],
        )
        other = exchange(ffn_part, "head", pair, 1)
        saved.append((*attn, first_in, h_low, active, slope))

    count = segments

    def weight_grad(names, plan, kinds, base=None):
        sizes = (8, 8)
        slots = range(count) if base is None else (0,)
        operands = [stacks[s][n] for n in names for s in slots]
        at = {n: [i * len(slots) + j for j in range(len(slots))] for i, n in enumerate(names)}
        steps = [[(at[a], at[b], start, length) for a, b, start, length in pieces] for pieces in plan]
        result = call(
            functools.partial(weight_grad_kernel, steps, kinds, sizes, None if base is None else len(operands)),
            [((length, model // SLOTS, model), BF) for kind in kinds for length in sizes],
            [me, *operands] + ([] if base is None else [base]),
            scalars=1,
            scratch=[pltpu.VMEM((model, model), F32)],
        )
        return result[: len(sizes)], result[len(sizes) :]

    dmem = jnp.zeros((pad, model), F32)
    grads = [None] * segments
    stacks = [None] * segments
    smalls, base = [], None
    ffn_outs = [((rows, model), BF), ((rows, model), F32), ((rows, model), BF), ((rows, hidden), BF), ((1, hidden), F32), ((8, model), F32)]
    for slot in reversed(range(segments)):
        low, qkv, lse, ctx, first_in, h_low, active, slope = saved[slot][:8]
        weights = [alive[slot], shared_params, w_up, w_down, slope]
        if slot == segments - 1:
            outputs, part, dsecond, df_low, du, dbias, dvec_two = call(
                functools.partial(ffn_last_kernel, slot),
                [((segments, seg, model), BF)] + ffn_outs,
                [*tokens_out, first_in, ffn_part, other, cotangent[0, slot], dmem, *weights],
            )
        else:
            grads[slot + 1], dmem, part, dsecond, df_low, du, dbias, dvec_two = call(
                ffn_before_kernel,
                [((seg, model), BF), ((pad, model), F32)] + ffn_outs,
                [dfirst, part, other, alive[slot + 1], dmem, saved[slot][8], cotangent[0, slot], *weights],
            )
        other = exchange(part, "head", pair, 1)
        stacks[slot] = (low, ctx, h_low, active, df_low, du)
        if slot == 0:
            dw_down = weight_grad((DF_LOW, ACTIVE), [[(DF_LOW, ACTIVE, 0, half)], [(DF_LOW, ACTIVE, half, half)]], z_first, base)
            dw_up = weight_grad((H_LOW, DU), [[(H_LOW, DU, 0, half)], [(H_LOW, DU, half, half)]], z_first)
            dsecond = after(dsecond, dw_down[0][0], dw_up[0][0])
        elif segments == 2:
            (base,) = call(weight_start_kernel, [((model, hidden), F32)], [df_low, active])
            dsecond = after(dsecond, base)
        part, dfirst, da, dqkv, dhead, dvec_one = call(
            attn_backward_kernel,
            [((rows, model), BF), ((rows, model), F32), ((rows, model), BF), ((rows, 3 * width), BF), ((1, 2 * width), F32), ((8, model), F32)],
            [dsecond, part, other, first_in, shared_params, w_qk, w_vo, qkv, lse],
            scratch=[pltpu.VMEM((rows, width), BF), pltpu.VMEM((128, rows), F32)],
        )
        other = exchange(part, "head", pair, 1)
        stacks[slot] += (da, dqkv)
        smalls += [dvec_one, dvec_two, dhead, dbias]
    input_grad, dmem = call(
        input_grad_kernel,
        [((segments, seg, model), BF), ((pad, model), F32)],
        [dfirst, part, other, alive[0], dmem, *grads[1:]],
    )

    def fallback(parts, kinds):
        full = [canonical_join(p, kind) for p, kind in zip(parts, kinds)]
        full = jnp.concatenate(full, axis=1)
        return lax.psum_scatter(full, "dp", scatter_dimension=0, tiled=True).astype(F32)

    def hop(blocks, flips):
        return [exchange(block, "dp", size, flip) for block, flip in zip(blocks, flips)]

    def add_halves(keep, got):
        return [add_low(k, g).astype(BF) for k, g in zip(keep, got)]

    def line_hop(four):
        return [exchange(four[j], "dp", size, 4 * j) for j in (1, 2, 3)]

    x_first, y_first = (1, 2), (2, 1)
    if size == SLOTS:
        got_down, got_up = hop([p[1] for p in dw_down], x_first), hop([p[1] for p in dw_up], x_first)
        down = add_halves([p[0] for p in dw_down], [after(g, stacks[0][DQKV]) for g in got_down])
        got_down = hop([v[4:] for v in down], y_first)
        up = add_halves([p[0] for p in dw_up], [after(g, *down) for g in got_up])
        stacks[0] = stacks[0][:DQKV] + (after(stacks[0][DQKV], *up),)
        got_up = hop([v[4:] for v in up], y_first)
    dw_qkvo = weight_grad(
        (LOW, DQKV, DA, CTX),
        [[(LOW, DQKV, 0, 2 * width)], [(LOW, DQKV, 2 * width, width), (DA, CTX, 0, width)]],
        z_first,
    )
    if size == SLOTS:
        got_down = [after(g, dw_qkvo[0][0]) for g in got_down]
        down = jnp.concatenate(add_halves([v[:4] for v in down], got_down), axis=2)
        got_down = line_hop(down)
        dw_qkvo = [[after(v, *got_up) for v in part] for part in dw_qkvo]
        got_qkvo = hop([p[1] for p in dw_qkvo], x_first)
        up = jnp.concatenate(add_halves([v[:4] for v in up], got_up), axis=2)
        got_up = line_hop(up)
        last = add_halves([p[0] for p in dw_qkvo], [after(g, *got_down, *got_up) for g in got_qkvo])
        got_qkvo = hop([v[4:] for v in last], y_first)
        last = jnp.concatenate(add_halves([v[:4] for v in last], got_qkvo), axis=2)
        sums = [[down[0], *got_down], [up[0], *got_up], [last[0], *line_hop(last)]]
    else:
        sums = [[fallback(p, z_first)] for p in (dw_down, dw_up, dw_qkvo)]
    height, wide = sums[0][0].shape
    *matrices, small = call(
        functools.partial(grad_close_kernel, len(sums[0])),
        [((height, wide), F32)] * 3 + [((24, model), F32)],
        [*sums[0], *sums[1], *sums[2], dmem, *smalls],
    )
    small = sum_all(small, "dp", size)
    other = exchange(small, "head", pair, 1)
    plan = (
        (2, 0, 0, LEARN_RATE, DECAY_RATE),
        (2, 0, 3 * width, LEARN_RATE, DECAY_RATE),
        (1, 0, 0, LEARN_RATE, DECAY_RATE),
        (0, 0, 0, LEARN_RATE, DECAY_RATE),
        (None, used + 6, 0, VECTOR_RATE, 0.0),
        (None, 0, 0, VECTOR_RATE, 0.0),
    )
    olds = (
        (qkv_weight, qkv_first, qkv_second),
        (out_weight.T, out_first.T, out_second.T),
        (up_weight, up_first, up_second),
        (down_weight.T, down_first.T, down_second.T),
        (head_bias, bias_first, bias_second),
        (shared_params, shared_first, shared_second),
    )
    grad_norm, *news = call(
        functools.partial(adam_kernel, plan),
        [((1, 1), F32)] + [(o.shape, F32) for old in olds for o in old],
        [small, other, *matrices, *[o for old in olds for o in old]],
    )
    results = [news[3 * i : 3 * i + 3] for i in range(6)]
    for number in (1, 3):
        results[number] = [r.T for r in results[number]]
    return (outputs[None], input_grad[None], grad_norm[0, 0]) + tuple(r[i] for i in range(3) for r in results)


def solution(mesh):
    weights = (P(None, "dp", "head"), P("head", "dp"), P("dp", "head"), P("head", "dp"), P("head", None), P())
    rows = P("dp", None, None, None)
    return jax.shard_map(
        functools.partial(shards, mesh.shape["dp"], mesh.shape["head"]),
        mesh=mesh,
        in_specs=(rows, rows, P("dp")) + weights * 3,
        out_specs=(rows, rows, P()) + weights * 3,
        check_vma=False,
    )
```
